128 devices in a mesh: dp: 8 (over z, core), tensor: 16 (over x, y).
Axes of the slice: x: 4, y: 4, z: 4, core: 2. Of those that a mesh axis runs over, the one named last changes fastest.
Arguments:
- queries: bfloat16 [4096, 36864], P('dp', 'tensor'), may hold values from -6.8560344 to 6.8560344
- cache: bfloat16 [8, 3072, 576], P('dp', 'tensor'), may hold values from -4 to 4
- offsets: int32 [8], P('dp'), may hold values from 0 to 2560, as said below
- value_up: bfloat16 [64, 512, 128], P('tensor'), may hold values from -0.25 to 0.25
- out_proj: bfloat16 [8192, 3584], P('tensor', 'dp'), may hold values from -0.0625 to 0.0625
- resid: bfloat16 [4096, 3584], P(('dp', 'tensor')), may hold values from -3 to 3
- norm_gain: float32 [3584], replicated, may hold values from 0.25 to 1.75
- routes: int32 [4096, 8], P(('dp', 'tensor')), may hold values from 0 to 127, as said below
- route_weights: float32 [4096, 8], P(('dp', 'tensor')), may hold values from 0.1 to 0.6
- expert_in: bfloat16 [128, 3584, 2048], P(('dp', 'tensor')), may hold values from -0.09375 to 0.09375
- expert_down: bfloat16 [128, 1024, 3584], P(('dp', 'tensor')), may hold values from -0.1875 to 0.1875
Outputs:
- mixed: bfloat16 [4096, 3584], P(('dp', 'tensor'))
The draws below stay inside these ranges and needn't reach their ends.
Inputs may be any that keep to these rules, and one draw needn't show every extreme that they name: `routes`: each row names 8 different experts. Among the 32 rows of one device (aligned blocks of rows) a quarter of the experts is named 4 times, a quarter 3 times, a quarter once and a quarter never; in every draw one expert is named 4 times in every block. `offsets`: some sequence's offset is 2560; the new tokens' own latents are in the cache at their positions.
All inputs are finite; a program needn't handle non-finite values.
Results may differ from the reference program's by a relative error of at most 0.024.
Values may be sent and summed in bfloat16 or wider, within the bound.
A program may use at most 192 MiB of HBM per device.

```python
import jax
import jax.numpy as jnp
from jax import lax

D = 3584
HEADS = 64
LAT = 512
ROPE = 64
VDIM = 128
FF = 1024
TOP = 8
TOK_DEV = 32
EXPERTS = 128
TOK_GRP = 512
TOKENS = 4096
CACHE = 3072
CAP = 4
N_DP = 8
N_TENSOR = 16


def attention_inputs(key):
    key_cache = jax.random.fold_in(key, 101)
    key_query = jax.random.fold_in(key, 102)
    key_width = LAT + ROPE
    cache = jnp.clip(jax.random.normal(key_cache, (N_DP, CACHE, key_width), jnp.float32), -4.0, 4.0)
    queries = jnp.clip(1.5 * jax.random.normal(key_query, (N_DP, TOK_GRP, HEADS, key_width), jnp.float32), -6.0, 6.0)
    queries = queries.reshape(N_DP * TOK_GRP, HEADS * key_width)
    return (queries.astype(jnp.bfloat16), cache.astype(jnp.bfloat16))


def draw_queries(key, part):
    return attention_inputs(key)[0]


def draw_cache(key, part):
    return attention_inputs(key)[1]


def draw_offsets(key, part):
    highest = CACHE - TOK_GRP
    values = jax.random.randint(jax.random.fold_in(key, 201), (N_DP,), 0, highest + 1)
    picked = jax.random.randint(jax.random.fold_in(key, 202), (), 0, N_DP)
    return jnp.where(jnp.arange(N_DP) == picked, highest, values).astype(jnp.int32)


def draw_routes(key, part):
    quarter = EXPERTS // 4
    hot_expert = jax.random.randint(jax.random.fold_in(key, 301), (), 0, EXPERTS)
    base_counts = jnp.concatenate([jnp.full((quarter,), CAP, jnp.int32), jnp.full((quarter,), 3 * CAP // 4, jnp.int32), jnp.full((quarter,), CAP // 4, jnp.int32), jnp.zeros((quarter,), jnp.int32)])

    def one_block(block_key):
        key_perm = jax.random.fold_in(block_key, 1)
        key_order = jax.random.fold_in(block_key, 2)
        key_tokens = jax.random.fold_in(block_key, 3)
        perm = jax.random.permutation(key_perm, EXPERTS)
        counts = jnp.zeros((EXPERTS,), jnp.int32).at[perm].set(base_counts)
        first_full = perm[0]
        held = counts[hot_expert]
        counts = counts.at[first_full].set(held).at[hot_expert].set(CAP)
        expert_order = jax.random.permutation(key_order, EXPERTS)
        sequence = jnp.repeat(expert_order, counts[expert_order], total_repeat_length=TOK_DEV * TOP)
        table = sequence.reshape(TOP, TOK_DEV).T
        token_perm = jax.random.permutation(key_tokens, TOK_DEV)
        return table[token_perm]
    block_keys = jax.random.split(jax.random.fold_in(key, 302), N_DP * N_TENSOR)
    return jax.vmap(one_block)(block_keys).reshape(TOKENS, TOP).astype(jnp.int32)


def steps_of(rng, extent, pieces, low, high):
    factor_of, own = 1.0, jax.random.fold_in(rng, 6)
    for axis_at, shards_of in pieces:
        draws = jnp.exp(jax.random.uniform(jax.random.fold_in(own, axis_at), (shards_of,), jnp.float32, low / len(pieces), high / len(pieces)))
        factor_of = factor_of * jnp.repeat(draws, extent[axis_at] // shards_of).reshape([-1 if axis == axis_at else 1 for axis in range(len(extent))])
    return factor_of


def normal_values(stream_key, dims, deviation, reach, cuts=(), kind=jnp.bfloat16):
    array = deviation * jax.random.normal(stream_key, dims, jnp.float32)
    if cuts:
        array = array * steps_of(stream_key, dims, cuts, -0.22, 0.18)
    return jnp.clip(array, -reach, reach).astype(kind)


def setup_inputs(seed: int = 0) -> dict:
    arg_keys = jax.random.split(jax.random.key(seed), 12)
    queries = draw_queries(jax.random.fold_in(arg_keys[11], 71), 0)
    cache = draw_cache(jax.random.fold_in(arg_keys[11], 71), 0)
    offsets = draw_offsets(jax.random.fold_in(arg_keys[11], 71), 0)
    value_up = normal_values(arg_keys[3], (HEADS, LAT, VDIM), LAT ** -0.5, 0.25, ((0, 16),))
    out_proj = normal_values(arg_keys[4], (HEADS * VDIM, D), (HEADS * VDIM) ** -0.5, 0.0625, ((0, 16), (1, 8)))
    resid = normal_values(arg_keys[5], (TOKENS, D), 0.5, 3.0, ((0, 128),))
    norm_gain = jnp.clip(1.0 + 0.15 * jax.random.normal(arg_keys[6], (D,), jnp.float32), 0.25, 1.75)
    routes = draw_routes(jax.random.fold_in(arg_keys[11], 71), 0)
    route_weights = jnp.clip(0.1 + 0.5 * jax.random.uniform(arg_keys[8], (TOKENS, TOP), jnp.float32) ** steps_of(arg_keys[8], (TOKENS, TOP), ((0, 128),), -0.2, 0.2), 0.1, 0.6)
    expert_in = normal_values(arg_keys[9], (EXPERTS, D, 2 * FF), D ** -0.5, 0.09375, ((0, 128),))
    expert_down = normal_values(arg_keys[10], (EXPERTS, FF, D), FF ** -0.5, 0.1875, ((0, 128),))
    return dict(queries=queries, cache=cache, offsets=offsets, value_up=value_up, out_proj=out_proj, resid=resid, norm_gain=norm_gain, routes=routes, route_weights=route_weights, expert_in=expert_in, expert_down=expert_down)


def attend_head(query_head, key_rows, start_pos, value_map):
    score_scale = (VDIM + ROPE) ** (-0.5)
    scores = jnp.dot(query_head, key_rows.T, preferred_element_type=jnp.float32) * score_scale
    query_pos = start_pos + jnp.arange(TOK_GRP, dtype=jnp.int32)
    key_pos = jnp.arange(CACHE, dtype=jnp.int32)
    visible = key_pos[None, :] <= query_pos[:, None]
    scores = jnp.where(visible, scores, jnp.float32(-1e+30))
    row_max = lax.optimization_barrier(jnp.max(scores, axis=1, keepdims=True))
    weights = jnp.where(visible, jnp.exp(scores - row_max), jnp.float32(0.0))
    total = lax.optimization_barrier(jnp.sum(weights, axis=1))
    context = jnp.dot(weights.astype(jnp.bfloat16), key_rows[:, :LAT], preferred_element_type=jnp.float32)
    context = (context / total[:, None]).astype(jnp.bfloat16)
    return jnp.dot(context, value_map, preferred_element_type=jnp.float32).astype(jnp.bfloat16)

def reference(queries, cache, offsets, value_up, out_proj, resid, norm_gain, routes, route_weights, expert_in, expert_down):
    key_width = LAT + ROPE
    attn_parts = []
    for group in range(N_DP):
        group_q = queries[group * TOK_GRP:(group + 1) * TOK_GRP].reshape(TOK_GRP, HEADS, key_width)
        group_q = jnp.transpose(group_q, (1, 0, 2))
        key_rows = cache[group]
        start_pos = offsets[group].astype(jnp.int32)

        def one_head(inputs):
            return attend_head(inputs[0], key_rows, start_pos, inputs[1])
        head_out = lax.map(one_head, (group_q, value_up))
        flat_out = jnp.transpose(head_out, (1, 0, 2)).reshape(TOK_GRP, HEADS * VDIM)
        attn_parts.append(jnp.dot(flat_out, out_proj, preferred_element_type=jnp.float32))
    attn = jnp.concatenate(attn_parts, axis=0)
    stream = resid.astype(jnp.float32) + attn
    mean_square = lax.optimization_barrier(jnp.mean(stream * stream, axis=1, keepdims=True))
    normed = (stream * lax.rsqrt(mean_square + 1e-06) * norm_gain).astype(jnp.bfloat16)
    slots_max = EXPERTS * CAP

    def expert_step(running_sum, inputs):
        expert_id, w_in, w_down = inputs
        hit_mask = routes == expert_id
        weight_tok = lax.optimization_barrier(jnp.sum(jnp.where(hit_mask, route_weights, jnp.zeros_like(route_weights)), axis=1))
        is_named = jnp.any(hit_mask, axis=1)
        row_ids = jnp.nonzero(is_named, size=slots_max, fill_value=0)[0].astype(jnp.int32)
        named_count = jnp.sum(is_named.astype(jnp.int32))
        live_rows = jnp.arange(slots_max, dtype=jnp.int32) < named_count
        gathered = normed[row_ids]
        joint_proj = jnp.dot(gathered, w_in, preferred_element_type=jnp.float32)
        hidden = (jax.nn.silu(joint_proj[:, :FF]) * joint_proj[:, FF:]).astype(jnp.bfloat16)
        expert_out = jnp.dot(hidden, w_down, preferred_element_type=jnp.float32).astype(jnp.bfloat16)
        addition = weight_tok[row_ids][:, None] * expert_out.astype(jnp.float32)
        addition = jnp.where(live_rows[:, None], addition, jnp.zeros_like(addition))
        return (running_sum.at[row_ids].add(addition), None)
    start_sum = jnp.zeros((TOKENS, D), jnp.float32)
    routed, unused = lax.scan(expert_step, start_sum, (jnp.arange(EXPERTS, dtype=jnp.int32), expert_in, expert_down))
    return (stream + routed).astype(jnp.bfloat16)
```

```python
import functools

import jax
import jax.numpy as jnp
from jax import lax
from jax.experimental import pallas as pl
from jax.experimental.pallas import tpu as pltpu
from jax.sharding import PartitionSpec as P

MESH = pl.DeviceIdType.MESH
BF16, F32, I32 = jnp.bfloat16, jnp.float32, jnp.int32
NEAR = (
    (1, 0), (0, 1), (3, 0), (0, 3), (1, 1), (3, 3), (1, 3), (3, 1),
    (2, 0), (0, 2), (2, 2), (2, 1), (1, 2), (2, 3), (3, 2),
)
ROUNDS = (
    ((0, 0, 640), (1, 640, 640), (2, 1280, 512)),
    ((0, 1792, 640), (1, 2432, 512), (2, 2944, 640)),
)


def whole(ref, sem):
    pltpu.make_async_copy(ref, ref, sem).wait()


def dot(a, b):
    return jnp.dot(a, b, preferred_element_type=F32)


class Place:
    def __init__(self):
        dp, t = lax.axis_index("dp"), lax.axis_index("tensor")
        self.z, self.c = lax.div(dp, 2), lax.rem(dp, 2)
        self.x, self.y = lax.div(t, 4), lax.rem(t, 4)

    def line(self, part, a, core):
        if part == 0:
            return (a * 2 + core, self.x * 4 + self.y)
        if part == 1:
            return (self.z * 2 + core, a * 4 + self.y)
        return (self.z * 2 + core, self.x * 4 + a)

    def own_line(self, part):
        return (self.z, self.x, self.y)[part]

    def plane(self, part, b1, b2):
        if part == 0:
            return (self.z * 2 + self.c, b1 * 4 + b2)
        if part == 1:
            return (b1 * 2 + self.c, self.x * 4 + b2)
        return (b2 * 2 + self.c, b1 * 4 + self.y)

    def own_plane(self, part):
        return ((self.x, self.y), (self.z, self.y), (self.x, self.z))[part]

    def expert(self, part, j):
        b1, b2 = j // 4, j % 4
        if part == 0:
            return (self.z * 2 + self.c) * 16 + j
        if part == 1:
            return (b1 * 2 + self.c) * 16 + self.x * 4 + b2
        return (b2 * 2 + self.c) * 16 + b1 * 4 + self.y


def up(v, n):
    return lax.rem(v + n, 4)


def partners(me):
    out = [(me.z * 2 + 1 - me.c, me.x * 4 + me.y)]
    for part in range(3):
        for n in (1, 2, 3):
            out.append(me.line(part, up(me.own_line(part), n), 1 - me.c))
    for dz in range(4):
        for dx in range(4):
            for dy in range(4):
                if (dz, dx, dy) != (0, 0, 0) and 0 in (dz, dx, dy):
                    out.append((up(me.z, dz) * 2 + me.c, up(me.x, dx) * 4 + up(me.y, dy)))
    return out


def back_kernel(
    ho_ref, wo_ref, resid_ref, gain_ref, meta_ref, win_hbm, wdown_hbm,
    out_ref,
    win, wdown, part4, r1, l1, r2, l2, mid, r1b, l1b, r2b, l2b,
    metas, pick, wgt, swap, stream, nrm, toks, outg, rows, stage, acc, hid, psum, recv,
    wsem, rs_s, rs_r, m_s, m_r, g_s, g_r, d_s, d_r, t_s, t_r, c_s, c_r,
):
    me = Place()
    loads = [
        pltpu.make_async_copy(win_hbm.at[pl.ds(0, 1792)], win.at[pl.ds(0, 1792)], wsem.at[0]),
        pltpu.make_async_copy(win_hbm.at[pl.ds(1792, 1792)], win.at[pl.ds(1792, 1792)], wsem.at[1]),
        pltpu.make_async_copy(wdown_hbm, wdown, wsem.at[2]),
    ]
    for load in loads:
        load.start()

    barrier = pltpu.get_barrier_semaphore()
    others = partners(me)
    for other in others:
        pl.semaphore_signal(barrier, inc=1, device_id=other, device_id_type=MESH)
    pl.semaphore_wait(barrier, len(others))

    def send(src, dst, ssem, rsem, device):
        copy = pltpu.make_async_remote_copy(
            src_ref=src, dst_ref=dst, send_sem=ssem, recv_sem=rsem,
            device_id=device, device_id_type=MESH,
        )
        copy.start()
        return copy

    def half_cols(h):
        return pl.ds(h * 1792, 1792)

    def group(h, k, lo, n):
        cols = pl.ds(h * 1792 + lo, n)
        return part4.at[k, :, :, cols] if h == 0 else part4.at[:, k, :, cols]

    def project(h, k):
        head = ho_ref[k] if h == 0 else ho_ref[:, k]
        value = dot(head.reshape(128, 512), wo_ref[:, half_cols(h)])
        group(h, k, 0, 1792)[...] = value.astype(BF16).reshape(4, 32, 1792)

    def neighbour(h, phase, n):
        along_x = (h == 0) == (phase == 0)
        if along_x:
            return (me.z * 2 + me.c, up(me.x, n) * 4 + me.y)
        return (me.z * 2 + me.c, me.x * 4 + up(me.y, n))

    def position(h, phase):
        return me.x if (h == 0) == (phase == 0) else me.y

    def piece(h, phase, k, lo, n):
        return group(h, k, lo, n) if phase == 0 else mid.at[h, k, :, pl.ds(lo, n)]

    def boxes(phase):
        return (r1, l1, r2, l2) if phase == 0 else (r1b, l1b, r2b, l2b)

    def box(ref, h, phase, lo, n):
        if phase == 0:
            return ref.at[h, :, :, pl.ds(lo, n)]
        return ref.at[h, :, pl.ds(lo, n)]

    started = {}

    def first_far(h, phase):
        k = up(position(h, phase), 2)
        br1, bl1, _, _ = boxes(phase)
        for side, (ref, lo, n) in enumerate(((br1, 0, 1), (bl1, 896, 3))):
            i = (h * 2 + phase) * 6 + side
            started[h, phase, side] = send(
                piece(h, phase, k, lo, 896), box(ref, h, phase, 0, 896),
                rs_s.at[i], rs_r.at[i], neighbour(h, phase, n),
            )

    def first_near(h, phase):
        _, _, br2, bl2 = boxes(phase)
        for side, (ref, lo, n) in enumerate(((br2, 896, 1), (bl2, 0, 3))):
            i = (h * 2 + phase) * 6 + 2 + side
            started[h, phase, 2 + side] = send(
                piece(h, phase, up(position(h, phase), n), lo, 896), box(ref, h, phase, lo, 896),
                rs_s.at[i], rs_r.at[i], neighbour(h, phase, n),
            )

    def second(h, phase):
        br1, bl1, br2, bl2 = boxes(phase)
        for side, (ref, to, lo, n) in enumerate(((br1, br2, 0, 1), (bl1, bl2, 896, 3))):
            i = (h * 2 + phase) * 6 + 4 + side
            started[h, phase, side].wait_recv()
            mine = piece(h, phase, up(position(h, phase), n), lo, 896)
            mine[...] = (mine[...].astype(F32) + box(ref, h, phase, 0, 896)[...].astype(F32)).astype(BF16)
            started[h, phase, 4 + side] = send(
                mine, box(to, h, phase, lo, 896), rs_s.at[i], rs_r.at[i], neighbour(h, phase, n)
            )

    def last(h, phase):
        for i in (2, 3, 4, 5):
            started[h, phase, i].wait_recv()
        _, _, br2, bl2 = boxes(phase)
        total = piece(h, phase, position(h, phase), 0, 1792)[...].astype(F32)
        total += box(br2, h, phase, 0, 1792)[...].astype(F32)
        return total + box(bl2, h, phase, 0, 1792)[...].astype(F32)

    meta_sends = []
    for part in range(3):
        own = me.own_line(part) * 2 + me.c
        for n in range(4):
            for core in range(2):
                if (n, core) == (0, 0):
                    continue
                to = me.line(part, up(me.own_line(part), n), lax.rem(me.c + core, 2))
                meta_sends.append(send(meta_ref, metas.at[part, own], m_s.at[part], m_r.at[part], to))
        pltpu.make_async_copy(meta_ref, metas.at[part, own], m_r.at[part]).start()

    for h in range(2):
        project(h, up(position(h, 0), 2))
    for h in range(2):
        first_far(h, 0)
    for n in (1, 3):
        for h in range(2):
            project(h, up(position(h, 0), n))
    for h in range(2):
        first_near(h, 0)
    for h in range(2):
        project(h, position(h, 0))

    token = lax.broadcasted_iota(I32, (256, 256), 0)
    other = lax.broadcasted_iota(I32, (256, 256), 1)
    earlier = jnp.where((token // 32 == other // 32) & (other < token), 1.0, 0.0).astype(BF16)
    lane = lax.broadcasted_iota(I32, (128, 512), 1)
    spread = jnp.where(lane // 32 == lax.broadcasted_iota(I32, (128, 512), 0), 1.0, 0.0).astype(BF16)
    slot = lax.broadcasted_iota(I32, (256, 512), 1) % 32
    of_source = slot // 4 == lax.broadcasted_iota(I32, (256, 512), 0) // 32
    rank_wanted = (slot % 4).astype(F32)
    for part in range(3):
        whole(metas.at[part], m_r.at[part])
        table = metas[part].reshape(256, 128)
        column = lax.broadcasted_iota(I32, (256, 128), 1)
        wanted = jnp.where(column < 16, me.expert(part, column), -1).astype(F32)
        hit = jnp.zeros((256, 128), F32)
        weight = jnp.zeros((256, 128), F32)
        for k in range(8):
            same = table[:, k : k + 1] == wanted
            hit = jnp.where(same, 1.0, hit)
            weight = jnp.where(same, table[:, 8 + k : 9 + k], weight)
        rank = dot(earlier, hit.astype(BF16))
        rank = jnp.where(hit > 0.5, rank, -1.0)
        chosen = (dot(rank.astype(BF16), spread) == rank_wanted) & of_source
        pick[part] = jnp.where(chosen, 1.0, 0.0).T.astype(BF16)
        wgt[part] = jnp.where(chosen, dot(weight.astype(BF16), spread), 0.0).astype(BF16)
    row = lax.broadcasted_iota(I32, (512, 512), 0)
    col = lax.broadcasted_iota(I32, (512, 512), 1)
    rx, ry, rz, low = row // 128, (row // 32) % 4, (row // 8) % 4, row % 8
    swap[0] = jnp.where(col == rz * 128 + ry * 32 + rx * 8 + low, 1.0, 0.0).astype(BF16)
    swap[1] = jnp.where(col == rx * 128 + rz * 32 + ry * 8 + low, 1.0, 0.0).astype(BF16)

    for h in range(2):
        second(h, 0)
    for h in range(2):
        mid[h] = last(h, 0).astype(BF16)
    for h in range(2):
        first_far(h, 1)
    for h in range(2):
        first_near(h, 1)
    for h in range(2):
        second(h, 1)
    for h in range(2):
        stream[:, half_cols(h)] = last(h, 1) + resid_ref[:, half_cols(h)].astype(F32)
    value = stream[...]
    mean_square = jnp.mean(value * value, axis=1, keepdims=True)
    nrm[...] = (value * lax.rsqrt(mean_square + 1e-06) * gain_ref[...]).astype(BF16)
    for copy in started.values():
        copy.wait_send()

    def gather(i):
        for p, (part, lo, n) in enumerate(ROUNDS[i]):
            own = me.own_line(part) * 2 + me.c
            at = i * 3 + p
            for step, core in ((0, 1), (1, 0), (3, 0), (1, 1), (3, 1), (2, 0), (2, 1)):
                to = me.line(part, up(me.own_line(part), step), lax.rem(me.c + core, 2))
                send(nrm.at[:, pl.ds(lo, n)], toks.at[own, :, pl.ds(lo, n)], g_s.at[at], g_r.at[at], to)
            pltpu.make_async_copy(nrm.at[:, pl.ds(lo, n)], toks.at[own, :, pl.ds(lo, n)], g_r.at[at]).start()

    def flat(ref, lo, n):
        return ref[:, :, :, pl.ds(lo, n)].reshape(512, n)

    def exchange(i, src, dst_of, ssem, rsem):
        for d1, d2 in NEAR:
            for p, (part, lo, n) in enumerate(ROUNDS[i]):
                b1, b2 = me.own_plane(part)
                e1, e2 = up(b1, d1), up(b2, d2)
                send(
                    src.at[e1, e2, :, pl.ds(lo, n)], dst_of(part).at[b1, b2, :, pl.ds(lo, n)],
                    ssem.at[i * 3 + p], rsem.at[i * 3 + p], me.plane(part, e1, e2),
                )
        for p, (part, lo, n) in enumerate(ROUNDS[i]):
            b1, b2 = me.own_plane(part)
            pltpu.make_async_copy(
                src.at[b1, b2, :, pl.ds(lo, n)], dst_of(part).at[b1, b2, :, pl.ds(lo, n)],
                rsem.at[i * 3 + p],
            ).start()

    def landing(part):
        return rows if part == 0 else stage

    def block(ref, lo, n):
        return ref.at[:, :, :, pl.ds(lo, n)]

    def sent(ref, lo, n, sem):
        for k in range(3):
            whole(ref.at[k, :, :, pl.ds(lo, n)], sem)
        whole(ref.at[3, pl.ds(0, 3), :, pl.ds(lo, n)], sem)

    def dispatch(i):
        for p, (part, lo, n) in enumerate(ROUNDS[i]):
            whole(toks.at[:, :, pl.ds(lo, n)], g_r.at[i * 3 + p])
            value = dot(pick[part], toks[:, :, pl.ds(lo, n)].reshape(256, n))
            outg[:, :, :, pl.ds(lo, n)] = value.astype(BF16).reshape(4, 4, 32, n)
        exchange(i, outg, landing, d_s, d_r)

    def arrive(i):
        for p, (part, lo, n) in enumerate(ROUNDS[i]):
            whole(block(landing(part), lo, n), d_r.at[i * 3 + p])
            if part:
                value = dot(swap[part - 1], flat(stage, lo, n))
                rows[:, :, :, pl.ds(lo, n)] = value.astype(BF16).reshape(4, 4, 32, n)

    gather(0)
    gather(1)
    dispatch(0)
    dispatch(1)

    loads[0].wait()
    arrive(0)

    def first_half(j, carry):
        cols = pl.ds(pl.multiple_of(j * 256, 256), 256)
        acc[:, cols] = dot(flat(rows, 0, 1792), win[pl.ds(0, 1792), cols])
        return carry

    lax.fori_loop(0, 8, first_half, 0)
    loads[1].wait()
    arrive(1)

    def second_half(j, carry):
        cols = pl.ds(pl.multiple_of(j * 256, 256), 256)
        more = pl.ds(pl.multiple_of(j * 256 + 1024, 256), 256)
        gate = acc[:, cols] + dot(flat(rows, 1792, 1792), win[pl.ds(1792, 1792), cols])
        lift = acc[:, more] + dot(flat(rows, 1792, 1792), win[pl.ds(1792, 1792), more])
        hid[0, :, cols] = (gate / (1.0 + jnp.exp(-gate)) * lift).astype(BF16)
        return carry

    lax.fori_loop(0, 4, second_half, 0)
    loads[2].wait()
    for part in (1, 2):
        hid[part] = dot(swap[part - 1], hid[0]).astype(BF16)
    for i in range(2):
        for p, (part, lo, n) in enumerate(ROUNDS[i]):
            sent(outg, lo, n, d_s.at[i * 3 + p])
            whole_gather = toks.at[pl.ds(0, 7), :, pl.ds(lo, n)]
            whole(whole_gather, g_s.at[i * 3 + p])
            value = dot(hid[part], wdown[:, pl.ds(lo, n)])
            outg[:, :, :, pl.ds(lo, n)] = value.astype(BF16).reshape(4, 4, 32, n)
        exchange(i, outg, lambda part: part4, t_s, t_r)

    for i in range(2):
        for p, (part, lo, n) in enumerate(ROUNDS[i]):
            at = i * 3 + p
            whole(block(part4, lo, n), t_r.at[at])
            value = dot(wgt[part], flat(part4, lo, n))
            psum[:, :, pl.ds(lo, n)] = value.astype(BF16).reshape(8, 32, n)
            own = me.own_line(part) * 2 + me.c
            for step, core in ((0, 1), (1, 0), (3, 0), (1, 1), (3, 1), (2, 0), (2, 1)):
                a, k = up(me.own_line(part), step), lax.rem(me.c + core, 2)
                send(
                    psum.at[a * 2 + k, :, pl.ds(lo, n)], recv.at[own, :, pl.ds(lo, n)],
                    c_s.at[at], c_r.at[at], me.line(part, a, k),
                )
            pltpu.make_async_copy(
                psum.at[own, :, pl.ds(lo, n)], recv.at[own, :, pl.ds(lo, n)], c_r.at[at]
            ).start()
    for i in range(2):
        for p, (part, lo, n) in enumerate(ROUNDS[i]):
            at = i * 3 + p
            whole(recv.at[:, :, pl.ds(lo, n)], c_r.at[at])
            total = stream[:, pl.ds(lo, n)]
            for q in range(8):
                total += recv[q, :, pl.ds(lo, n)].astype(F32)
            out_ref[:, pl.ds(lo, n)] = total.astype(BF16)
    for i in range(2):
        for p, (part, lo, n) in enumerate(ROUNDS[i]):
            at = i * 3 + p
            sent(outg, lo, n, t_s.at[at])
            whole(psum.at[pl.ds(0, 7), :, pl.ds(lo, n)], c_s.at[at])
    for part in range(3):
        whole(metas.at[part, pl.ds(0, 7)], m_s.at[part])


def back(head_out, out_proj, resid, norm_gain, meta, expert_in, expert_down):
    vmem = pl.BlockSpec(memory_space=pltpu.VMEM)
    hbm = pl.BlockSpec(memory_space=pl.ANY)
    dma = pltpu.SemaphoreType.DMA
    grid_rows = (4, 4, 32, 3584)
    return pl.pallas_call(
        back_kernel,
        out_shape=jax.ShapeDtypeStruct((32, 3584), BF16),
        in_specs=[vmem, vmem, vmem, vmem, vmem, hbm, hbm],
        out_specs=vmem,
        scratch_shapes=[
            pltpu.VMEM((3584, 2048), BF16),
            pltpu.VMEM((1024, 3584), BF16),
            pltpu.VMEM(grid_rows, BF16),
            pltpu.VMEM((2, 4, 32, 896), BF16),
            pltpu.VMEM((2, 4, 32, 896), BF16),
            pltpu.VMEM((2, 4, 32, 1792), BF16),
            pltpu.VMEM((2, 4, 32, 1792), BF16),
            pltpu.VMEM((2, 4, 32, 1792), BF16),
            pltpu.VMEM((2, 32, 896), BF16),
            pltpu.VMEM((2, 32, 896), BF16),
            pltpu.VMEM((2, 32, 1792), BF16),
            pltpu.VMEM((2, 32, 1792), BF16),
            pltpu.VMEM((3, 8, 32, 128), F32),
            pltpu.VMEM((3, 512, 256), BF16),
            pltpu.VMEM((3, 256, 512), BF16),
            pltpu.VMEM((2, 512, 512), BF16),
            pltpu.VMEM((32, 3584), F32),
            pltpu.VMEM((32, 3584), BF16),
            pltpu.VMEM((8, 32, 3584), BF16),
            pltpu.VMEM(grid_rows, BF16),
            pltpu.VMEM(grid_rows, BF16),
            pltpu.VMEM(grid_rows, BF16),
            pltpu.VMEM((512, 2048), F32),
            pltpu.VMEM((3, 512, 1024), BF16),
            pltpu.VMEM((8, 32, 3584), BF16),
            pltpu.VMEM((8, 32, 3584), BF16),
            dma((3,)),
            dma((24,)),
            dma((24,)),
            dma((3,)),
            dma((3,)),
            dma((6,)),
            dma((6,)),
            dma((6,)),
            dma((6,)),
            dma((6,)),
            dma((6,)),
            dma((6,)),
            dma((6,)),
        ],
        compiler_params=pltpu.CompilerParams(
            collective_id=1, has_side_effects=True, vmem_limit_bytes=67043328
        ),
        name="back",
    )(head_out, out_proj, resid, norm_gain, meta, expert_in, expert_down)


def shards(
    queries,
    cache,
    offsets,
    value_up,
    out_proj,
    resid,
    norm_gain,
    routes,
    route_weights,
    expert_in,
    expert_down,
):
    heads_dev = value_up.shape[0]
    latent_width = value_up.shape[1]
    key_width = cache.shape[2]
    tok_grp = queries.shape[0]
    score_scale = (value_up.shape[2] + key_width - latent_width) ** (-0.5)
    query_heads = queries.reshape(tok_grp, heads_dev, key_width)
    start_pos = offsets[0]
    query_pos = start_pos + jnp.arange(tok_grp, dtype=jnp.int32)
    key_rows = lax.all_gather(cache, "tensor", axis=1, tiled=True)[0]
    key_count = key_rows.shape[0]
    scores = (
        jnp.einsum("thc,kc->htk", query_heads, key_rows, preferred_element_type=jnp.float32)
        * score_scale
    )
    key_pos = jnp.arange(key_count, dtype=jnp.int32)
    visible = key_pos[None, :] <= query_pos[:, None]
    scores = jnp.where(visible[None], scores, jnp.float32(-1e30))
    highest = jnp.max(scores, axis=2)
    weights = jnp.where(visible[None], jnp.exp(scores - highest[..., None]), jnp.float32(0.0))
    totals = jnp.sum(weights, axis=2)
    weighted = jnp.einsum(
        "htk,kc->htc",
        weights.astype(jnp.bfloat16),
        key_rows[:, :latent_width],
        preferred_element_type=jnp.float32,
    )
    context = (weighted / totals[..., None]).astype(jnp.bfloat16)
    head_out = jnp.einsum("htc,hcv->thv", context, value_up, preferred_element_type=jnp.float32)
    head_out = head_out.astype(jnp.bfloat16).reshape(4, 4, 32, -1)
    wide = lax.all_gather(out_proj, "dp", axis=1, tiled=True)
    meta = jnp.concatenate([routes.astype(F32), route_weights], axis=1)
    meta = jnp.pad(meta, ((0, 0), (0, 112)))
    return back(head_out, wide, resid, norm_gain[None], meta, expert_in[0], expert_down[0])


def solution(mesh):
    return jax.shard_map(
        shards,
        mesh=mesh,
        in_specs=(
            P("dp", "tensor"),
            P("dp", "tensor", None),
            P("dp"),
            P("tensor", None, None),
            P("tensor", "dp"),
            P(("dp", "tensor"), None),
            P(),
            P(("dp", "tensor"), None),
            P(("dp", "tensor"), None),
            P(("dp", "tensor"), None, None),
            P(("dp", "tensor"), None, None),
        ),
        out_specs=P(("dp", "tensor"), None),
        check_vma=False,
    )
```

```python
import functools

import jax
import jax.numpy as jnp
from jax import lax
from jax.experimental import pallas as pl
from jax.experimental.pallas import tpu as pltpu
from jax.sharding import PartitionSpec as P

MESH = pl.DeviceIdType.MESH
LOG2_E = 1.4426950408889634
BF16, F32, I32 = jnp.bfloat16, jnp.float32, jnp.int32
NEAR = (
    (1, 0), (0, 1), (3, 0), (0, 3), (1, 1), (3, 3), (1, 3), (3, 1),
    (2, 0), (0, 2), (2, 2), (2, 1), (1, 2), (2, 3), (3, 2),
)
ROUNDS = (
    ((0, 0, 640), (1, 640, 640), (2, 1280, 512)),
    ((0, 1792, 640), (1, 2432, 512), (2, 2944, 640)),
)


def whole(ref, sem):
    pltpu.make_async_copy(ref, ref, sem).wait()


def dot(a, b):
    return jnp.dot(a, b, preferred_element_type=F32)


class Place:
    def __init__(self):
        dp, t = lax.axis_index("dp"), lax.axis_index("tensor")
        self.z, self.c = lax.div(dp, 2), lax.rem(dp, 2)
        self.x, self.y = lax.div(t, 4), lax.rem(t, 4)

    def line(self, part, a, core):
        if part == 0:
            return (a * 2 + core, self.x * 4 + self.y)
        if part == 1:
            return (self.z * 2 + core, a * 4 + self.y)
        return (self.z * 2 + core, self.x * 4 + a)

    def own_line(self, part):
        return (self.z, self.x, self.y)[part]

    def plane(self, part, b1, b2):
        if part == 0:
            return (self.z * 2 + self.c, b1 * 4 + b2)
        if part == 1:
            return (b1 * 2 + self.c, self.x * 4 + b2)
        return (b2 * 2 + self.c, b1 * 4 + self.y)

    def own_plane(self, part):
        return ((self.x, self.y), (self.z, self.y), (self.x, self.z))[part]

    def expert(self, part, j):
        b1, b2 = j // 4, j % 4
        if part == 0:
            return (self.z * 2 + self.c) * 16 + j
        if part == 1:
            return (b1 * 2 + self.c) * 16 + self.x * 4 + b2
        return (b2 * 2 + self.c) * 16 + b1 * 4 + self.y


def up(v, n):
    return lax.rem(v + n, 4)


def partners(me):
    out = [(me.z * 2 + 1 - me.c, me.x * 4 + me.y)]
    for part in range(3):
        for n in (1, 2, 3):
            out.append(me.line(part, up(me.own_line(part), n), 1 - me.c))
    for dz in range(4):
        for dx in range(4):
            for dy in range(4):
                if (dz, dx, dy) != (0, 0, 0) and 0 in (dz, dx, dy):
                    out.append((up(me.z, dz) * 2 + me.c, up(me.x, dx) * 4 + up(me.y, dy)))
    return out


def back_kernel(
    ho_ref, wo_ref, resid_ref, gain_ref, meta_ref, win_hbm, wdown_hbm,
    out_ref,
    win, wdown, part4, r1, l1, r2, l2, mid, r1b, l1b, r2b, l2b,
    metas, pick, wgt, swap, stream, nrm, toks, outg, rows, stage, acc, hid, psum, recv,
    wsem, rs_s, rs_r, m_s, m_r, g_s, g_r, d_s, d_r, t_s, t_r, c_s, c_r,
):
    me = Place()
    loads = [
        pltpu.make_async_copy(win_hbm.at[pl.ds(0, 1792)], win.at[pl.ds(0, 1792)], wsem.at[0]),
        pltpu.make_async_copy(win_hbm.at[pl.ds(1792, 1792)], win.at[pl.ds(1792, 1792)], wsem.at[1]),
        pltpu.make_async_copy(wdown_hbm, wdown, wsem.at[2]),
    ]
    for load in loads:
        load.start()

    barrier = pltpu.get_barrier_semaphore()
    others = partners(me)
    for other in others:
        pl.semaphore_signal(barrier, inc=1, device_id=other, device_id_type=MESH)
    pl.semaphore_wait(barrier, len(others))

    def send(src, dst, ssem, rsem, device):
        copy = pltpu.make_async_remote_copy(
            src_ref=src, dst_ref=dst, send_sem=ssem, recv_sem=rsem,
            device_id=device, device_id_type=MESH,
        )
        copy.start()
        return copy

    def half_cols(h):
        return pl.ds(h * 1792, 1792)

    def group(h, k, lo, n):
        cols = pl.ds(h * 1792 + lo, n)
        return part4.at[k, :, :, cols] if h == 0 else part4.at[:, k, :, cols]

    def project(h, k):
        head = ho_ref[k] if h == 0 else ho_ref[:, k]
        for b in range(2):
            value = dot(head.reshape(128, 512), wo_ref[2 * h + b])
            group(h, k, b * 896, 896)[...] = value.astype(BF16).reshape(4, 32, 896)

    def neighbour(h, phase, n):
        along_x = (h == 0) == (phase == 0)
        if along_x:
            return (me.z * 2 + me.c, up(me.x, n) * 4 + me.y)
        return (me.z * 2 + me.c, me.x * 4 + up(me.y, n))

    def position(h, phase):
        return me.x if (h == 0) == (phase == 0) else me.y

    def piece(h, phase, k, lo, n):
        return group(h, k, lo, n) if phase == 0 else mid.at[h, k, :, pl.ds(lo, n)]

    def boxes(phase):
        return (r1, l1, r2, l2) if phase == 0 else (r1b, l1b, r2b, l2b)

    def box(ref, h, phase, lo, n):
        if phase == 0:
            return ref.at[h, :, :, pl.ds(lo, n)]
        return ref.at[h, :, pl.ds(lo, n)]

    started = {}

    def first_far(h, phase):
        k = up(position(h, phase), 2)
        br1, bl1, _, _ = boxes(phase)
        for side, (ref, lo, n) in enumerate(((br1, 0, 1), (bl1, 896, 3))):
            i = (h * 2 + phase) * 6 + side
            started[h, phase, side] = send(
                piece(h, phase, k, lo, 896), box(ref, h, phase, 0, 896),
                rs_s.at[i], rs_r.at[i], neighbour(h, phase, n),
            )

    def first_near(h, phase):
        _, _, br2, bl2 = boxes(phase)
        for side, (ref, lo, n) in enumerate(((br2, 896, 1), (bl2, 0, 3))):
            i = (h * 2 + phase) * 6 + 2 + side
            started[h, phase, 2 + side] = send(
                piece(h, phase, up(position(h, phase), n), lo, 896), box(ref, h, phase, lo, 896),
                rs_s.at[i], rs_r.at[i], neighbour(h, phase, n),
            )

    def second(h, phase):
        br1, bl1, br2, bl2 = boxes(phase)
        for side, (ref, to, lo, n) in enumerate(((br1, br2, 0, 1), (bl1, bl2, 896, 3))):
            i = (h * 2 + phase) * 6 + 4 + side
            started[h, phase, side].wait_recv()
            mine = piece(h, phase, up(position(h, phase), n), lo, 896)
            mine[...] = (mine[...].astype(F32) + box(ref, h, phase, 0, 896)[...].astype(F32)).astype(BF16)
            started[h, phase, 4 + side] = send(
                mine, box(to, h, phase, lo, 896), rs_s.at[i], rs_r.at[i], neighbour(h, phase, n)
            )

    def last(h, phase):
        for i in (2, 3, 4, 5):
            started[h, phase, i].wait_recv()
        _, _, br2, bl2 = boxes(phase)
        total = piece(h, phase, position(h, phase), 0, 1792)[...].astype(F32)
        total += box(br2, h, phase, 0, 1792)[...].astype(F32)
        return total + box(bl2, h, phase, 0, 1792)[...].astype(F32)

    meta_sends = []
    for part in range(3):
        own = me.own_line(part) * 2 + me.c
        for n in range(4):
            for core in range(2):
                if (n, core) == (0, 0):
                    continue
                to = me.line(part, up(me.own_line(part), n), lax.rem(me.c + core, 2))
                meta_sends.append(send(meta_ref, metas.at[part, own], m_s.at[part], m_r.at[part], to))
        pltpu.make_async_copy(meta_ref, metas.at[part, own], m_r.at[part]).start()

    for h in range(2):
        project(h, up(position(h, 0), 2))
    for h in range(2):
        first_far(h, 0)
    for n in (1, 3):
        for h in range(2):
            project(h, up(position(h, 0), n))
    for h in range(2):
        first_near(h, 0)
    for h in range(2):
        project(h, position(h, 0))

    token = lax.broadcasted_iota(I32, (256, 256), 0)
    other = lax.broadcasted_iota(I32, (256, 256), 1)
    earlier = jnp.where((token // 32 == other // 32) & (other < token), 1.0, 0.0).astype(BF16)
    lane = lax.broadcasted_iota(I32, (128, 512), 1)
    spread = jnp.where(lane // 32 == lax.broadcasted_iota(I32, (128, 512), 0), 1.0, 0.0).astype(BF16)
    slot = lax.broadcasted_iota(I32, (256, 512), 1) % 32
    of_source = slot // 4 == lax.broadcasted_iota(I32, (256, 512), 0) // 32
    rank_wanted = (slot % 4).astype(F32)
    for part in range(3):
        whole(metas.at[part], m_r.at[part])
        table = metas[part].reshape(256, 128)
        column = lax.broadcasted_iota(I32, (256, 128), 1)
        wanted = jnp.where(column < 16, me.expert(part, column), -1).astype(F32)
        hit = jnp.zeros((256, 128), F32)
        weight = jnp.zeros((256, 128), F32)
        for k in range(8):
            same = table[:, k : k + 1] == wanted
            hit = jnp.where(same, 1.0, hit)
            weight = jnp.where(same, table[:, 8 + k : 9 + k], weight)
        rank = dot(earlier, hit.astype(BF16))
        rank = jnp.where(hit > 0.5, rank, -1.0)
        chosen = (dot(rank.astype(BF16), spread) == rank_wanted) & of_source
        pick[part] = jnp.where(chosen, 1.0, 0.0).T.astype(BF16)
        wgt[part] = jnp.where(chosen, dot(weight.astype(BF16), spread), 0.0).astype(BF16)
    row = lax.broadcasted_iota(I32, (512, 512), 0)
    col = lax.broadcasted_iota(I32, (512, 512), 1)
    rx, ry, rz, low = row // 128, (row // 32) % 4, (row // 8) % 4, row % 8
    swap[0] = jnp.where(col == rz * 128 + ry * 32 + rx * 8 + low, 1.0, 0.0).astype(BF16)
    swap[1] = jnp.where(col == rx * 128 + rz * 32 + ry * 8 + low, 1.0, 0.0).astype(BF16)

    for h in range(2):
        second(h, 0)
    for h in range(2):
        mid[h] = last(h, 0).astype(BF16)
    for h in range(2):
        first_far(h, 1)
    for h in range(2):
        first_near(h, 1)
    for h in range(2):
        second(h, 1)
    for h in range(2):
        stream[:, half_cols(h)] = last(h, 1) + resid_ref[:, half_cols(h)].astype(F32)
    value = stream[...]
    mean_square = jnp.mean(value * value, axis=1, keepdims=True)
    nrm[...] = (value * lax.rsqrt(mean_square + 1e-06) * gain_ref[...]).astype(BF16)
    for copy in started.values():
        copy.wait_send()

    def gather(i):
        for p, (part, lo, n) in enumerate(ROUNDS[i]):
            own = me.own_line(part) * 2 + me.c
            at = i * 3 + p
            for step, core in ((0, 1), (1, 0), (3, 0), (1, 1), (3, 1), (2, 0), (2, 1)):
                to = me.line(part, up(me.own_line(part), step), lax.rem(me.c + core, 2))
                send(nrm.at[:, pl.ds(lo, n)], toks.at[own, :, pl.ds(lo, n)], g_s.at[at], g_r.at[at], to)
            pltpu.make_async_copy(nrm.at[:, pl.ds(lo, n)], toks.at[own, :, pl.ds(lo, n)], g_r.at[at]).start()

    def flat(ref, lo, n):
        return ref[:, :, :, pl.ds(lo, n)].reshape(512, n)

    def exchange(i, src, dst_of, ssem, rsem):
        for d1, d2 in NEAR:
            for p, (part, lo, n) in enumerate(ROUNDS[i]):
                b1, b2 = me.own_plane(part)
                e1, e2 = up(b1, d1), up(b2, d2)
                send(
                    src.at[e1, e2, :, pl.ds(lo, n)], dst_of(part).at[b1, b2, :, pl.ds(lo, n)],
                    ssem.at[i * 3 + p], rsem.at[i * 3 + p], me.plane(part, e1, e2),
                )
        for p, (part, lo, n) in enumerate(ROUNDS[i]):
            b1, b2 = me.own_plane(part)
            pltpu.make_async_copy(
                src.at[b1, b2, :, pl.ds(lo, n)], dst_of(part).at[b1, b2, :, pl.ds(lo, n)],
                rsem.at[i * 3 + p],
            ).start()

    def landing(part):
        return rows if part == 0 else stage

    def block(ref, lo, n):
        return ref.at[:, :, :, pl.ds(lo, n)]

    def sent(ref, lo, n, sem):
        for k in range(3):
            whole(ref.at[k, :, :, pl.ds(lo, n)], sem)
        whole(ref.at[3, pl.ds(0, 3), :, pl.ds(lo, n)], sem)

    def dispatch(i):
        for p, (part, lo, n) in enumerate(ROUNDS[i]):
            whole(toks.at[:, :, pl.ds(lo, n)], g_r.at[i * 3 + p])
            value = dot(pick[part], toks[:, :, pl.ds(lo, n)].reshape(256, n))
            outg[:, :, :, pl.ds(lo, n)] = value.astype(BF16).reshape(4, 4, 32, n)
        exchange(i, outg, landing, d_s, d_r)

    def arrive(i):
        for p, (part, lo, n) in enumerate(ROUNDS[i]):
            whole(block(landing(part), lo, n), d_r.at[i * 3 + p])
            if part:
                value = dot(swap[part - 1], flat(stage, lo, n))
                rows[:, :, :, pl.ds(lo, n)] = value.astype(BF16).reshape(4, 4, 32, n)

    gather(0)
    gather(1)
    dispatch(0)
    dispatch(1)

    loads[0].wait()
    arrive(0)

    def first_half(j, carry):
        cols = pl.ds(pl.multiple_of(j * 256, 256), 256)
        acc[:, cols] = dot(flat(rows, 0, 1792), win[pl.ds(0, 1792), cols])
        return carry

    lax.fori_loop(0, 8, first_half, 0)
    loads[1].wait()
    arrive(1)

    def second_half(j, carry):
        cols = pl.ds(pl.multiple_of(j * 256, 256), 256)
        more = pl.ds(pl.multiple_of(j * 256 + 1024, 256), 256)
        gate = acc[:, cols] + dot(flat(rows, 1792, 1792), win[pl.ds(1792, 1792), cols])
        lift = acc[:, more] + dot(flat(rows, 1792, 1792), win[pl.ds(1792, 1792), more])
        hid[0, :, cols] = (gate / (1.0 + jnp.exp(-gate)) * lift).astype(BF16)
        return carry

    lax.fori_loop(0, 4, second_half, 0)
    loads[2].wait()
    for part in (1, 2):
        hid[part] = dot(swap[part - 1], hid[0]).astype(BF16)
    for i in range(2):
        for p, (part, lo, n) in enumerate(ROUNDS[i]):
            sent(outg, lo, n, d_s.at[i * 3 + p])
            whole_gather = toks.at[pl.ds(0, 7), :, pl.ds(lo, n)]
            whole(whole_gather, g_s.at[i * 3 + p])
            value = dot(hid[part], wdown[:, pl.ds(lo, n)])
            outg[:, :, :, pl.ds(lo, n)] = value.astype(BF16).reshape(4, 4, 32, n)
        exchange(i, outg, lambda part: part4, t_s, t_r)

    for i in range(2):
        for p, (part, lo, n) in enumerate(ROUNDS[i]):
            at = i * 3 + p
            whole(block(part4, lo, n), t_r.at[at])
            value = dot(wgt[part], flat(part4, lo, n))
            psum[:, :, pl.ds(lo, n)] = value.astype(BF16).reshape(8, 32, n)
            own = me.own_line(part) * 2 + me.c
            for step, core in ((0, 1), (1, 0), (3, 0), (1, 1), (3, 1), (2, 0), (2, 1)):
                a, k = up(me.own_line(part), step), lax.rem(me.c + core, 2)
                send(
                    psum.at[a * 2 + k, :, pl.ds(lo, n)], recv.at[own, :, pl.ds(lo, n)],
                    c_s.at[at], c_r.at[at], me.line(part, a, k),
                )
            pltpu.make_async_copy(
                psum.at[own, :, pl.ds(lo, n)], recv.at[own, :, pl.ds(lo, n)], c_r.at[at]
            ).start()
    for i in range(2):
        for p, (part, lo, n) in enumerate(ROUNDS[i]):
            at = i * 3 + p
            whole(recv.at[:, :, pl.ds(lo, n)], c_r.at[at])
            total = stream[:, pl.ds(lo, n)]
            for q in range(8):
                total += recv[q, :, pl.ds(lo, n)].astype(F32)
            out_ref[:, pl.ds(lo, n)] = total.astype(BF16)
    for i in range(2):
        for p, (part, lo, n) in enumerate(ROUNDS[i]):
            at = i * 3 + p
            sent(outg, lo, n, t_s.at[at])
            whole(psum.at[pl.ds(0, 7), :, pl.ds(lo, n)], c_s.at[at])
    for part in range(3):
        whole(metas.at[part, pl.ds(0, 7)], m_s.at[part])


def back(head_out, out_proj, resid, norm_gain, meta, expert_in, expert_down):
    vmem = pl.BlockSpec(memory_space=pltpu.VMEM)
    hbm = pl.BlockSpec(memory_space=pl.ANY)
    dma = pltpu.SemaphoreType.DMA
    grid_rows = (4, 4, 32, 3584)
    return pl.pallas_call(
        back_kernel,
        out_shape=jax.ShapeDtypeStruct((32, 3584), BF16),
        in_specs=[vmem, vmem, vmem, vmem, vmem, hbm, hbm],
        out_specs=vmem,
        scratch_shapes=[
            pltpu.VMEM((3584, 2048), BF16),
            pltpu.VMEM((1024, 3584), BF16),
            pltpu.VMEM(grid_rows, BF16),
            pltpu.VMEM((2, 4, 32, 896), BF16),
            pltpu.VMEM((2, 4, 32, 896), BF16),
            pltpu.VMEM((2, 4, 32, 1792), BF16),
            pltpu.VMEM((2, 4, 32, 1792), BF16),
            pltpu.VMEM((2, 4, 32, 1792), BF16),
            pltpu.VMEM((2, 32, 896), BF16),
            pltpu.VMEM((2, 32, 896), BF16),
            pltpu.VMEM((2, 32, 1792), BF16),
            pltpu.VMEM((2, 32, 1792), BF16),
            pltpu.VMEM((3, 8, 32, 128), F32),
            pltpu.VMEM((3, 512, 256), BF16),
            pltpu.VMEM((3, 256, 512), BF16),
            pltpu.VMEM((2, 512, 512), BF16),
            pltpu.VMEM((32, 3584), F32),
            pltpu.VMEM((32, 3584), BF16),
            pltpu.VMEM((8, 32, 3584), BF16),
            pltpu.VMEM(grid_rows, BF16),
            pltpu.VMEM(grid_rows, BF16),
            pltpu.VMEM(grid_rows, BF16),
            pltpu.VMEM((512, 2048), F32),
            pltpu.VMEM((3, 512, 1024), BF16),
            pltpu.VMEM((8, 32, 3584), BF16),
            pltpu.VMEM((8, 32, 3584), BF16),
            dma((3,)),
            dma((24,)),
            dma((24,)),
            dma((3,)),
            dma((3,)),
            dma((6,)),
            dma((6,)),
            dma((6,)),
            dma((6,)),
            dma((6,)),
            dma((6,)),
            dma((6,)),
            dma((6,)),
        ],
        compiler_params=pltpu.CompilerParams(
            collective_id=1, has_side_effects=True, vmem_limit_bytes=67043328
        ),
        name="back",
    )(head_out, out_proj, resid, norm_gain, meta, expert_in, expert_down)


LOWEST = -1e30


def front_kernel(
    scale, off_ref, q_ref, cache_ref, vup_ref, wo_ref,
    ho_ref, wide_ref,
    keys, kc, vt, qt, vupt, bias, acc, top, tot, pair,
    k_s, k_r, w_s, w_r, own_sem,
):
    me = Place()
    here = me.z * 2 + me.c

    def along(axis, n):
        if axis == 0:
            return (here, up(me.x, n) * 4 + me.y)
        return (here, me.x * 4 + up(me.y, n))

    own_copy = pltpu.make_async_copy(cache_ref, keys.at[me.x, me.y], own_sem)
    own_copy.start()

    twin = (me.z * 2 + 1 - me.c, me.x * 4 + me.y)
    above = [(up(me.z, n) * 2 + me.c, me.x * 4 + me.y) for n in (1, 3, 2)]
    others = [along(0, 1), along(0, 3), along(1, 1), along(1, 3), twin] + above
    barrier = pltpu.get_barrier_semaphore()
    for other in others:
        pl.semaphore_signal(barrier, inc=1, device_id=other, device_id_type=MESH)
    pl.semaphore_wait(barrier, len(others))

    def send(src, dst, ssem, rsem, device):
        copy = pltpu.make_async_remote_copy(
            src_ref=src, dst_ref=dst, send_sem=ssem, recv_sem=rsem,
            device_id=device, device_id_type=MESH,
        )
        copy.start()
        return copy

    def axis_of(half, phase):
        return half if phase == 0 else 1 - half

    def spot(half, phase, n, lo, rows):
        rows = pl.ds(half * 96 + lo, rows)
        if axis_of(half, phase) == 0:
            a = up(me.x, n)
            return keys.at[a, me.y, rows] if phase == 0 else keys.at[a, :, rows]
        b = up(me.y, n)
        return keys.at[me.x, b, rows] if phase == 0 else keys.at[:, b, rows]

    def sem(half, phase, k):
        return (half * 2 + phase) * 4 + k

    def spread(half, phase):
        axis = axis_of(half, phase)
        for k, n in ((0, 1), (1, 3)):
            at = spot(half, phase, 0, 0, 96)
            src = cache_ref.at[pl.ds(half * 96, 96)] if phase == 0 else at
            i = sem(half, phase, k)
            send(src, at, k_s.at[i], k_r.at[i], along(axis, n))

    def forward(half, phase):
        axis = axis_of(half, phase)
        for k, n, lo in ((0, 3, 0), (1, 1, 48)):
            whole(spot(half, phase, n, 0, 96), k_r.at[sem(half, phase, k)])
            part = spot(half, phase, n, lo, 48)
            i = sem(half, phase, 2 + k)
            send(part, part, k_s.at[i], k_r.at[i], along(axis, 4 - n))

    def far(half, phase):
        for k, lo in ((0, 0), (1, 48)):
            whole(spot(half, phase, 2, lo, 48), k_r.at[sem(half, phase, 2 + k)])

    for half in range(2):
        spread(half, 0)
    send(wo_ref, pair, w_s.at[0], w_r.at[0], twin)

    qt[:, pl.ds(576, 64), :] = jnp.zeros((4, 64, 512), BF16)
    for h in range(2):
        lo = h * 1152
        qt[2 * h, pl.ds(0, 576), :] = q_ref[:, lo : lo + 640].T[:576]
        qt[2 * h + 1, pl.ds(0, 576), :] = q_ref[:, lo + 512 : lo + 1152].T[64:]
    for half in range(2):
        forward(half, 0)
    for h in range(4):
        vupt[h] = vup_ref[h].T
    kc[:, pl.ds(512, 128)] = jnp.zeros((768, 128), BF16)
    top[...] = jnp.full((4, 1, 512), -3e38, F32)
    tot[...] = jnp.zeros((4, 1, 512), F32)
    acc[...] = jnp.zeros((4, 512, 512), F32)
    whole(pair, w_r.at[0])
    first = wo_ref[...]
    second = pair[...]
    low = jnp.where(me.c == 0, first, second)
    high = jnp.where(me.c == 0, second, first)
    wide_ref[me.z] = jnp.concatenate([low, high], axis=1)
    own_copy.wait()
    for half in range(2):
        far(half, 0)
    for half in range(2):
        spread(half, 1)
    rows = pl.ds(pl.multiple_of(me.c * 256, 256), 256)
    for k, to in enumerate(above):
        send(wide_ref.at[me.z, rows], wide_ref.at[me.z, rows], w_s.at[1 + k], w_r.at[1 + k], to)

    row = lax.broadcasted_iota(I32, (768, 1), 0)
    in_first = row < 384
    low_row = jnp.where(in_first, row, row - 384)
    nth = (low_row >= 96).astype(I32) + (low_row >= 192).astype(I32) + (low_row >= 288).astype(I32)
    low_row = low_row - nth * 96
    base = jnp.where(in_first, nth * 768 + low_row, nth * 192 + 96 + low_row)
    query = lax.broadcasted_iota(I32, (768, 512), 1)

    def step(i, carry):
        @pl.when(i == 1)
        def _():
            for half in range(2):
                forward(half, 1)

        @pl.when(i == 3)
        def _():
            for half in range(2):
                far(half, 1)
            for k, n in enumerate((3, 1, 2)):
                z = up(me.z, n)
                got = wide_ref.at[z, rows]
                whole(got, w_r.at[1 + k])
                send(got, got, w_s.at[4 + k], w_r.at[4 + k], twin)

        turn = i + lax.div(i, 2) - 2 * lax.div(i, 3)
        b, a = up(me.y, turn), up(me.x, turn)
        kc[pl.ds(0, 384), pl.ds(0, 576)] = keys[:, b, pl.ds(0, 96), :].reshape(384, 576)
        kc[pl.ds(384, 384), pl.ds(0, 576)] = keys[a, :, pl.ds(96, 96), :].reshape(384, 576)
        vt[...] = kc[:, pl.ds(0, 512)].T
        start = jnp.where(in_first, b * 192, a * 768)
        bias[...] = jnp.where(base + start - off_ref[0] <= query, 0.0, LOWEST)
        for h in range(4):
            s = dot(kc[...], qt[h]) * scale + bias[...]
            old = top[h]
            new = jnp.maximum(old, jnp.max(s, axis=0, keepdims=True))
            p = jnp.exp2(s - new)
            shrink = jnp.exp2(old - new)
            top[h] = new
            tot[h] = tot[h] * shrink + jnp.sum(p, axis=0, keepdims=True)
            acc[h] = acc[h] * shrink + dot(vt[...], p.astype(BF16))
        return carry

    lax.fori_loop(0, 4, step, 0)
    for h in range(4):
        context = (acc[h] / tot[h]).astype(BF16)
        value = dot(vupt[h], context).T.astype(BF16)
        ho_ref[:, :, :, pl.ds(h * 128, 128)] = value.reshape(4, 4, 32, 128)
    rest = pl.ds(pl.multiple_of(256 - me.c * 256, 256), 256)
    for k, n in enumerate((3, 1, 2)):
        z = up(me.z, n)
        whole(wide_ref.at[z, rest], w_r.at[4 + k])
        whole(wide_ref.at[z, rows], w_s.at[4 + k])
        whole(wide_ref.at[me.z, rows], w_s.at[1 + k])
    whole(wo_ref, w_s.at[0])
    for half in range(2):
        for phase in range(2):
            for k in range(2):
                whole(spot(half, phase, 0, 0, 96), k_s.at[sem(half, phase, k)])
                whole(spot(half, phase, 0, 0, 48), k_s.at[sem(half, phase, 2 + k)])


def front(offsets, queries, cache, value_up, out_proj, scale):
    vmem = pl.BlockSpec(memory_space=pltpu.VMEM)
    dma = pltpu.SemaphoreType.DMA
    return pl.pallas_call(
        functools.partial(front_kernel, scale),
        out_shape=(
            jax.ShapeDtypeStruct((4, 4, 32, 512), BF16),
            jax.ShapeDtypeStruct((4, 512, 896), BF16),
        ),
        in_specs=[pl.BlockSpec(memory_space=pltpu.SMEM), vmem, vmem, vmem, vmem],
        out_specs=(vmem, vmem),
        scratch_shapes=[
            pltpu.VMEM((4, 4, 192, 576), BF16),
            pltpu.VMEM((768, 640), BF16),
            pltpu.VMEM((512, 768), BF16),
            pltpu.VMEM((4, 640, 512), BF16),
            pltpu.VMEM((4, 128, 512), BF16),
            pltpu.VMEM((768, 512), F32),
            pltpu.VMEM((4, 512, 512), F32),
            pltpu.VMEM((4, 1, 512), F32),
            pltpu.VMEM((4, 1, 512), F32),
            pltpu.VMEM((512, 448), BF16),
            dma((16,)),
            dma((16,)),
            dma((7,)),
            dma((7,)),
            dma(()),
        ],
        compiler_params=pltpu.CompilerParams(
            collective_id=2, has_side_effects=True, vmem_limit_bytes=60 * 1024 * 1024
        ),
        name="front",
    )(offsets, queries, cache, value_up, out_proj)


def shards(
    queries,
    cache,
    offsets,
    value_up,
    out_proj,
    resid,
    norm_gain,
    routes,
    route_weights,
    expert_in,
    expert_down,
):
    latent_width = value_up.shape[1]
    key_width = cache.shape[2]
    score_scale = (value_up.shape[2] + key_width - latent_width) ** (-0.5)
    head_out, wide = front(
        offsets, queries, cache[0], value_up, out_proj, score_scale * LOG2_E
    )
    meta = jnp.concatenate([routes.astype(F32), route_weights], axis=1)
    meta = jnp.pad(meta, ((0, 0), (0, 112)))
    return back(head_out, wide, resid, norm_gain[None], meta, expert_in[0], expert_down[0])


def solution(mesh):
    return jax.shard_map(
        shards,
        mesh=mesh,
        in_specs=(
            P("dp", "tensor"),
            P("dp", "tensor", None),
            P("dp"),
            P("tensor", None, None),
            P("tensor", "dp"),
            P(("dp", "tensor"), None),
            P(),
            P(("dp", "tensor"), None),
            P(("dp", "tensor"), None),
            P(("dp", "tensor"), None, None),
            P(("dp", "tensor"), None, None),
        ),
        out_specs=P(("dp", "tensor"), None),
        check_vma=False,
    )
```

```python
import functools

import jax
import jax.numpy as jnp
from jax import lax
from jax.experimental import pallas as pl
from jax.experimental.pallas import tpu as pltpu
from jax.sharding import PartitionSpec as P

MESH = pl.DeviceIdType.MESH
LOG2_E = 1.4426950408889634
BF16, F32, I32 = jnp.bfloat16, jnp.float32, jnp.int32
NEAR = (
    (1, 0), (0, 1), (3, 0), (0, 3), (1, 1), (3, 3), (1, 3), (3, 1),
    (2, 0), (0, 2), (2, 2), (2, 1), (1, 2), (2, 3), (3, 2),
)
PARTS = ((0, 0, 1280), (1, 1280, 1152), (2, 2432, 1152))


def whole(ref, sem):
    pltpu.make_async_copy(ref, ref, sem).wait()


def dot(a, b):
    return jnp.dot(a, b, preferred_element_type=F32)


class Place:
    def __init__(self):
        dp, t = lax.axis_index("dp"), lax.axis_index("tensor")
        self.z, self.c = lax.div(dp, 2), lax.rem(dp, 2)
        self.x, self.y = lax.div(t, 4), lax.rem(t, 4)

    def line(self, part, a, core):
        if part == 0:
            return (a * 2 + core, self.x * 4 + self.y)
        if part == 1:
            return (self.z * 2 + core, a * 4 + self.y)
        return (self.z * 2 + core, self.x * 4 + a)

    def own_line(self, part):
        return (self.z, self.x, self.y)[part]

    def plane(self, part, b1, b2):
        if part == 0:
            return (self.z * 2 + self.c, b1 * 4 + b2)
        if part == 1:
            return (b1 * 2 + self.c, self.x * 4 + b2)
        return (b2 * 2 + self.c, b1 * 4 + self.y)

    def own_plane(self, part):
        return ((self.x, self.y), (self.z, self.y), (self.x, self.z))[part]

    def expert(self, part, j):
        b1, b2 = j // 4, j % 4
        if part == 0:
            return (self.z * 2 + self.c) * 16 + j
        if part == 1:
            return (b1 * 2 + self.c) * 16 + self.x * 4 + b2
        return (b2 * 2 + self.c) * 16 + b1 * 4 + self.y


def up(v, n):
    return lax.rem(v + n, 4)


def partners(me):
    out = [(me.z * 2 + 1 - me.c, me.x * 4 + me.y)]
    for part in range(3):
        for n in (1, 2, 3):
            out.append(me.line(part, up(me.own_line(part), n), 1 - me.c))
    for dz in range(4):
        for dx in range(4):
            for dy in range(4):
                if (dz, dx, dy) != (0, 0, 0) and 0 in (dz, dx, dy):
                    out.append((up(me.z, dz) * 2 + me.c, up(me.x, dx) * 4 + up(me.y, dy)))
    return out


def back_kernel(
    ho_hbm, wo_hbm, resid_ref, gain_ref, routes_ref, weights_ref, win_hbm, wdown_hbm,
    out_ref,
    ho_ref, wo_ref, win, wdown, part4, r1, l1, r2, l2, mid, r1b, l1b, r2b, l2b,
    turned, table_ref, metas, pick, wgt, swap, stream, nrm, toks, outg, rows, stage, hid, half_sum, psum, recv,
    wsem, rs_s, rs_r, m_s, m_r, g_s, g_r, d_s, d_r, t_s, t_r, c_s, c_r,
):
    me = Place()
    loads = [
        pltpu.make_async_copy(ho_hbm, ho_ref, wsem.at[0]),
        pltpu.make_async_copy(wo_hbm, wo_ref, wsem.at[1]),
        pltpu.make_async_copy(win_hbm, win, wsem.at[2]),
        pltpu.make_async_copy(wdown_hbm, wdown, wsem.at[3]),
    ]
    for load in loads:
        load.start()

    barrier = pltpu.get_barrier_semaphore()
    others = partners(me)
    for other in others:
        pl.semaphore_signal(barrier, inc=1, device_id=other, device_id_type=MESH)
    turned[...] = jnp.zeros((128, 128), F32)
    turned[pl.ds(0, 8), pl.ds(0, 32)] = routes_ref[...].astype(F32)
    turned[pl.ds(8, 8), pl.ds(0, 32)] = weights_ref[...]
    table_ref[...] = turned[...].T[:32]
    pl.semaphore_wait(barrier, len(others))

    def send(src, dst, ssem, rsem, device):
        copy = pltpu.make_async_remote_copy(
            src_ref=src, dst_ref=dst, send_sem=ssem, recv_sem=rsem,
            device_id=device, device_id_type=MESH,
        )
        copy.start()
        return copy

    def half_cols(h):
        return pl.ds(h * 1792, 1792)

    def group(h, k, lo, n):
        cols = pl.ds(h * 1792 + lo, n)
        return part4.at[k, :, :, cols] if h == 0 else part4.at[:, k, :, cols]

    def project(h, k):
        head = ho_ref[k] if h == 0 else ho_ref[:, k]
        for b in range(2):
            value = dot(head.reshape(128, 512), wo_ref[2 * h + b])
            group(h, k, b * 896, 896)[...] = value.astype(BF16).reshape(4, 32, 896)

    def neighbour(h, phase, n):
        along_x = (h == 0) == (phase == 0)
        if along_x:
            return (me.z * 2 + me.c, up(me.x, n) * 4 + me.y)
        return (me.z * 2 + me.c, me.x * 4 + up(me.y, n))

    def position(h, phase):
        return me.x if (h == 0) == (phase == 0) else me.y

    def piece(h, phase, k, lo, n):
        return group(h, k, lo, n) if phase == 0 else mid.at[h, k, :, pl.ds(lo, n)]

    def boxes(phase):
        return (r1, l1, r2, l2) if phase == 0 else (r1b, l1b, r2b, l2b)

    def box(ref, h, phase, lo, n):
        if phase == 0:
            return ref.at[h, :, :, pl.ds(lo, n)]
        return ref.at[h, :, pl.ds(lo, n)]

    started = {}

    def first_far(h, phase):
        k = up(position(h, phase), 2)
        br1, bl1, _, _ = boxes(phase)
        for side, (ref, lo, n) in enumerate(((br1, 0, 1), (bl1, 896, 3))):
            i = (h * 2 + phase) * 6 + side
            started[h, phase, side] = send(
                piece(h, phase, k, lo, 896), box(ref, h, phase, 0, 896),
                rs_s.at[i], rs_r.at[i], neighbour(h, phase, n),
            )

    def first_near(h, phase):
        _, _, br2, bl2 = boxes(phase)
        for side, (ref, lo, n) in enumerate(((br2, 896, 1), (bl2, 0, 3))):
            i = (h * 2 + phase) * 6 + 2 + side
            started[h, phase, 2 + side] = send(
                piece(h, phase, up(position(h, phase), n), lo, 896), box(ref, h, phase, lo, 896),
                rs_s.at[i], rs_r.at[i], neighbour(h, phase, n),
            )

    def second(h, phase):
        br1, bl1, br2, bl2 = boxes(phase)
        for side, (ref, to, lo, n) in enumerate(((br1, br2, 0, 1), (bl1, bl2, 896, 3))):
            i = (h * 2 + phase) * 6 + 4 + side
            started[h, phase, side].wait_recv()
            mine = piece(h, phase, up(position(h, phase), n), lo, 896)
            mine[...] = (mine[...].astype(F32) + box(ref, h, phase, 0, 896)[...].astype(F32)).astype(BF16)
            started[h, phase, 4 + side] = send(
                mine, box(to, h, phase, lo, 896), rs_s.at[i], rs_r.at[i], neighbour(h, phase, n)
            )

    def last(h, phase):
        for i in (2, 3, 4, 5):
            started[h, phase, i].wait_recv()
        _, _, br2, bl2 = boxes(phase)
        total = piece(h, phase, position(h, phase), 0, 1792)[...].astype(F32)
        total += box(br2, h, phase, 0, 1792)[...].astype(F32)
        return total + box(bl2, h, phase, 0, 1792)[...].astype(F32)

    meta_sends = []
    for part in range(3):
        own = me.own_line(part) * 2 + me.c
        for n in range(4):
            for core in range(2):
                if (n, core) == (0, 0):
                    continue
                to = me.line(part, up(me.own_line(part), n), lax.rem(me.c + core, 2))
                meta_sends.append(send(table_ref, metas.at[part, own], m_s.at[part], m_r.at[part], to))
        pltpu.make_async_copy(table_ref, metas.at[part, own], m_r.at[part]).start()

    loads[0].wait()
    loads[1].wait()
    for h in range(2):
        project(h, up(position(h, 0), 2))
    for h in range(2):
        first_far(h, 0)
    for n in (1, 3):
        for h in range(2):
            project(h, up(position(h, 0), n))
    for h in range(2):
        first_near(h, 0)
    for h in range(2):
        project(h, position(h, 0))

    token = lax.broadcasted_iota(I32, (256, 256), 0)
    other = lax.broadcasted_iota(I32, (256, 256), 1)
    earlier = jnp.where((token // 32 == other // 32) & (other < token), 1.0, 0.0).astype(BF16)
    lane = lax.broadcasted_iota(I32, (128, 256), 1)
    spread = jnp.where(lane // 16 == lax.broadcasted_iota(I32, (128, 256), 0), 1.0, 0.0).astype(BF16)
    of_source = other % 16 // 2 == token // 32
    rank_wanted = (other % 2).astype(F32)
    for part in range(3):
        whole(metas.at[part], m_r.at[part])
        table = metas[part].reshape(256, 128)
        column = lax.broadcasted_iota(I32, (256, 128), 1)
        wanted = jnp.where(column < 16, me.expert(part, column), -1).astype(F32)
        hit = jnp.zeros((256, 128), F32)
        weight = jnp.zeros((256, 128), F32)
        for k in range(8):
            same = table[:, k : k + 1] == wanted
            hit = jnp.where(same, 1.0, hit)
            weight = jnp.where(same, table[:, 8 + k : 9 + k], weight)
        rank = dot(earlier, hit.astype(BF16))
        rank = jnp.where(hit > 0.5, rank, -1.0)
        rank = jnp.where(of_source, dot(rank.astype(BF16), spread) - rank_wanted, -1.0)
        weight = dot(weight.astype(BF16), spread)
        for half in range(2):
            chosen = rank == half * 2.0
            pick[part, half] = jnp.where(chosen, 1.0, 0.0).T.astype(BF16)
            wgt[part, half] = jnp.where(chosen, weight, 0.0).astype(BF16)
    rx, ry, rz, low = token // 64, token // 16 % 4, token // 4 % 4, token % 4
    swap[0] = jnp.where(other == rz * 64 + ry * 16 + rx * 4 + low, 1.0, 0.0).astype(BF16)
    swap[1] = jnp.where(other == rx * 64 + rz * 16 + ry * 4 + low, 1.0, 0.0).astype(BF16)

    for h in range(2):
        second(h, 0)
    for h in range(2):
        mid[h] = last(h, 0).astype(BF16)
    for h in range(2):
        first_far(h, 1)
    for h in range(2):
        first_near(h, 1)
    for h in range(2):
        second(h, 1)
    for h in range(2):
        stream[:, half_cols(h)] = last(h, 1) + resid_ref[:, half_cols(h)].astype(F32)
    value = stream[...]
    mean_square = jnp.mean(value * value, axis=1, keepdims=True)
    nrm[...] = (value * lax.rsqrt(mean_square + 1e-06) * gain_ref[...].reshape(1, 3584)).astype(BF16)
    for copy in started.values():
        copy.wait_send()

    LINE = ((0, 1), (1, 0), (3, 0), (1, 1), (3, 1), (2, 0), (2, 1))
    for part, lo, n in PARTS:
        cols = pl.ds(lo, n)
        own = me.own_line(part) * 2 + me.c
        for step, core in LINE:
            to = me.line(part, up(me.own_line(part), step), lax.rem(me.c + core, 2))
            send(nrm.at[:, cols], toks.at[own, :, cols], g_s.at[part], g_r.at[part], to)
        pltpu.make_async_copy(nrm.at[:, cols], toks.at[own, :, cols], g_r.at[part]).start()

    def half_of(ref, half):
        if ref is part4:
            return lambda b1, b2, cols: part4.at[b1, b2, pl.ds(half * 16, 16), cols]
        return lambda b1, b2, cols: ref.at[half, b1, b2, :, cols]

    def exchange(half, src, dst_of, ssem, rsem, parts):
        for d1, d2 in NEAR:
            for part, lo, n in parts:
                b1, b2 = me.own_plane(part)
                e1, e2 = up(b1, d1), up(b2, d2)
                at, cols = half * 3 + part, pl.ds(lo, n)
                send(
                    half_of(src, half)(e1, e2, cols), half_of(dst_of(part), half)(b1, b2, cols),
                    ssem.at[at], rsem.at[at], me.plane(part, e1, e2),
                )
        for part, lo, n in parts:
            b1, b2 = me.own_plane(part)
            at, cols = half * 3 + part, pl.ds(lo, n)
            pltpu.make_async_copy(
                half_of(src, half)(b1, b2, cols), half_of(dst_of(part), half)(b1, b2, cols), rsem.at[at]
            ).start()

    def landing(part):
        return rows if part == 0 else stage

    def sent(half, lo, n, sem):
        for k in range(3):
            whole(outg.at[half, k, :, :, pl.ds(lo, n)], sem)
        whole(outg.at[half, 3, pl.ds(0, 3), :, pl.ds(lo, n)], sem)

    def dispatch(half):
        for part, lo, n in PARTS:
            cols = pl.ds(lo, n)
            if half == 0:
                whole(toks.at[:, :, cols], g_r.at[part])
            value = dot(pick[part, half], toks[:, :, cols].reshape(256, n))
            outg[half, :, :, :, cols] = value.astype(BF16).reshape(4, 4, 16, n)
        exchange(half, outg, landing, d_s, d_r, PARTS)

    def expert(half):
        for part, lo, n in PARTS:
            cols = pl.ds(lo, n)
            whole(landing(part).at[half, :, :, :, cols], d_r.at[half * 3 + part])
            if part:
                value = dot(swap[part - 1], stage[half, :, :, :, cols].reshape(256, n))
                rows[half, :, :, :, cols] = value.astype(BF16).reshape(4, 4, 16, n)
        if half == 0:
            loads[2].wait()
            loads[3].wait()

        def hidden(j, carry):
            cols = pl.ds(pl.multiple_of(j * 256, 256), 256)
            more = pl.ds(pl.multiple_of(j * 256 + 1024, 256), 256)
            here = rows[half].reshape(256, 3584)
            gate = dot(here, win[:, cols])
            lift = dot(here, win[:, more])
            hid[0, :, cols] = (gate / (1.0 + jnp.exp(-gate)) * lift).astype(BF16)
            return carry

        lax.fori_loop(0, 4, hidden, 0)
        for part, lo, n in PARTS:
            if part:
                hid[part] = dot(swap[part - 1], hid[0]).astype(BF16)
            sent(half, lo, n, d_s.at[half * 3 + part])
            value = dot(hid[part], wdown[:, pl.ds(lo, n)])
            outg[half, :, :, :, pl.ds(lo, n)] = value.astype(BF16).reshape(4, 4, 16, n)
            if half:
                exchange(half, outg, lambda part: part4, t_s, t_r, ((part, lo, n),))
        if half == 0:
            exchange(half, outg, lambda part: part4, t_s, t_r, PARTS)

    dispatch(0)
    dispatch(1)
    expert(0)
    expert(1)

    for half in range(2):
        for part, lo, n in PARTS:
            cols = pl.ds(lo, n)
            back_rows = part4.at[:, :, pl.ds(half * 16, 16), cols]
            whole(back_rows, t_r.at[half * 3 + part])
            value = dot(wgt[part, half], back_rows[...].reshape(256, n))
            if half == 0:
                half_sum[:, cols] = value
                continue
            psum[:, :, cols] = (half_sum[:, cols] + value).astype(BF16).reshape(8, 32, n)
            own = me.own_line(part) * 2 + me.c
            for step, core in LINE:
                a, k = up(me.own_line(part), step), lax.rem(me.c + core, 2)
                send(
                    psum.at[a * 2 + k, :, cols], recv.at[own, :, cols],
                    c_s.at[part], c_r.at[part], me.line(part, a, k),
                )
            pltpu.make_async_copy(psum.at[own, :, cols], recv.at[own, :, cols], c_r.at[part]).start()
    for part, lo, n in PARTS:
        cols = pl.ds(lo, n)
        whole(recv.at[:, :, cols], c_r.at[part])
        total = stream[:, cols]
        for q in range(8):
            total += recv[q, :, cols].astype(F32)
        out_ref[:, cols] = total.astype(BF16)
    for part, lo, n in PARTS:
        for half in range(2):
            sent(half, lo, n, t_s.at[half * 3 + part])
        whole(toks.at[pl.ds(0, 7), :, pl.ds(lo, n)], g_s.at[part])
        whole(psum.at[pl.ds(0, 7), :, pl.ds(lo, n)], c_s.at[part])
        whole(metas.at[part, pl.ds(0, 7)], m_s.at[part])


def back(head_out, out_proj, resid, norm_gain, routes, weights, expert_in, expert_down):
    vmem = pl.BlockSpec(memory_space=pltpu.VMEM)
    hbm = pl.BlockSpec(memory_space=pl.ANY)
    dma = pltpu.SemaphoreType.DMA
    halves = (2, 4, 4, 16, 3584)
    return pl.pallas_call(
        back_kernel,
        out_shape=jax.ShapeDtypeStruct((32, 3584), BF16),
        in_specs=[hbm, hbm, vmem, vmem, vmem, vmem, hbm, hbm],
        out_specs=vmem,
        scratch_shapes=[
            pltpu.VMEM((4, 4, 32, 512), BF16),
            pltpu.VMEM((4, 512, 896), BF16),
            pltpu.VMEM((3584, 2048), BF16),
            pltpu.VMEM((1024, 3584), BF16),
            pltpu.VMEM((4, 4, 32, 3584), BF16),
            pltpu.VMEM((2, 4, 32, 896), BF16),
            pltpu.VMEM((2, 4, 32, 896), BF16),
            pltpu.VMEM((2, 4, 32, 1792), BF16),
            pltpu.VMEM((2, 4, 32, 1792), BF16),
            pltpu.VMEM((2, 4, 32, 1792), BF16),
            pltpu.VMEM((2, 32, 896), BF16),
            pltpu.VMEM((2, 32, 896), BF16),
            pltpu.VMEM((2, 32, 1792), BF16),
            pltpu.VMEM((2, 32, 1792), BF16),
            pltpu.VMEM((128, 128), F32),
            pltpu.VMEM((32, 128), F32),
            pltpu.VMEM((3, 8, 32, 128), F32),
            pltpu.VMEM((3, 2, 256, 256), BF16),
            pltpu.VMEM((3, 2, 256, 256), BF16),
            pltpu.VMEM((2, 256, 256), BF16),
            pltpu.VMEM((32, 3584), F32),
            pltpu.VMEM((32, 3584), BF16),
            pltpu.VMEM((8, 32, 3584), BF16),
            pltpu.VMEM(halves, BF16),
            pltpu.VMEM(halves, BF16),
            pltpu.VMEM(halves, BF16),
            pltpu.VMEM((3, 256, 1024), BF16),
            pltpu.VMEM((256, 3584), F32),
            pltpu.VMEM((8, 32, 3584), BF16),
            pltpu.VMEM((8, 32, 3584), BF16),
            dma((4,)),
            dma((24,)),
            dma((24,)),
            dma((3,)),
            dma((3,)),
            dma((3,)),
            dma((3,)),
            dma((6,)),
            dma((6,)),
            dma((6,)),
            dma((6,)),
            dma((3,)),
            dma((3,)),
        ],
        compiler_params=pltpu.CompilerParams(
            collective_id=1, has_side_effects=True, vmem_limit_bytes=67043328
        ),
        name="back",
    )(head_out, out_proj, resid, norm_gain, routes, weights, expert_in, expert_down)


LOWEST = -1e30


def front_kernel(
    scale, off_ref, q_ref, cache_ref, vup_ref, wot_ref,
    ho_ref, wide_ref,
    keys, kc, vt, qt, vupt, bias, scores, acc, top, tot, wo_ref, pair,
    k_s, k_r, w_s, w_r, own_sem,
):
    me = Place()
    here = me.z * 2 + me.c

    def along(axis, n):
        if axis == 0:
            return (here, up(me.x, n) * 4 + me.y)
        return (here, me.x * 4 + up(me.y, n))

    own_copy = pltpu.make_async_copy(cache_ref, keys.at[me.x, me.y], own_sem)
    own_copy.start()

    wo_ref[...] = wot_ref[...].T
    twin = (me.z * 2 + 1 - me.c, me.x * 4 + me.y)
    above = [(up(me.z, n) * 2 + me.c, me.x * 4 + me.y) for n in (1, 3, 2)]
    others = [along(0, 1), along(0, 3), along(1, 1), along(1, 3), twin] + above
    barrier = pltpu.get_barrier_semaphore()
    for other in others:
        pl.semaphore_signal(barrier, inc=1, device_id=other, device_id_type=MESH)
    pl.semaphore_wait(barrier, len(others))

    def send(src, dst, ssem, rsem, device):
        copy = pltpu.make_async_remote_copy(
            src_ref=src, dst_ref=dst, send_sem=ssem, recv_sem=rsem,
            device_id=device, device_id_type=MESH,
        )
        copy.start()
        return copy

    def axis_of(half, phase):
        return half if phase == 0 else 1 - half

    def spot(half, phase, n, lo, rows):
        rows = pl.ds(half * 96 + lo, rows)
        if axis_of(half, phase) == 0:
            a = up(me.x, n)
            return keys.at[a, me.y, rows] if phase == 0 else keys.at[a, :, rows]
        b = up(me.y, n)
        return keys.at[me.x, b, rows] if phase == 0 else keys.at[:, b, rows]

    def sem(half, phase, k):
        return (half * 2 + phase) * 4 + k

    def spread(half, phase):
        axis = axis_of(half, phase)
        for k, n in ((0, 1), (1, 3)):
            at = spot(half, phase, 0, 0, 96)
            src = cache_ref.at[pl.ds(half * 96, 96)] if phase == 0 else at
            i = sem(half, phase, k)
            send(src, at, k_s.at[i], k_r.at[i], along(axis, n))

    def forward(half, phase):
        axis = axis_of(half, phase)
        for k, n, lo in ((0, 3, 0), (1, 1, 48)):
            whole(spot(half, phase, n, 0, 96), k_r.at[sem(half, phase, k)])
            part = spot(half, phase, n, lo, 48)
            i = sem(half, phase, 2 + k)
            send(part, part, k_s.at[i], k_r.at[i], along(axis, 4 - n))

    def far(half, phase):
        for k, lo in ((0, 0), (1, 48)):
            whole(spot(half, phase, 2, lo, 48), k_r.at[sem(half, phase, 2 + k)])

    for half in range(2):
        spread(half, 0)
    send(wo_ref, pair, w_s.at[0], w_r.at[0], twin)

    qt[:, pl.ds(576, 64), :] = jnp.zeros((4, 64, 512), BF16)
    for h in range(2):
        lo = h * 1152
        qt[2 * h, pl.ds(0, 576), :] = q_ref[:, lo : lo + 640].T[:576]
        qt[2 * h + 1, pl.ds(0, 576), :] = q_ref[:, lo + 512 : lo + 1152].T[64:]
    for half in range(2):
        forward(half, 0)
    for h in range(4):
        vupt[h] = vup_ref[h].T
    kc[:, pl.ds(512, 128)] = jnp.zeros((768, 128), BF16)
    top[...] = jnp.full((4, 1, 512), -3e38, F32)
    tot[...] = jnp.zeros((4, 1, 512), F32)
    acc[...] = jnp.zeros((4, 512, 512), F32)
    whole(pair, w_r.at[0])
    first = wo_ref[...]
    second = pair[...]
    low = jnp.where(me.c == 0, first, second)
    high = jnp.where(me.c == 0, second, first)
    wide_ref[me.z] = jnp.concatenate([low, high], axis=1)
    own_copy.wait()
    for half in range(2):
        far(half, 0)
    for half in range(2):
        spread(half, 1)
    rows = pl.ds(pl.multiple_of(me.c * 256, 256), 256)
    for k, to in enumerate(above):
        send(wide_ref.at[me.z, rows], wide_ref.at[me.z, rows], w_s.at[1 + k], w_r.at[1 + k], to)

    row = lax.broadcasted_iota(I32, (768, 1), 0)
    in_first = row < 384
    low_row = jnp.where(in_first, row, row - 384)
    nth = (low_row >= 96).astype(I32) + (low_row >= 192).astype(I32) + (low_row >= 288).astype(I32)
    low_row = low_row - nth * 96
    base = jnp.where(in_first, nth * 768 + low_row, nth * 192 + 96 + low_row)
    query = lax.broadcasted_iota(I32, (768, 512), 1)

    def step(i, carry):
        @pl.when(i == 1)
        def _():
            for half in range(2):
                forward(half, 1)

        @pl.when(i == 3)
        def _():
            for half in range(2):
                far(half, 1)
            for k, n in enumerate((3, 1, 2)):
                z = up(me.z, n)
                got = wide_ref.at[z, rows]
                whole(got, w_r.at[1 + k])
                send(got, got, w_s.at[4 + k], w_r.at[4 + k], twin)

        turn = i + lax.div(i, 2) - 2 * lax.div(i, 3)
        b, a = up(me.y, turn), up(me.x, turn)
        kc[pl.ds(0, 384), pl.ds(0, 576)] = keys[:, b, pl.ds(0, 96), :].reshape(384, 576)
        kc[pl.ds(384, 384), pl.ds(0, 576)] = keys[a, :, pl.ds(96, 96), :].reshape(384, 576)

        def score(u):
            scores[u % 2] = dot(kc[...], qt[u])

        score(0)
        vt[...] = kc[:, pl.ds(0, 512)].T
        start = jnp.where(in_first, b * 192, a * 768)
        bias[...] = jnp.where(base + start - off_ref[0] <= query, 0.0, LOWEST)
        for h in range(4):
            if h < 3:
                score(h + 1)
            s = scores[h % 2] * scale + bias[...]
            old = top[h]
            new = jnp.maximum(old, jnp.max(s, axis=0, keepdims=True))
            p = jnp.exp2(s - new)
            shrink = jnp.exp2(old - new)
            top[h] = new
            tot[h] = tot[h] * shrink + jnp.sum(p, axis=0, keepdims=True)
            acc[h] = acc[h] * shrink + dot(vt[...], p.astype(BF16))
        return carry

    lax.fori_loop(0, 4, step, 0)
    for h in range(4):
        context = (acc[h] / tot[h]).astype(BF16)
        value = dot(vupt[h], context).T.astype(BF16)
        ho_ref[:, :, :, pl.ds(h * 128, 128)] = value.reshape(4, 4, 32, 128)
    rest = pl.ds(pl.multiple_of(256 - me.c * 256, 256), 256)
    for k, n in enumerate((3, 1, 2)):
        z = up(me.z, n)
        whole(wide_ref.at[z, rest], w_r.at[4 + k])
        whole(wide_ref.at[z, rows], w_s.at[4 + k])
        whole(wide_ref.at[me.z, rows], w_s.at[1 + k])
    whole(wo_ref, w_s.at[0])
    for half in range(2):
        for phase in range(2):
            for k in range(2):
                whole(spot(half, phase, 0, 0, 96), k_s.at[sem(half, phase, k)])
                whole(spot(half, phase, 0, 0, 48), k_s.at[sem(half, phase, 2 + k)])


def front(offsets, queries, cache, value_up, out_proj, scale):
    vmem = pl.BlockSpec(memory_space=pltpu.VMEM)
    dma = pltpu.SemaphoreType.DMA
    return pl.pallas_call(
        functools.partial(front_kernel, scale),
        out_shape=(
            jax.ShapeDtypeStruct((4, 4, 32, 512), BF16),
            jax.ShapeDtypeStruct((4, 512, 896), BF16),
        ),
        in_specs=[pl.BlockSpec(memory_space=pltpu.SMEM), vmem, vmem, vmem, vmem],
        out_specs=(vmem, vmem),
        scratch_shapes=[
            pltpu.VMEM((4, 4, 192, 576), BF16),
            pltpu.VMEM((768, 640), BF16),
            pltpu.VMEM((512, 768), BF16),
            pltpu.VMEM((4, 640, 512), BF16),
            pltpu.VMEM((4, 128, 512), BF16),
            pltpu.VMEM((768, 512), F32),
            pltpu.VMEM((2, 768, 512), F32),
            pltpu.VMEM((4, 512, 512), F32),
            pltpu.VMEM((4, 1, 512), F32),
            pltpu.VMEM((4, 1, 512), F32),
            pltpu.VMEM((512, 448), BF16),
            pltpu.VMEM((512, 448), BF16),
            dma((16,)),
            dma((16,)),
            dma((7,)),
            dma((7,)),
            dma(()),
        ],
        compiler_params=pltpu.CompilerParams(
            collective_id=2, has_side_effects=True, vmem_limit_bytes=60 * 1024 * 1024
        ),
        name="front",
    )(offsets, queries, cache, value_up, out_proj)


def shards(
    queries,
    cache,
    offsets,
    value_up,
    out_proj,
    resid,
    norm_gain,
    routes,
    route_weights,
    expert_in,
    expert_down,
):
    latent_width = value_up.shape[1]
    key_width = cache.shape[2]
    score_scale = (value_up.shape[2] + key_width - latent_width) ** (-0.5)
    head_out, wide = front(
        offsets, queries, cache[0], value_up, out_proj.T, score_scale * LOG2_E
    )
    return back(
        head_out, wide, resid, norm_gain, routes.T, route_weights.T, expert_in[0], expert_down[0]
    )


def solution(mesh):
    return jax.shard_map(
        shards,
        mesh=mesh,
        in_specs=(
            P("dp", "tensor"),
            P("dp", "tensor", None),
            P("dp"),
            P("tensor", None, None),
            P("tensor", "dp"),
            P(("dp", "tensor"), None),
            P(),
            P(("dp", "tensor"), None),
            P(("dp", "tensor"), None),
            P(("dp", "tensor"), None, None),
            P(("dp", "tensor"), None, None),
        ),
        out_specs=P(("dp", "tensor"), None),
        check_vma=False,
    )
```

```python
import functools

import jax
import jax.numpy as jnp
from jax import lax
from jax.experimental import pallas as pl
from jax.experimental.pallas import tpu as pltpu
from jax.sharding import PartitionSpec as P

MESH = pl.DeviceIdType.MESH
LOG2_E = 1.4426950408889634
BF16, F32, I32 = jnp.bfloat16, jnp.float32, jnp.int32
NEAR = (
    (1, 0), (0, 1), (3, 0), (0, 3), (1, 1), (3, 3), (1, 3), (3, 1),
    (2, 0), (0, 2), (2, 2), (2, 1), (1, 2), (2, 3), (3, 2),
)
PARTS = ((0, 0, 1280), (1, 1280, 1152), (2, 2432, 1152))


def whole(ref, sem):
    pltpu.make_async_copy(ref, ref, sem).wait()


def dot(a, b):
    return jnp.dot(a, b, preferred_element_type=F32)


class Place:
    def __init__(self):
        dp, t = lax.axis_index("dp"), lax.axis_index("tensor")
        self.z, self.c = lax.div(dp, 2), lax.rem(dp, 2)
        self.x, self.y = lax.div(t, 4), lax.rem(t, 4)

    def line(self, part, a, core):
        if part == 0:
            return (a * 2 + core, self.x * 4 + self.y)
        if part == 1:
            return (self.z * 2 + core, a * 4 + self.y)
        return (self.z * 2 + core, self.x * 4 + a)

    def own_line(self, part):
        return (self.z, self.x, self.y)[part]

    def plane(self, part, b1, b2):
        if part == 0:
            return (self.z * 2 + self.c, b1 * 4 + b2)
        if part == 1:
            return (b1 * 2 + self.c, self.x * 4 + b2)
        return (b2 * 2 + self.c, b1 * 4 + self.y)

    def own_plane(self, part):
        return ((self.x, self.y), (self.z, self.y), (self.x, self.z))[part]

    def expert(self, part, j):
        b1, b2 = j // 4, j % 4
        if part == 0:
            return (self.z * 2 + self.c) * 16 + j
        if part == 1:
            return (b1 * 2 + self.c) * 16 + self.x * 4 + b2
        return (b2 * 2 + self.c) * 16 + b1 * 4 + self.y


def up(v, n):
    return lax.rem(v + n, 4)


def partners(me):
    out = [(me.z * 2 + 1 - me.c, me.x * 4 + me.y)]
    for part in range(3):
        for n in (1, 2, 3):
            out.append(me.line(part, up(me.own_line(part), n), 1 - me.c))
    for dz in range(4):
        for dx in range(4):
            for dy in range(4):
                if (dz, dx, dy) != (0, 0, 0) and 0 in (dz, dx, dy):
                    out.append((up(me.z, dz) * 2 + me.c, up(me.x, dx) * 4 + up(me.y, dy)))
    return out


def back_kernel(
    stream_ref, gain_ref, routes_ref, weights_ref, win_hbm, wdown_hbm,
    out_ref,
    win, wdown, part4, turned, table_ref, metas, pick, wgt, swap,
    nrm, toks, outg, rows, stage, hid, half_sum, psum, recv,
    wsem, m_s, m_r, g_s, g_r, d_s, d_r, t_s, t_r, c_s, c_r,
):
    me = Place()
    barrier = pltpu.get_barrier_semaphore()
    others = partners(me)
    for other in others:
        pl.semaphore_signal(barrier, inc=1, device_id=other, device_id_type=MESH)
    loads = [
        pltpu.make_async_copy(win_hbm, win, wsem.at[0]),
        pltpu.make_async_copy(wdown_hbm, wdown, wsem.at[1]),
    ]
    for load in loads:
        load.start()
    turned[...] = jnp.zeros((128, 128), F32)
    turned[pl.ds(0, 8), pl.ds(0, 32)] = routes_ref[...].astype(F32)
    turned[pl.ds(8, 8), pl.ds(0, 32)] = weights_ref[...]
    table_ref[...] = turned[...].T[:32]
    value = stream_ref[...]
    mean_square = jnp.mean(value * value, axis=1, keepdims=True)
    nrm[...] = (value * lax.rsqrt(mean_square + 1e-06) * gain_ref[...].reshape(1, 3584)).astype(BF16)
    pl.semaphore_wait(barrier, len(others))

    def send(src, dst, ssem, rsem, device):
        copy = pltpu.make_async_remote_copy(
            src_ref=src, dst_ref=dst, send_sem=ssem, recv_sem=rsem,
            device_id=device, device_id_type=MESH,
        )
        copy.start()
        return copy

    meta_sends = []
    for part in range(3):
        own = me.own_line(part) * 2 + me.c
        for n in range(4):
            for core in range(2):
                if (n, core) == (0, 0):
                    continue
                to = me.line(part, up(me.own_line(part), n), lax.rem(me.c + core, 2))
                meta_sends.append(send(table_ref, metas.at[part, own], m_s.at[part], m_r.at[part], to))
        pltpu.make_async_copy(table_ref, metas.at[part, own], m_r.at[part]).start()

    LINE = ((0, 1), (1, 0), (3, 0), (1, 1), (3, 1), (2, 0), (2, 1))
    for part, lo, n in PARTS:
        cols = pl.ds(lo, n)
        own = me.own_line(part) * 2 + me.c
        for step, core in LINE:
            to = me.line(part, up(me.own_line(part), step), lax.rem(me.c + core, 2))
            send(nrm.at[:, cols], toks.at[own, :, cols], g_s.at[part], g_r.at[part], to)
        pltpu.make_async_copy(nrm.at[:, cols], toks.at[own, :, cols], g_r.at[part]).start()

    token = lax.broadcasted_iota(I32, (256, 256), 0)
    other = lax.broadcasted_iota(I32, (256, 256), 1)
    earlier = jnp.where((token // 32 == other // 32) & (other < token), 1.0, 0.0).astype(BF16)
    lane = lax.broadcasted_iota(I32, (128, 256), 1)
    spread = jnp.where(lane // 16 == lax.broadcasted_iota(I32, (128, 256), 0), 1.0, 0.0).astype(BF16)
    of_source = other % 16 // 2 == token // 32
    rank_wanted = (other % 2).astype(F32)
    for part in range(3):
        whole(metas.at[part], m_r.at[part])
        table = metas[part].reshape(256, 128)
        column = lax.broadcasted_iota(I32, (256, 128), 1)
        wanted = jnp.where(column < 16, me.expert(part, column), -1).astype(F32)
        hit = jnp.zeros((256, 128), F32)
        weight = jnp.zeros((256, 128), F32)
        for k in range(8):
            same = table[:, k : k + 1] == wanted
            hit = jnp.where(same, 1.0, hit)
            weight = jnp.where(same, table[:, 8 + k : 9 + k], weight)
        rank = dot(earlier, hit.astype(BF16))
        rank = jnp.where(hit > 0.5, rank, -1.0)
        rank = jnp.where(of_source, dot(rank.astype(BF16), spread) - rank_wanted, -1.0)
        weight = dot(weight.astype(BF16), spread)
        for half in range(2):
            chosen = rank == half * 2.0
            pick[part, half] = jnp.where(chosen, 1.0, 0.0).T.astype(BF16)
            wgt[part, half] = jnp.where(chosen, weight, 0.0).astype(BF16)
    rx, ry, rz, low = token // 64, token // 16 % 4, token // 4 % 4, token % 4
    swap[0] = jnp.where(other == rz * 64 + ry * 16 + rx * 4 + low, 1.0, 0.0).astype(BF16)
    swap[1] = jnp.where(other == rx * 64 + rz * 16 + ry * 4 + low, 1.0, 0.0).astype(BF16)

    def half_of(ref, half):
        if ref is part4:
            return lambda b1, b2, cols: part4.at[b1, b2, pl.ds(half * 16, 16), cols]
        return lambda b1, b2, cols: ref.at[half, b1, b2, :, cols]

    def exchange(half, src, dst_of, ssem, rsem, parts):
        for d1, d2 in NEAR:
            for part, lo, n in parts:
                b1, b2 = me.own_plane(part)
                e1, e2 = up(b1, d1), up(b2, d2)
                at, cols = half * 3 + part, pl.ds(lo, n)
                send(
                    half_of(src, half)(e1, e2, cols), half_of(dst_of(part), half)(b1, b2, cols),
                    ssem.at[at], rsem.at[at], me.plane(part, e1, e2),
                )
        for part, lo, n in parts:
            b1, b2 = me.own_plane(part)
            at, cols = half * 3 + part, pl.ds(lo, n)
            pltpu.make_async_copy(
                half_of(src, half)(b1, b2, cols), half_of(dst_of(part), half)(b1, b2, cols), rsem.at[at]
            ).start()

    def landing(part):
        return rows if part == 0 else stage

    def sent(half, lo, n, sem):
        for k in range(3):
            whole(outg.at[half, k, :, :, pl.ds(lo, n)], sem)
        whole(outg.at[half, 3, pl.ds(0, 3), :, pl.ds(lo, n)], sem)

    def dispatch(half):
        for part, lo, n in PARTS:
            cols = pl.ds(lo, n)
            if half == 0:
                whole(toks.at[:, :, cols], g_r.at[part])
            value = dot(pick[part, half], toks[:, :, cols].reshape(256, n))
            outg[half, :, :, :, cols] = value.astype(BF16).reshape(4, 4, 16, n)
        exchange(half, outg, landing, d_s, d_r, PARTS)

    def expert(half):
        for part, lo, n in PARTS:
            cols = pl.ds(lo, n)
            whole(landing(part).at[half, :, :, :, cols], d_r.at[half * 3 + part])
            if part:
                value = dot(swap[part - 1], stage[half, :, :, :, cols].reshape(256, n))
                rows[half, :, :, :, cols] = value.astype(BF16).reshape(4, 4, 16, n)
        if half == 0:
            loads[0].wait()
            loads[1].wait()

        def hidden(j, carry):
            cols = pl.ds(pl.multiple_of(j * 256, 256), 256)
            more = pl.ds(pl.multiple_of(j * 256 + 1024, 256), 256)
            here = rows[half].reshape(256, 3584)
            gate = dot(here, win[:, cols])
            lift = dot(here, win[:, more])
            hid[0, :, cols] = (gate / (1.0 + jnp.exp(-gate)) * lift).astype(BF16)
            return carry

        lax.fori_loop(0, 4, hidden, 0)
        for part, lo, n in PARTS:
            if part:
                hid[part] = dot(swap[part - 1], hid[0]).astype(BF16)
            sent(half, lo, n, d_s.at[half * 3 + part])
            value = dot(hid[part], wdown[:, pl.ds(lo, n)])
            outg[half, :, :, :, pl.ds(lo, n)] = value.astype(BF16).reshape(4, 4, 16, n)
            if half:
                exchange(half, outg, lambda part: part4, t_s, t_r, ((part, lo, n),))
        if half == 0:
            exchange(half, outg, lambda part: part4, t_s, t_r, PARTS)

    dispatch(0)
    dispatch(1)
    expert(0)
    expert(1)

    for half in range(2):
        for part, lo, n in PARTS:
            cols = pl.ds(lo, n)
            back_rows = part4.at[:, :, pl.ds(half * 16, 16), cols]
            whole(back_rows, t_r.at[half * 3 + part])
            value = dot(wgt[part, half], back_rows[...].reshape(256, n))
            if half == 0:
                half_sum[:, cols] = value
                continue
            psum[:, :, cols] = (half_sum[:, cols] + value).astype(BF16).reshape(8, 32, n)
            own = me.own_line(part) * 2 + me.c
            for step, core in LINE:
                a, k = up(me.own_line(part), step), lax.rem(me.c + core, 2)
                send(
                    psum.at[a * 2 + k, :, cols], recv.at[own, :, cols],
                    c_s.at[part], c_r.at[part], me.line(part, a, k),
                )
            pltpu.make_async_copy(psum.at[own, :, cols], recv.at[own, :, cols], c_r.at[part]).start()
    for part, lo, n in PARTS:
        cols = pl.ds(lo, n)
        whole(recv.at[:, :, cols], c_r.at[part])
        total = stream_ref[:, cols]
        for q in range(8):
            total += recv[q, :, cols].astype(F32)
        out_ref[:, cols] = total.astype(BF16)
    for part, lo, n in PARTS:
        for half in range(2):
            sent(half, lo, n, t_s.at[half * 3 + part])
        whole(toks.at[pl.ds(0, 7), :, pl.ds(lo, n)], g_s.at[part])
        whole(psum.at[pl.ds(0, 7), :, pl.ds(lo, n)], c_s.at[part])
        whole(metas.at[part, pl.ds(0, 7)], m_s.at[part])


def back(stream, norm_gain, routes, weights, expert_in, expert_down):
    vmem = pl.BlockSpec(memory_space=pltpu.VMEM)
    hbm = pl.BlockSpec(memory_space=pl.ANY)
    dma = pltpu.SemaphoreType.DMA
    halves = (2, 4, 4, 16, 3584)
    return pl.pallas_call(
        back_kernel,
        out_shape=jax.ShapeDtypeStruct((32, 3584), BF16),
        in_specs=[vmem, vmem, vmem, vmem, hbm, hbm],
        out_specs=vmem,
        scratch_shapes=[
            pltpu.VMEM((3584, 2048), BF16),
            pltpu.VMEM((1024, 3584), BF16),
            pltpu.VMEM((4, 4, 32, 3584), BF16),
            pltpu.VMEM((128, 128), F32),
            pltpu.VMEM((32, 128), F32),
            pltpu.VMEM((3, 8, 32, 128), F32),
            pltpu.VMEM((3, 2, 256, 256), BF16),
            pltpu.VMEM((3, 2, 256, 256), BF16),
            pltpu.VMEM((2, 256, 256), BF16),
            pltpu.VMEM((32, 3584), BF16),
            pltpu.VMEM((8, 32, 3584), BF16),
            pltpu.VMEM(halves, BF16),
            pltpu.VMEM(halves, BF16),
            pltpu.VMEM(halves, BF16),
            pltpu.VMEM((3, 256, 1024), BF16),
            pltpu.VMEM((256, 3584), F32),
            pltpu.VMEM((8, 32, 3584), BF16),
            pltpu.VMEM((8, 32, 3584), BF16),
            dma((2,)),
            dma((3,)),
            dma((3,)),
            dma((3,)),
            dma((3,)),
            dma((6,)),
            dma((6,)),
            dma((6,)),
            dma((6,)),
            dma((3,)),
            dma((3,)),
        ],
        compiler_params=pltpu.CompilerParams(
            collective_id=1, has_side_effects=True, vmem_limit_bytes=67043328
        ),
        name="back",
    )(stream, norm_gain, routes, weights, expert_in, expert_down)


LOWEST = -1e30


def front_kernel(
    scale, off_ref, q_ref, cache_ref, vup_ref, wot_ref, resid_ref,
    stream_ref,
    keys, kc, vt, qt, vupt, bias, scores, probs, acc, top, tot, slabs, wide, ho,
    part4, r1, l1, r2, l2, mid, r1b, l1b, r2b, l2b,
    k_s, k_r, w_s, w_r, own_sem, rs_s, rs_r,
):
    me = Place()
    here = me.z * 2 + me.c

    def along(axis, n):
        if axis == 0:
            return (here, up(me.x, n) * 4 + me.y)
        return (here, me.x * 4 + up(me.y, n))

    own_copy = pltpu.make_async_copy(cache_ref, keys.at[me.x, me.y], own_sem)
    own_copy.start()

    slabs[me.z, me.c] = wot_ref[...].T
    twin = (me.z * 2 + 1 - me.c, me.x * 4 + me.y)
    above = [(up(me.z, n) * 2 + me.c, me.x * 4 + me.y) for n in (1, 3, 2)]
    others = [along(0, 1), along(0, 3), along(1, 1), along(1, 3), twin] + above
    barrier = pltpu.get_barrier_semaphore()
    for other in others:
        pl.semaphore_signal(barrier, inc=1, device_id=other, device_id_type=MESH)
    pl.semaphore_wait(barrier, len(others))

    def send(src, dst, ssem, rsem, device):
        copy = pltpu.make_async_remote_copy(
            src_ref=src, dst_ref=dst, send_sem=ssem, recv_sem=rsem,
            device_id=device, device_id_type=MESH,
        )
        copy.start()
        return copy

    def axis_of(half, phase):
        return half if phase == 0 else 1 - half

    def spot(half, phase, n, lo, rows):
        rows = pl.ds(half * 96 + lo, rows)
        if axis_of(half, phase) == 0:
            a = up(me.x, n)
            return keys.at[a, me.y, rows] if phase == 0 else keys.at[a, :, rows]
        b = up(me.y, n)
        return keys.at[me.x, b, rows] if phase == 0 else keys.at[:, b, rows]

    def sem(half, phase, k):
        return (half * 2 + phase) * 4 + k

    def spread(half, phase):
        axis = axis_of(half, phase)
        for k, n in ((0, 1), (1, 3)):
            at = spot(half, phase, 0, 0, 96)
            src = cache_ref.at[pl.ds(half * 96, 96)] if phase == 0 else at
            i = sem(half, phase, k)
            send(src, at, k_s.at[i], k_r.at[i], along(axis, n))

    def forward(half, phase):
        axis = axis_of(half, phase)
        for k, n, lo in ((0, 3, 0), (1, 1, 48)):
            whole(spot(half, phase, n, 0, 96), k_r.at[sem(half, phase, k)])
            part = spot(half, phase, n, lo, 48)
            i = sem(half, phase, 2 + k)
            send(part, part, k_s.at[i], k_r.at[i], along(axis, 4 - n))

    def far(half, phase):
        for k, lo in ((0, 0), (1, 48)):
            whole(spot(half, phase, 2, lo, 48), k_r.at[sem(half, phase, 2 + k)])

    for half in range(2):
        spread(half, 0)
    mine = slabs.at[me.z, me.c]
    send(mine, mine, w_s.at[0], w_r.at[0], twin)
    for k, to in enumerate(above):
        send(mine, mine, w_s.at[1 + k], w_r.at[1 + k], to)

    qt[:, :, pl.ds(576, 64), :] = jnp.zeros((2, 2, 64, 512), BF16)
    for tile in range(2):
        for h in range(4):
            lo = h * 576 - h % 2 * 64
            some = q_ref[:, pl.ds(tile * 16, 16), lo : lo + 640].reshape(256, 640).T
            lanes = pl.ds(h % 2 * 256, 256)
            qt[tile, h // 2, pl.ds(0, 576), lanes] = some[64:] if h % 2 else some[:576]
    for half in range(2):
        forward(half, 0)
    for h in range(4):
        vupt[h] = vup_ref[h].T
    kc[:, :, pl.ds(512, 128)] = jnp.zeros((4, 768, 128), BF16)
    top[...] = jnp.full((2, 2, 1, 512), -3e38, F32)
    tot[...] = jnp.zeros((2, 2, 1, 512), F32)
    acc[...] = jnp.zeros((2, 2, 512, 512), F32)
    own_copy.wait()
    for half in range(2):
        far(half, 0)
    for half in range(2):
        spread(half, 1)

    row = lax.broadcasted_iota(I32, (768, 1), 0)
    in_first = row < 384
    low_row = jnp.where(in_first, row, row - 384)
    nth = (low_row >= 96).astype(I32) + (low_row >= 192).astype(I32) + (low_row >= 288).astype(I32)
    low_row = low_row - nth * 96
    base = jnp.where(in_first, nth * 768 + low_row, nth * 192 + 96 + low_row)
    lane = lax.broadcasted_iota(I32, (768, 256), 1)
    query = lane // 16 * 32 + lane % 16

    def turn_of(chunk):
        return chunk + lax.div(chunk, 2) - 2 * lax.div(chunk, 3)

    def build(chunk):
        turn = (0, 1, 3, 2)[chunk]
        b, a = up(me.y, turn), up(me.x, turn)
        kc[chunk, pl.ds(0, 384), pl.ds(0, 576)] = keys[:, b, pl.ds(0, 96), :].reshape(384, 576)
        kc[chunk, pl.ds(384, 384), pl.ds(0, 576)] = keys[a, :, pl.ds(96, 96), :].reshape(384, 576)
        vt[chunk] = kc[chunk, :, pl.ds(0, 512)].T

    def finish(tile):
        for g in range(2):
            context = (acc[tile, g] / tot[tile, g]).astype(BF16)
            for k in range(2):
                value = dot(vupt[2 * g + k], context[:, k * 256 : k * 256 + 256]).T.astype(BF16)
                ho[tile, :, :, :, pl.ds((2 * g + k) * 128, 128)] = value.reshape(4, 4, 16, 128)
        for h in range(2):
            for b in range(2):
                value = dot(ho[tile].reshape(256, 512), wide[2 * h + b])
                cols = pl.ds(h * 1792 + b * 896, 896)
                part4[tile, :, :, :, cols] = value.astype(BF16).reshape(4, 4, 16, 896)

    def position(h, phase):
        return me.x if h == phase else me.y

    def piece(tile, h, phase, k, lo, n):
        if phase:
            return mid.at[tile, h, k, :, pl.ds(lo, n)]
        cols = pl.ds(h * 1792 + lo, n)
        return part4.at[tile, :, k, :, cols] if h else part4.at[tile, k, :, :, cols]

    def box(i, tile, h, phase, lo, n):
        ref = (r1b, l1b, r2b, l2b)[i] if phase else (r1, l1, r2, l2)[i]
        if phase:
            return ref.at[tile, h, :, pl.ds(lo, n)]
        return ref.at[tile, h, :, :, pl.ds(lo, n)]

    def rs_sem(tile, h, phase, k):
        return ((tile * 2 + h) * 2 + phase) * 6 + k

    def give(tile, h, phase, k, src, dst, n):
        i = rs_sem(tile, h, phase, k)
        send(src, dst, rs_s.at[i], rs_r.at[i], along(0 if h == phase else 1, n))

    def first(tile, phase):
        for h in range(2):
            for side, (lo, n) in enumerate(((0, 1), (896, 3))):
                src = piece(tile, h, phase, up(position(h, phase), 2), lo, 896)
                give(tile, h, phase, side, src, box(side, tile, h, phase, 0, 896), n)
        for h in range(2):
            for side, (lo, n) in enumerate(((896, 1), (0, 3))):
                src = piece(tile, h, phase, up(position(h, phase), n), lo, 896)
                give(tile, h, phase, 2 + side, src, box(2 + side, tile, h, phase, lo, 896), n)

    def second(tile, phase):
        for h in range(2):
            for side, (lo, n) in enumerate(((0, 1), (896, 3))):
                came = box(side, tile, h, phase, 0, 896)
                whole(came, rs_r.at[rs_sem(tile, h, phase, side)])
                own = piece(tile, h, phase, up(position(h, phase), n), lo, 896)
                own[...] = (own[...].astype(F32) + came[...].astype(F32)).astype(BF16)
                give(tile, h, phase, 4 + side, own, box(2 + side, tile, h, phase, lo, 896), n)

    def last(tile, h, phase):
        for k, (side, lo) in enumerate(((2, 896), (3, 0), (2, 0), (3, 896))):
            whole(box(side, tile, h, phase, lo, 896), rs_r.at[rs_sem(tile, h, phase, 2 + k)])
        total = piece(tile, h, phase, position(h, phase), 0, 1792)[...].astype(F32)
        total += box(2, tile, h, phase, 0, 1792)[...].astype(F32)
        return total + box(3, tile, h, phase, 0, 1792)[...].astype(F32)

    def middle(tile):
        for h in range(2):
            mid[tile, h] = last(tile, h, 0).astype(BF16)
        first(tile, 1)

    def settle(tile):
        rows, cols = pl.ds(tile * 16, 16), (pl.ds(0, 1792), pl.ds(1792, 1792))
        for h in range(2):
            stream_ref[rows, cols[h]] = last(tile, h, 1) + resid_ref[rows, cols[h]].astype(F32)

    build(0)

    def step(i, carry):
        @pl.when(i == 1)
        def _():
            for half in range(2):
                forward(half, 1)
            build(1)
            build(2)

        @pl.when(i == 2)
        def _():
            for half in range(2):
                far(half, 1)
            build(3)
            for k, n in enumerate((3, 1, 2)):
                got = slabs.at[up(me.z, n), me.c]
                whole(got, w_r.at[1 + k])
                send(got, got, w_s.at[4 + k], w_r.at[4 + k], twin)

        @pl.when(i == 3)
        def _():
            whole(slabs.at[me.z, 1 - me.c], w_r.at[0])
            for k, n in enumerate((3, 1, 2)):
                whole(slabs.at[up(me.z, n), 1 - me.c], w_r.at[4 + k])
            for z in range(4):
                wide[z] = jnp.concatenate([slabs[z, 0], slabs[z, 1]], axis=1)
            finish(0)
            first(0, 0)

        tiles = (lax.div(i, 3), jnp.where(i == 1, 0, 1))
        chunks = (turn_of(i), jnp.where(i == 1, 2, jnp.where(i == 2, 1, i)))

        def score(u):
            scores[u % 2] = dot(kc[chunks[u // 2]], qt[tiles[u // 2], u % 2])

        score(0)
        for u in range(4):
            tile, g = tiles[u // 2], u % 2
            if u < 3:
                score(u + 1)
            if g == 0:
                turn = turn_of(chunks[u // 2])
                start = jnp.where(in_first, up(me.y, turn) * 192, up(me.x, turn) * 768)
                limit = query + (tile * 16 + off_ref[0])
                bias[...] = jnp.where(base + start <= limit, 0.0, LOWEST)
            for k in range(2):
                lanes = pl.ds(k * 256, 256)
                s = scores[g, :, lanes] * scale + bias[...]
                old = top[tile, g, :, lanes]
                new = jnp.maximum(old, jnp.max(s, axis=0, keepdims=True))
                p = jnp.exp2(s - new)
                shrink = jnp.exp2(old - new)
                top[tile, g, :, lanes] = new
                tot[tile, g, :, lanes] = tot[tile, g, :, lanes] * shrink + jnp.sum(p, axis=0, keepdims=True)
                acc[tile, g, :, lanes] = acc[tile, g, :, lanes] * shrink
                probs[g, :, lanes] = p.astype(BF16)
            acc[tile, g] += dot(vt[chunks[u // 2]], probs[g])
            if u == 1:

                @pl.when(i == 3)
                def _():
                    second(0, 0)

        return carry

    lax.fori_loop(0, 4, step, 0)
    middle(0)
    finish(1)
    first(1, 0)
    second(0, 1)
    second(1, 0)
    settle(0)
    middle(1)
    second(1, 1)
    settle(1)
    for k, n in enumerate((3, 1, 2)):
        whole(mine, w_s.at[1 + k])
        whole(slabs.at[up(me.z, n), me.c], w_s.at[4 + k])
    whole(mine, w_s.at[0])
    for half in range(2):
        for phase in range(2):
            for k in range(2):
                whole(spot(half, phase, 0, 0, 96), k_s.at[sem(half, phase, k)])
                whole(spot(half, phase, 0, 0, 48), k_s.at[sem(half, phase, 2 + k)])
    for tile in range(2):
        for h in range(2):
            for phase in range(2):
                for k in range(6):
                    src = piece(tile, h, phase, 0, 0, 896)
                    whole(src, rs_s.at[rs_sem(tile, h, phase, k)])


def front(offsets, queries, cache, value_up, out_proj, resid, scale):
    vmem = pl.BlockSpec(memory_space=pltpu.VMEM)
    dma = pltpu.SemaphoreType.DMA
    return pl.pallas_call(
        functools.partial(front_kernel, scale),
        out_shape=jax.ShapeDtypeStruct((32, 3584), F32),
        in_specs=[pl.BlockSpec(memory_space=pltpu.SMEM), vmem, vmem, vmem, vmem, vmem],
        out_specs=vmem,
        scratch_shapes=[
            pltpu.VMEM((4, 4, 192, 576), BF16),
            pltpu.VMEM((4, 768, 640), BF16),
            pltpu.VMEM((4, 512, 768), BF16),
            pltpu.VMEM((2, 2, 640, 512), BF16),
            pltpu.VMEM((4, 128, 512), BF16),
            pltpu.VMEM((768, 256), F32),
            pltpu.VMEM((2, 768, 512), F32),
            pltpu.VMEM((2, 768, 512), BF16),
            pltpu.VMEM((2, 2, 512, 512), F32),
            pltpu.VMEM((2, 2, 1, 512), F32),
            pltpu.VMEM((2, 2, 1, 512), F32),
            pltpu.VMEM((4, 2, 512, 448), BF16),
            pltpu.VMEM((4, 512, 896), BF16),
            pltpu.VMEM((2, 4, 4, 16, 512), BF16),
            pltpu.VMEM((2, 4, 4, 16, 3584), BF16),
            pltpu.VMEM((2, 2, 4, 16, 896), BF16),
            pltpu.VMEM((2, 2, 4, 16, 896), BF16),
            pltpu.VMEM((2, 2, 4, 16, 1792), BF16),
            pltpu.VMEM((2, 2, 4, 16, 1792), BF16),
            pltpu.VMEM((2, 2, 4, 16, 1792), BF16),
            pltpu.VMEM((2, 2, 16, 896), BF16),
            pltpu.VMEM((2, 2, 16, 896), BF16),
            pltpu.VMEM((2, 2, 16, 1792), BF16),
            pltpu.VMEM((2, 2, 16, 1792), BF16),
            dma((16,)),
            dma((16,)),
            dma((7,)),
            dma((7,)),
            dma(()),
            dma((48,)),
            dma((48,)),
        ],
        compiler_params=pltpu.CompilerParams(
            collective_id=2, has_side_effects=True, vmem_limit_bytes=67043328
        ),
        name="front",
    )(offsets, queries, cache, value_up, out_proj, resid)


def shards(
    queries,
    cache,
    offsets,
    value_up,
    out_proj,
    resid,
    norm_gain,
    routes,
    route_weights,
    expert_in,
    expert_down,
):
    latent_width = value_up.shape[1]
    key_width = cache.shape[2]
    score_scale = (value_up.shape[2] + key_width - latent_width) ** (-0.5)
    stream = front(
        offsets, queries.reshape(16, 32, -1), cache[0], value_up, out_proj.T, resid,
        score_scale * LOG2_E,
    )
    return back(stream, norm_gain, routes.T, route_weights.T, expert_in[0], expert_down[0])


def solution(mesh):
    return jax.shard_map(
        shards,
        mesh=mesh,
        in_specs=(
            P("dp", "tensor"),
            P("dp", "tensor", None),
            P("dp"),
            P("tensor", None, None),
            P("tensor", "dp"),
            P(("dp", "tensor"), None),
            P(),
            P(("dp", "tensor"), None),
            P(("dp", "tensor"), None),
            P(("dp", "tensor"), None, None),
            P(("dp", "tensor"), None, None),
        ),
        out_specs=P(("dp", "tensor"), None),
        check_vma=False,
    )
```

```python
import functools

import jax
import jax.numpy as jnp
from jax import lax
from jax.experimental import pallas as pl
from jax.experimental.pallas import tpu as pltpu
from jax.sharding import PartitionSpec as P

MESH = pl.DeviceIdType.MESH
LOG2_E = 1.4426950408889634
BF16, F32, I32 = jnp.bfloat16, jnp.float32, jnp.int32
NEAR = (
    (1, 0), (0, 1), (3, 0), (0, 3), (1, 1), (3, 3), (1, 3), (3, 1),
    (2, 0), (0, 2), (2, 2), (2, 1), (1, 2), (2, 3), (3, 2),
)
PARTS = ((0, 0, 1280), (1, 1280, 1152), (2, 2432, 1152))


def whole(ref, sem):
    pltpu.make_async_copy(ref, ref, sem).wait()


def dot(a, b):
    return jnp.dot(a, b, preferred_element_type=F32)


class Place:
    def __init__(self):
        dp, t = lax.axis_index("dp"), lax.axis_index("tensor")
        self.z, self.c = lax.div(dp, 2), lax.rem(dp, 2)
        self.x, self.y = lax.div(t, 4), lax.rem(t, 4)

    def line(self, part, a, core):
        if part == 0:
            return (a * 2 + core, self.x * 4 + self.y)
        if part == 1:
            return (self.z * 2 + core, a * 4 + self.y)
        return (self.z * 2 + core, self.x * 4 + a)

    def own_line(self, part):
        return (self.z, self.x, self.y)[part]

    def plane(self, part, b1, b2):
        if part == 0:
            return (self.z * 2 + self.c, b1 * 4 + b2)
        if part == 1:
            return (b1 * 2 + self.c, self.x * 4 + b2)
        return (b2 * 2 + self.c, b1 * 4 + self.y)

    def own_plane(self, part):
        return ((self.x, self.y), (self.z, self.y), (self.x, self.z))[part]

    def expert(self, part, j):
        b1, b2 = j // 4, j % 4
        if part == 0:
            return (self.z * 2 + self.c) * 16 + j
        if part == 1:
            return (b1 * 2 + self.c) * 16 + self.x * 4 + b2
        return (b2 * 2 + self.c) * 16 + b1 * 4 + self.y


def up(v, n):
    return lax.rem(v + n, 4)


def partners(me):
    out = [(me.z * 2 + 1 - me.c, me.x * 4 + me.y)]
    for part in range(3):
        for n in (1, 2, 3):
            out.append(me.line(part, up(me.own_line(part), n), 1 - me.c))
    for dz in range(4):
        for dx in range(4):
            for dy in range(4):
                if (dz, dx, dy) != (0, 0, 0) and 0 in (dz, dx, dy):
                    out.append((up(me.z, dz) * 2 + me.c, up(me.x, dx) * 4 + up(me.y, dy)))
    return out


def back_kernel(
    stream_ref, gain_ref, routes_ref, weights_ref, win_hbm, wdown_hbm,
    out_ref,
    win, wdown, part4, turned, table_ref, metas, pick, wgt, swap,
    nrm, toks, outg, rows, stage, hid, half_sum, psum, other_core, recv,
    wsem, m_s, m_r, g_s, g_r, d_s, d_r, t_s, t_r, x_s, x_r, c_s, c_r,
):
    me = Place()
    barrier = pltpu.get_barrier_semaphore()
    others = partners(me)
    for other in others:
        pl.semaphore_signal(barrier, inc=1, device_id=other, device_id_type=MESH)
    loads = [
        pltpu.make_async_copy(win_hbm, win, wsem.at[0]),
        pltpu.make_async_copy(wdown_hbm, wdown, wsem.at[1]),
    ]
    for load in loads:
        load.start()
    turned[...] = jnp.zeros((128, 128), F32)
    turned[pl.ds(0, 8), pl.ds(0, 32)] = routes_ref[...].astype(F32)
    turned[pl.ds(8, 8), pl.ds(0, 32)] = weights_ref[...]
    table_ref[...] = turned[...].T[:32]
    value = stream_ref[...]
    mean_square = jnp.mean(value * value, axis=1, keepdims=True)
    nrm[...] = (value * lax.rsqrt(mean_square + 1e-06) * gain_ref[...].reshape(1, 3584)).astype(BF16)
    pl.semaphore_wait(barrier, len(others))

    def send(src, dst, ssem, rsem, device):
        copy = pltpu.make_async_remote_copy(
            src_ref=src, dst_ref=dst, send_sem=ssem, recv_sem=rsem,
            device_id=device, device_id_type=MESH,
        )
        copy.start()
        return copy

    meta_sends = []
    for part in range(3):
        own = me.own_line(part) * 2 + me.c
        for n in range(4):
            for core in range(2):
                if (n, core) == (0, 0):
                    continue
                to = me.line(part, up(me.own_line(part), n), lax.rem(me.c + core, 2))
                meta_sends.append(send(table_ref, metas.at[part, own], m_s.at[part], m_r.at[part], to))
        pltpu.make_async_copy(table_ref, metas.at[part, own], m_r.at[part]).start()

    def to_line(part, n):
        return me.line(part, up(me.own_line(part), n), me.c)

    twin = (me.z * 2 + 1 - me.c, me.x * 4 + me.y)
    for part, lo, n in PARTS:
        spot = (me.own_line(part), me.c, slice(None), pl.ds(lo, n))
        toks[spot] = nrm[:, pl.ds(lo, n)]
        for k, step in enumerate((1, 3, 2)):
            send(nrm.at[:, pl.ds(lo, n)], toks.at[spot], g_s.at[part], g_r.at[part * 4 + k], to_line(part, step))
        send(nrm.at[:, pl.ds(lo, n)], toks.at[spot], g_s.at[part], g_r.at[part * 4 + 3], twin)

    def pass_on(k):
        for part, lo, n in PARTS:
            got = toks.at[up(me.own_line(part), (3, 1, 2)[k]), me.c, :, pl.ds(lo, n)]
            whole(got, g_r.at[part * 4 + k])
            send(got, got, g_s.at[part], g_r.at[part * 4 + 3], twin)

    token = lax.broadcasted_iota(I32, (256, 256), 0)
    other = lax.broadcasted_iota(I32, (256, 256), 1)
    earlier = jnp.where((token // 32 == other // 32) & (other < token), 1.0, 0.0).astype(BF16)
    lane = lax.broadcasted_iota(I32, (128, 256), 1)
    spread = jnp.where(lane // 16 == lax.broadcasted_iota(I32, (128, 256), 0), 1.0, 0.0).astype(BF16)
    of_source = other % 16 // 2 == token // 32
    rank_wanted = (other % 2).astype(F32)
    for part in range(3):
        whole(metas.at[part], m_r.at[part])
        table = metas[part].reshape(256, 128)
        column = lax.broadcasted_iota(I32, (256, 128), 1)
        wanted = jnp.where(column < 16, me.expert(part, column), -1).astype(F32)
        hit = jnp.zeros((256, 128), F32)
        weight = jnp.zeros((256, 128), F32)
        for k in range(8):
            same = table[:, k : k + 1] == wanted
            hit = jnp.where(same, 1.0, hit)
            weight = jnp.where(same, table[:, 8 + k : 9 + k], weight)
        rank = dot(earlier, hit.astype(BF16))
        rank = jnp.where(hit > 0.5, rank, -1.0)
        rank = jnp.where(of_source, dot(rank.astype(BF16), spread) - rank_wanted, -1.0)
        weight = dot(weight.astype(BF16), spread)
        for half in range(2):
            chosen = rank == half * 2.0
            pick[part, half] = jnp.where(chosen, 1.0, 0.0).T.astype(BF16)
            wgt[part, half] = jnp.where(chosen, weight, 0.0).astype(BF16)
        if part == 1:
            pass_on(0)
            pass_on(1)
    pass_on(2)
    rx, ry, rz, low = token // 64, token // 16 % 4, token // 4 % 4, token % 4
    swap[0] = jnp.where(other == rz * 64 + ry * 16 + rx * 4 + low, 1.0, 0.0).astype(BF16)
    swap[1] = jnp.where(other == rx * 64 + rz * 16 + ry * 4 + low, 1.0, 0.0).astype(BF16)

    def half_of(ref, half):
        if ref is part4:
            return lambda b1, b2, cols: part4.at[b1, b2, pl.ds(half * 16, 16), cols]
        return lambda b1, b2, cols: ref.at[half, b1, b2, :, cols]

    def exchange(half, src, dst_of, ssem, rsem, parts):
        for d1, d2 in NEAR:
            for part, lo, n in parts:
                b1, b2 = me.own_plane(part)
                e1, e2 = up(b1, d1), up(b2, d2)
                at, cols = half * 3 + part, pl.ds(lo, n)
                send(
                    half_of(src, half)(e1, e2, cols), half_of(dst_of(part), half)(b1, b2, cols),
                    ssem.at[at], rsem.at[at], me.plane(part, e1, e2),
                )
        for part, lo, n in parts:
            b1, b2 = me.own_plane(part)
            at, cols = half * 3 + part, pl.ds(lo, n)
            pltpu.make_async_copy(
                half_of(src, half)(b1, b2, cols), half_of(dst_of(part), half)(b1, b2, cols), rsem.at[at]
            ).start()

    def landing(part):
        return rows if part == 0 else stage

    def sent(half, lo, n, sem):
        for k in range(3):
            whole(outg.at[half, k, :, :, pl.ds(lo, n)], sem)
        whole(outg.at[half, 3, pl.ds(0, 3), :, pl.ds(lo, n)], sem)

    def dispatch(half):
        for part, lo, n in PARTS:
            cols = pl.ds(lo, n)
            if half == 0:
                whole(toks.at[:, 1 - me.c, :, cols], g_r.at[part * 4 + 3])
            value = dot(pick[part, half], toks[:, :, :, cols].reshape(256, n))
            outg[half, :, :, :, cols] = value.astype(BF16).reshape(4, 4, 16, n)
        exchange(half, outg, landing, d_s, d_r, PARTS)

    def expert(half):
        for part, lo, n in PARTS:
            cols = pl.ds(lo, n)
            whole(landing(part).at[half, :, :, :, cols], d_r.at[half * 3 + part])
            if part:
                value = dot(swap[part - 1], stage[half, :, :, :, cols].reshape(256, n))
                rows[half, :, :, :, cols] = value.astype(BF16).reshape(4, 4, 16, n)
        if half == 0:
            loads[0].wait()
            loads[1].wait()

        def hidden(j, carry):
            cols = pl.ds(pl.multiple_of(j * 256, 256), 256)
            more = pl.ds(pl.multiple_of(j * 256 + 1024, 256), 256)
            here = rows[half].reshape(256, 3584)
            gate = dot(here, win[:, cols])
            lift = dot(here, win[:, more])
            hid[0, :, cols] = (gate / (1.0 + jnp.exp(-gate)) * lift).astype(BF16)
            return carry

        lax.fori_loop(0, 4, hidden, 0)
        for part, lo, n in PARTS:
            if part:
                hid[part] = dot(swap[part - 1], hid[0]).astype(BF16)
            sent(half, lo, n, d_s.at[half * 3 + part])
            value = dot(hid[part], wdown[:, pl.ds(lo, n)])
            outg[half, :, :, :, pl.ds(lo, n)] = value.astype(BF16).reshape(4, 4, 16, n)
            if half:
                exchange(half, outg, lambda part: part4, t_s, t_r, ((part, lo, n),))
        if half == 0:
            exchange(half, outg, lambda part: part4, t_s, t_r, PARTS)

    dispatch(0)
    dispatch(1)
    expert(0)
    expert(1)

    for half in range(2):
        for part, lo, n in PARTS:
            cols = pl.ds(lo, n)
            back_rows = part4.at[:, :, pl.ds(half * 16, 16), cols]
            whole(back_rows, t_r.at[half * 3 + part])
            value = dot(wgt[part, half], back_rows[...].reshape(256, n))
            if half == 0:
                half_sum[:, cols] = value
                continue
            psum[:, :, :, cols] = (half_sum[:, cols] + value).astype(BF16).reshape(4, 2, 32, n)
            send(psum.at[:, 1 - me.c, :, cols], other_core.at[:, :, cols], x_s.at[part], x_r.at[part], twin)
    for part, lo, n in PARTS:
        cols = pl.ds(lo, n)
        own = me.own_line(part)
        whole(other_core.at[:, :, cols], x_r.at[part])
        both = psum[:, me.c, :, cols].astype(F32) + other_core[:, :, cols].astype(F32)
        psum[:, me.c, :, cols] = both.astype(BF16)
        for step in (1, 3, 2):
            send(
                psum.at[up(own, step), me.c, :, cols], recv.at[own, :, cols],
                c_s.at[part], c_r.at[part], to_line(part, step),
            )
        pltpu.make_async_copy(psum.at[own, me.c, :, cols], recv.at[own, :, cols], c_r.at[part]).start()
    for part, lo, n in PARTS:
        cols = pl.ds(lo, n)
        whole(recv.at[:, :, cols], c_r.at[part])
        total = stream_ref[:, cols]
        for q in range(4):
            total += recv[q, :, cols].astype(F32)
        out_ref[:, cols] = total
    for part, lo, n in PARTS:
        cols = pl.ds(lo, n)
        for half in range(2):
            sent(half, lo, n, t_s.at[half * 3 + part])
        whole(toks.at[pl.ds(0, 3), :, :, cols], g_s.at[part])
        whole(nrm.at[:, cols], g_s.at[part])
        whole(other_core.at[:, :, cols], x_s.at[part])
        whole(recv.at[pl.ds(0, 3), :, cols], c_s.at[part])
        whole(metas.at[part, pl.ds(0, 7)], m_s.at[part])


def back(stream, norm_gain, routes, weights, expert_in, expert_down):
    vmem = pl.BlockSpec(memory_space=pltpu.VMEM)
    hbm = pl.BlockSpec(memory_space=pl.ANY)
    dma = pltpu.SemaphoreType.DMA
    halves = (2, 4, 4, 16, 3584)
    return pl.pallas_call(
        back_kernel,
        out_shape=jax.ShapeDtypeStruct((32, 3584), F32),
        in_specs=[vmem, vmem, vmem, vmem, hbm, hbm],
        out_specs=vmem,
        scratch_shapes=[
            pltpu.VMEM((3584, 2048), BF16),
            pltpu.VMEM((1024, 3584), BF16),
            pltpu.VMEM((4, 4, 32, 3584), BF16),
            pltpu.VMEM((128, 128), F32),
            pltpu.VMEM((32, 128), F32),
            pltpu.VMEM((3, 8, 32, 128), F32),
            pltpu.VMEM((3, 2, 256, 256), BF16),
            pltpu.VMEM((3, 2, 256, 256), BF16),
            pltpu.VMEM((2, 256, 256), BF16),
            pltpu.VMEM((32, 3584), BF16),
            pltpu.VMEM((4, 2, 32, 3584), BF16),
            pltpu.VMEM(halves, BF16),
            pltpu.VMEM(halves, BF16),
            pltpu.VMEM(halves, BF16),
            pltpu.VMEM((3, 256, 1024), BF16),
            pltpu.VMEM((256, 3584), F32),
            pltpu.VMEM((4, 2, 32, 3584), BF16),
            pltpu.VMEM((4, 32, 3584), BF16),
            pltpu.VMEM((4, 32, 3584), BF16),
            dma((2,)),
            dma((3,)),
            dma((3,)),
            dma((3,)),
            dma((12,)),
            dma((6,)),
            dma((6,)),
            dma((6,)),
            dma((6,)),
            dma((3,)),
            dma((3,)),
            dma((3,)),
            dma((3,)),
        ],
        compiler_params=pltpu.CompilerParams(
            collective_id=1, has_side_effects=True, vmem_limit_bytes=67043328
        ),
        name="back",
    )(stream, norm_gain, routes, weights, expert_in, expert_down)


LOWEST = -1e30


def front_kernel(
    scale, off_ref, q_ref, cache_ref, vup_ref, wot_ref, resid_ref,
    stream_ref,
    keys, kc, vt, qt, vupt, bias, scores, probs, acc, top, tot, slabs, wide, ho,
    part4, r1, l1, r2, l2, mid, r1b, l1b, r2b, l2b,
    k_s, k_r, w_s, w_r, own_sem, rs_s, rs_r,
):
    me = Place()
    here = me.z * 2 + me.c

    def along(axis, n):
        if axis == 0:
            return (here, up(me.x, n) * 4 + me.y)
        return (here, me.x * 4 + up(me.y, n))

    own_copy = pltpu.make_async_copy(cache_ref, keys.at[me.x, me.y], own_sem)
    own_copy.start()

    slabs[me.z, me.c] = wot_ref[...].T
    twin = (me.z * 2 + 1 - me.c, me.x * 4 + me.y)
    above = [(up(me.z, n) * 2 + me.c, me.x * 4 + me.y) for n in (1, 3, 2)]
    others = [along(0, 1), along(0, 3), along(1, 1), along(1, 3), twin] + above
    barrier = pltpu.get_barrier_semaphore()
    for other in others:
        pl.semaphore_signal(barrier, inc=1, device_id=other, device_id_type=MESH)
    pl.semaphore_wait(barrier, len(others))

    def send(src, dst, ssem, rsem, device):
        copy = pltpu.make_async_remote_copy(
            src_ref=src, dst_ref=dst, send_sem=ssem, recv_sem=rsem,
            device_id=device, device_id_type=MESH,
        )
        copy.start()
        return copy

    def axis_of(half, phase):
        return half if phase == 0 else 1 - half

    def spot(half, phase, n, lo, rows):
        rows = pl.ds(half * 96 + lo, rows)
        if axis_of(half, phase) == 0:
            a = up(me.x, n)
            return keys.at[a, me.y, rows] if phase == 0 else keys.at[a, :, rows]
        b = up(me.y, n)
        return keys.at[me.x, b, rows] if phase == 0 else keys.at[:, b, rows]

    def sem(half, phase, k):
        return (half * 2 + phase) * 4 + k

    def spread(half, phase):
        axis = axis_of(half, phase)
        for k, n in ((0, 1), (1, 3)):
            at = spot(half, phase, 0, 0, 96)
            src = cache_ref.at[pl.ds(half * 96, 96)] if phase == 0 else at
            i = sem(half, phase, k)
            send(src, at, k_s.at[i], k_r.at[i], along(axis, n))

    def forward(half, phase):
        axis = axis_of(half, phase)
        for k, n, lo in ((0, 3, 0), (1, 1, 48)):
            whole(spot(half, phase, n, 0, 96), k_r.at[sem(half, phase, k)])
            part = spot(half, phase, n, lo, 48)
            i = sem(half, phase, 2 + k)
            send(part, part, k_s.at[i], k_r.at[i], along(axis, 4 - n))

    def far(half, phase):
        for k, lo in ((0, 0), (1, 48)):
            whole(spot(half, phase, 2, lo, 48), k_r.at[sem(half, phase, 2 + k)])

    for half in range(2):
        spread(half, 0)
    mine = slabs.at[me.z, me.c]
    send(mine, mine, w_s.at[0], w_r.at[0], twin)
    for k, to in enumerate(above):
        send(mine, mine, w_s.at[1 + k], w_r.at[1 + k], to)

    qt[:, :, pl.ds(576, 64), :] = jnp.zeros((2, 2, 64, 512), BF16)
    for tile in range(2):
        for h in range(4):
            lo = h * 576 - h % 2 * 64
            some = q_ref[:, pl.ds(tile * 16, 16), lo : lo + 640].reshape(256, 640).T
            lanes = pl.ds(h % 2 * 256, 256)
            qt[tile, h // 2, pl.ds(0, 576), lanes] = some[64:] if h % 2 else some[:576]
    for half in range(2):
        forward(half, 0)
    for h in range(4):
        vupt[h] = vup_ref[h].T
    kc[:, :, pl.ds(512, 128)] = jnp.zeros((4, 768, 128), BF16)
    top[...] = jnp.full((2, 2, 1, 512), -3e38, F32)
    tot[...] = jnp.zeros((2, 2, 1, 512), F32)
    acc[...] = jnp.zeros((2, 2, 512, 512), F32)
    own_copy.wait()
    for half in range(2):
        far(half, 0)
    for half in range(2):
        spread(half, 1)

    row = lax.broadcasted_iota(I32, (768, 1), 0)
    in_first = row < 384
    low_row = jnp.where(in_first, row, row - 384)
    nth = (low_row >= 96).astype(I32) + (low_row >= 192).astype(I32) + (low_row >= 288).astype(I32)
    low_row = low_row - nth * 96
    base = jnp.where(in_first, nth * 768 + low_row, nth * 192 + 96 + low_row)
    lane = lax.broadcasted_iota(I32, (768, 256), 1)
    query = lane // 16 * 32 + lane % 16

    def turn_of(chunk):
        return chunk + lax.div(chunk, 2) - 2 * lax.div(chunk, 3)

    def build(chunk):
        turn = (0, 1, 3, 2)[chunk]
        b, a = up(me.y, turn), up(me.x, turn)
        kc[chunk, pl.ds(0, 384), pl.ds(0, 576)] = keys[:, b, pl.ds(0, 96), :].reshape(384, 576)
        kc[chunk, pl.ds(384, 384), pl.ds(0, 576)] = keys[a, :, pl.ds(96, 96), :].reshape(384, 576)
        vt[chunk] = kc[chunk, :, pl.ds(0, 512)].T

    def heads(tile):
        for g in range(2):
            context = (acc[tile, g] / tot[tile, g]).astype(BF16)
            for k in range(2):
                value = dot(vupt[2 * g + k], context[:, k * 256 : k * 256 + 256]).T.astype(BF16)
                ho[tile, :, :, :, pl.ds((2 * g + k) * 128, 128)] = value.reshape(4, 4, 16, 128)

    def project(tile, h):
        for b in range(2):
            value = dot(ho[tile].reshape(256, 512), wide[2 * h + b])
            cols = pl.ds(h * 1792 + b * 896, 896)
            part4[tile, :, :, :, cols] = value.astype(BF16).reshape(4, 4, 16, 896)

    def position(h, phase):
        return me.x if h == phase else me.y

    def piece(tile, h, phase, k, lo, n):
        if phase:
            return mid.at[tile, h, k, :, pl.ds(lo, n)]
        cols = pl.ds(h * 1792 + lo, n)
        return part4.at[tile, :, k, :, cols] if h else part4.at[tile, k, :, :, cols]

    def box(i, tile, h, phase, lo, n):
        ref = (r1b, l1b, r2b, l2b)[i] if phase else (r1, l1, r2, l2)[i]
        if phase:
            return ref.at[tile, h, :, pl.ds(lo, n)]
        return ref.at[tile, h, :, :, pl.ds(lo, n)]

    def rs_sem(tile, h, phase, k):
        return ((tile * 2 + h) * 2 + phase) * 6 + k

    def give(tile, h, phase, k, src, dst, n):
        i = rs_sem(tile, h, phase, k)
        send(src, dst, rs_s.at[i], rs_r.at[i], along(0 if h == phase else 1, n))

    def first_far(tile, h, phase):
        for side, (lo, n) in enumerate(((0, 1), (896, 3))):
            src = piece(tile, h, phase, up(position(h, phase), 2), lo, 896)
            give(tile, h, phase, side, src, box(side, tile, h, phase, 0, 896), n)

    def first_near(tile, h, phase):
        for side, (lo, n) in enumerate(((896, 1), (0, 3))):
            src = piece(tile, h, phase, up(position(h, phase), n), lo, 896)
            give(tile, h, phase, 2 + side, src, box(2 + side, tile, h, phase, lo, 896), n)

    def finish(tile):
        heads(tile)
        for h in range(2):
            project(tile, h)
            first_far(tile, h, 0)
        for h in range(2):
            first_near(tile, h, 0)

    def second(tile, phase):
        for h in range(2):
            for side, (lo, n) in enumerate(((0, 1), (896, 3))):
                came = box(side, tile, h, phase, 0, 896)
                whole(came, rs_r.at[rs_sem(tile, h, phase, side)])
                own = piece(tile, h, phase, up(position(h, phase), n), lo, 896)
                own[...] = (own[...].astype(F32) + came[...].astype(F32)).astype(BF16)
                give(tile, h, phase, 4 + side, own, box(2 + side, tile, h, phase, lo, 896), n)

    def last(tile, h, phase):
        for k, (side, lo) in enumerate(((2, 896), (3, 0), (2, 0), (3, 896))):
            whole(box(side, tile, h, phase, lo, 896), rs_r.at[rs_sem(tile, h, phase, 2 + k)])
        total = piece(tile, h, phase, position(h, phase), 0, 1792)[...].astype(F32)
        total += box(2, tile, h, phase, 0, 1792)[...].astype(F32)
        return total + box(3, tile, h, phase, 0, 1792)[...].astype(F32)

    def middle(tile):
        for h in range(2):
            mid[tile, h] = last(tile, h, 0).astype(BF16)
        for h in range(2):
            first_far(tile, h, 1)
        for h in range(2):
            first_near(tile, h, 1)

    def settle(tile):
        rows, cols = pl.ds(tile * 16, 16), (pl.ds(0, 1792), pl.ds(1792, 1792))
        for h in range(2):
            stream_ref[rows, cols[h]] = last(tile, h, 1) + resid_ref[rows, cols[h]].astype(F32)

    build(0)

    def step(i, carry):
        @pl.when(i == 1)
        def _():
            for half in range(2):
                forward(half, 1)
            build(1)
            build(2)

        @pl.when(i == 2)
        def _():
            for half in range(2):
                far(half, 1)
            build(3)
            for k, n in enumerate((3, 1, 2)):
                got = slabs.at[up(me.z, n), me.c]
                whole(got, w_r.at[1 + k])
                send(got, got, w_s.at[4 + k], w_r.at[4 + k], twin)

        @pl.when(i == 3)
        def _():
            whole(slabs.at[me.z, 1 - me.c], w_r.at[0])
            for k, n in enumerate((3, 1, 2)):
                whole(slabs.at[up(me.z, n), 1 - me.c], w_r.at[4 + k])
            for z in range(4):
                wide[z] = jnp.concatenate([slabs[z, 0], slabs[z, 1]], axis=1)
            finish(0)

        tiles = (lax.div(i, 3), jnp.where(i == 1, 0, 1))
        chunks = (turn_of(i), jnp.where(i == 1, 2, jnp.where(i == 2, 1, i)))

        def score(u):
            scores[u % 2] = dot(kc[chunks[u // 2]], qt[tiles[u // 2], u % 2])

        def gather_values(u):
            tile, g = tiles[u // 2], u % 2
            acc[tile, g] += dot(vt[chunks[u // 2]], probs[g])

        score(0)
        for u in range(4):
            tile, g = tiles[u // 2], u % 2
            if u < 3:
                score(u + 1)
            if u > 0:
                gather_values(u - 1)
            if g == 0:
                turn = turn_of(chunks[u // 2])
                start = jnp.where(in_first, up(me.y, turn) * 192, up(me.x, turn) * 768)
                limit = query + (tile * 16 + off_ref[0])
                bias[...] = jnp.where(base + start <= limit, 0.0, LOWEST)
            for k in range(2):
                lanes = pl.ds(k * 256, 256)
                s = scores[g, :, lanes] * scale + bias[...]
                old = top[tile, g, :, lanes]
                new = jnp.maximum(old, jnp.max(s, axis=0, keepdims=True))
                p = jnp.exp2(s - new)
                shrink = jnp.exp2(old - new)
                top[tile, g, :, lanes] = new
                tot[tile, g, :, lanes] = tot[tile, g, :, lanes] * shrink + jnp.sum(p, axis=0, keepdims=True)
                acc[tile, g, :, lanes] = acc[tile, g, :, lanes] * shrink
                probs[g, :, lanes] = p.astype(BF16)
            if u == 1:

                @pl.when(i == 3)
                def _():
                    second(0, 0)

        gather_values(3)
        return carry

    lax.fori_loop(0, 4, step, 0)
    middle(0)
    finish(1)
    second(0, 1)
    second(1, 0)
    settle(0)
    middle(1)
    second(1, 1)
    settle(1)
    for k, n in enumerate((3, 1, 2)):
        whole(mine, w_s.at[1 + k])
        whole(slabs.at[up(me.z, n), me.c], w_s.at[4 + k])
    whole(mine, w_s.at[0])
    for half in range(2):
        for phase in range(2):
            for k in range(2):
                whole(spot(half, phase, 0, 0, 96), k_s.at[sem(half, phase, k)])
                whole(spot(half, phase, 0, 0, 48), k_s.at[sem(half, phase, 2 + k)])
    for tile in range(2):
        for h in range(2):
            for phase in range(2):
                for k in range(6):
                    src = piece(tile, h, phase, 0, 0, 896)
                    whole(src, rs_s.at[rs_sem(tile, h, phase, k)])


def front(offsets, queries, cache, value_up, out_proj, resid, scale):
    vmem = pl.BlockSpec(memory_space=pltpu.VMEM)
    dma = pltpu.SemaphoreType.DMA
    return pl.pallas_call(
        functools.partial(front_kernel, scale),
        out_shape=jax.ShapeDtypeStruct((32, 3584), F32),
        in_specs=[pl.BlockSpec(memory_space=pltpu.SMEM), vmem, vmem, vmem, vmem, vmem],
        out_specs=vmem,
        scratch_shapes=[
            pltpu.VMEM((4, 4, 192, 576), BF16),
            pltpu.VMEM((4, 768, 640), BF16),
            pltpu.VMEM((4, 512, 768), BF16),
            pltpu.VMEM((2, 2, 640, 512), BF16),
            pltpu.VMEM((4, 128, 512), BF16),
            pltpu.VMEM((768, 256), F32),
            pltpu.VMEM((2, 768, 512), F32),
            pltpu.VMEM((2, 768, 512), BF16),
            pltpu.VMEM((2, 2, 512, 512), F32),
            pltpu.VMEM((2, 2, 1, 512), F32),
            pltpu.VMEM((2, 2, 1, 512), F32),
            pltpu.VMEM((4, 2, 512, 448), BF16),
            pltpu.VMEM((4, 512, 896), BF16),
            pltpu.VMEM((2, 4, 4, 16, 512), BF16),
            pltpu.VMEM((2, 4, 4, 16, 3584), BF16),
            pltpu.VMEM((2, 2, 4, 16, 896), BF16),
            pltpu.VMEM((2, 2, 4, 16, 896), BF16),
            pltpu.VMEM((2, 2, 4, 16, 1792), BF16),
            pltpu.VMEM((2, 2, 4, 16, 1792), BF16),
            pltpu.VMEM((2, 2, 4, 16, 1792), BF16),
            pltpu.VMEM((2, 2, 16, 896), BF16),
            pltpu.VMEM((2, 2, 16, 896), BF16),
            pltpu.VMEM((2, 2, 16, 1792), BF16),
            pltpu.VMEM((2, 2, 16, 1792), BF16),
            dma((16,)),
            dma((16,)),
            dma((7,)),
            dma((7,)),
            dma(()),
            dma((48,)),
            dma((48,)),
        ],
        compiler_params=pltpu.CompilerParams(
            collective_id=2, has_side_effects=True, vmem_limit_bytes=67043328
        ),
        name="front",
    )(offsets, queries, cache, value_up, out_proj, resid)


def shards(
    queries,
    cache,
    offsets,
    value_up,
    out_proj,
    resid,
    norm_gain,
    routes,
    route_weights,
    expert_in,
    expert_down,
):
    latent_width = value_up.shape[1]
    key_width = cache.shape[2]
    score_scale = (value_up.shape[2] + key_width - latent_width) ** (-0.5)
    stream = front(
        offsets, queries.reshape(16, 32, -1), cache[0], value_up, out_proj.T, resid,
        score_scale * LOG2_E,
    )
    mixed = back(stream, norm_gain, routes.T, route_weights.T, expert_in[0], expert_down[0])
    return mixed.astype(BF16)


def solution(mesh):
    return jax.shard_map(
        shards,
        mesh=mesh,
        in_specs=(
            P("dp", "tensor"),
            P("dp", "tensor", None),
            P("dp"),
            P("tensor", None, None),
            P("tensor", "dp"),
            P(("dp", "tensor"), None),
            P(),
            P(("dp", "tensor"), None),
            P(("dp", "tensor"), None),
            P(("dp", "tensor"), None, None),
            P(("dp", "tensor"), None, None),
        ),
        out_specs=P(("dp", "tensor"), None),
        check_vma=False,
    )
```

```python
import functools

import jax
import jax.numpy as jnp
from jax import lax
from jax.experimental import pallas as pl
from jax.experimental.pallas import tpu as pltpu
from jax.sharding import PartitionSpec as P

MESH = pl.DeviceIdType.MESH
LOG2_E = 1.4426950408889634
BF16, F32, I32 = jnp.bfloat16, jnp.float32, jnp.int32
NEAR = (
    (1, 0), (0, 1), (3, 0), (0, 3), (1, 1), (3, 3), (1, 3), (3, 1),
    (2, 0), (0, 2), (2, 2), (2, 1), (1, 2), (2, 3), (3, 2),
)
PARTS = ((0, 0, 1280), (1, 1280, 1152), (2, 2432, 1152))


def whole(ref, sem):
    pltpu.make_async_copy(ref, ref, sem).wait()


def dot(a, b):
    return jnp.dot(a, b, preferred_element_type=F32)


class Place:
    def __init__(self):
        dp, t = lax.axis_index("dp"), lax.axis_index("tensor")
        self.z, self.c = lax.div(dp, 2), lax.rem(dp, 2)
        self.x, self.y = lax.div(t, 4), lax.rem(t, 4)

    def line(self, part, a, core):
        if part == 0:
            return (a * 2 + core, self.x * 4 + self.y)
        if part == 1:
            return (self.z * 2 + core, a * 4 + self.y)
        return (self.z * 2 + core, self.x * 4 + a)

    def own_line(self, part):
        return (self.z, self.x, self.y)[part]

    def plane(self, part, b1, b2):
        if part == 0:
            return (self.z * 2 + self.c, b1 * 4 + b2)
        if part == 1:
            return (b1 * 2 + self.c, self.x * 4 + b2)
        return (b2 * 2 + self.c, b1 * 4 + self.y)

    def own_plane(self, part):
        return ((self.x, self.y), (self.z, self.y), (self.x, self.z))[part]

    def expert(self, part, j):
        b1, b2 = j // 4, j % 4
        if part == 0:
            return (self.z * 2 + self.c) * 16 + j
        if part == 1:
            return (b1 * 2 + self.c) * 16 + self.x * 4 + b2
        return (b2 * 2 + self.c) * 16 + b1 * 4 + self.y


def up(v, n):
    return lax.rem(v + n, 4)


def partners(me):
    out = [(me.z * 2 + 1 - me.c, me.x * 4 + me.y)]
    for part in range(3):
        for n in (1, 2, 3):
            out.append(me.line(part, up(me.own_line(part), n), 1 - me.c))
    for dz in range(4):
        for dx in range(4):
            for dy in range(4):
                if (dz, dx, dy) != (0, 0, 0) and 0 in (dz, dx, dy):
                    out.append((up(me.z, dz) * 2 + me.c, up(me.x, dx) * 4 + up(me.y, dy)))
    return out


def back_kernel(
    stream_ref, gain_ref, routes_ref, weights_ref, win_hbm, wdown_hbm,
    out_ref,
    win, wdown, part4, turned, table_ref, metas, pick, wgt, swap,
    nrm, toks, outg, rows, stage, hid, half_sum, psum, other_core, recv,
    wsem, m_s, m_r, g_s, g_r, d_s, d_r, t_s, t_r, x_s, x_r, c_s, c_r,
):
    me = Place()
    barrier = pltpu.get_barrier_semaphore()
    others = partners(me)
    for other in others:
        pl.semaphore_signal(barrier, inc=1, device_id=other, device_id_type=MESH)
    loads = [
        pltpu.make_async_copy(win_hbm, win, wsem.at[0]),
        pltpu.make_async_copy(wdown_hbm, wdown, wsem.at[1]),
    ]
    for load in loads:
        load.start()
    turned[...] = jnp.zeros((128, 128), F32)
    turned[pl.ds(0, 8), pl.ds(0, 32)] = routes_ref[...].astype(F32)
    turned[pl.ds(8, 8), pl.ds(0, 32)] = weights_ref[...]
    table_ref[...] = turned[...].T[:32]
    value = stream_ref[...]
    mean_square = jnp.mean(value * value, axis=1, keepdims=True)
    nrm[...] = (value * lax.rsqrt(mean_square + 1e-06) * gain_ref[...].reshape(1, 3584)).astype(BF16)
    pl.semaphore_wait(barrier, len(others))

    def send(src, dst, ssem, rsem, device):
        copy = pltpu.make_async_remote_copy(
            src_ref=src, dst_ref=dst, send_sem=ssem, recv_sem=rsem,
            device_id=device, device_id_type=MESH,
        )
        copy.start()
        return copy

    meta_sends = []
    for part in range(3):
        own = me.own_line(part) * 2 + me.c
        for n in range(4):
            for core in range(2):
                if (n, core) == (0, 0):
                    continue
                to = me.line(part, up(me.own_line(part), n), lax.rem(me.c + core, 2))
                meta_sends.append(send(table_ref, metas.at[part, own], m_s.at[part], m_r.at[part], to))
        pltpu.make_async_copy(table_ref, metas.at[part, own], m_r.at[part]).start()

    def to_line(part, n):
        return me.line(part, up(me.own_line(part), n), me.c)

    twin = (me.z * 2 + 1 - me.c, me.x * 4 + me.y)
    for part, lo, n in PARTS:
        spot = (me.own_line(part), me.c, slice(None), pl.ds(lo, n))
        toks[spot] = nrm[:, pl.ds(lo, n)]
        for k, step in enumerate((1, 3, 2)):
            send(nrm.at[:, pl.ds(lo, n)], toks.at[spot], g_s.at[part], g_r.at[part * 4 + k], to_line(part, step))
        send(nrm.at[:, pl.ds(lo, n)], toks.at[spot], g_s.at[part], g_r.at[part * 4 + 3], twin)

    def pass_on(k):
        for part, lo, n in PARTS:
            got = toks.at[up(me.own_line(part), (3, 1, 2)[k]), me.c, :, pl.ds(lo, n)]
            whole(got, g_r.at[part * 4 + k])
            send(got, got, g_s.at[part], g_r.at[part * 4 + 3], twin)

    token = lax.broadcasted_iota(I32, (256, 256), 0)
    other = lax.broadcasted_iota(I32, (256, 256), 1)
    earlier = jnp.where((token // 32 == other // 32) & (other < token), 1.0, 0.0).astype(BF16)
    lane = lax.broadcasted_iota(I32, (128, 256), 1)
    spread = jnp.where(lane // 16 == lax.broadcasted_iota(I32, (128, 256), 0), 1.0, 0.0).astype(BF16)
    of_source = other % 16 // 2 == token // 32
    rank_wanted = (other % 2).astype(F32)
    for part in range(3):
        whole(metas.at[part], m_r.at[part])
        table = metas[part].reshape(256, 128)
        column = lax.broadcasted_iota(I32, (256, 128), 1)
        wanted = jnp.where(column < 16, me.expert(part, column), -1).astype(F32)
        hit = jnp.zeros((256, 128), F32)
        weight = jnp.zeros((256, 128), F32)
        for k in range(8):
            same = table[:, k : k + 1] == wanted
            hit = jnp.where(same, 1.0, hit)
            weight = jnp.where(same, table[:, 8 + k : 9 + k], weight)
        rank = dot(earlier, hit.astype(BF16))
        rank = jnp.where(hit > 0.5, rank, -1.0)
        rank = jnp.where(of_source, dot(rank.astype(BF16), spread) - rank_wanted, -1.0)
        weight = dot(weight.astype(BF16), spread)
        for half in range(2):
            chosen = rank == half * 2.0
            pick[part, half] = jnp.where(chosen, 1.0, 0.0).T.astype(BF16)
            wgt[part, half] = jnp.where(chosen, weight, 0.0).astype(BF16)
        if part == 1:
            pass_on(0)
            pass_on(1)
    pass_on(2)
    rx, ry, rz, low = token // 64, token // 16 % 4, token // 4 % 4, token % 4
    swap[0] = jnp.where(other == rz * 64 + ry * 16 + rx * 4 + low, 1.0, 0.0).astype(BF16)
    swap[1] = jnp.where(other == rx * 64 + rz * 16 + ry * 4 + low, 1.0, 0.0).astype(BF16)

    def half_of(ref, half):
        if ref is part4:
            return lambda b1, b2, cols: part4.at[b1, b2, pl.ds(half * 16, 16), cols]
        return lambda b1, b2, cols: ref.at[half, b1, b2, :, cols]

    def exchange(half, src, dst_of, ssem, rsem, parts):
        for d1, d2 in NEAR:
            for part, lo, n in parts:
                b1, b2 = me.own_plane(part)
                e1, e2 = up(b1, d1), up(b2, d2)
                at, cols = half * 3 + part, pl.ds(lo, n)
                send(
                    half_of(src, half)(e1, e2, cols), half_of(dst_of(part), half)(b1, b2, cols),
                    ssem.at[at], rsem.at[at], me.plane(part, e1, e2),
                )
        for part, lo, n in parts:
            b1, b2 = me.own_plane(part)
            at, cols = half * 3 + part, pl.ds(lo, n)
            pltpu.make_async_copy(
                half_of(src, half)(b1, b2, cols), half_of(dst_of(part), half)(b1, b2, cols), rsem.at[at]
            ).start()

    def landing(part):
        return rows if part == 0 else stage

    def sent(half, lo, n, sem):
        for k in range(3):
            whole(outg.at[half, k, :, :, pl.ds(lo, n)], sem)
        whole(outg.at[half, 3, pl.ds(0, 3), :, pl.ds(lo, n)], sem)

    def dispatch(half):
        for part, lo, n in PARTS:
            cols = pl.ds(lo, n)
            if half == 0:
                whole(toks.at[:, 1 - me.c, :, cols], g_r.at[part * 4 + 3])
            value = dot(pick[part, half], toks[:, :, :, cols].reshape(256, n))
            outg[half, :, :, :, cols] = value.astype(BF16).reshape(4, 4, 16, n)
        exchange(half, outg, landing, d_s, d_r, PARTS)

    def expert(half):
        for part, lo, n in PARTS:
            cols = pl.ds(lo, n)
            whole(landing(part).at[half, :, :, :, cols], d_r.at[half * 3 + part])
            if part:
                value = dot(swap[part - 1], stage[half, :, :, :, cols].reshape(256, n))
                rows[half, :, :, :, cols] = value.astype(BF16).reshape(4, 4, 16, n)
        if half == 0:
            loads[0].wait()
            loads[1].wait()

        def hidden(j, carry):
            cols = pl.ds(pl.multiple_of(j * 256, 256), 256)
            more = pl.ds(pl.multiple_of(j * 256 + 1024, 256), 256)
            here = rows[half].reshape(256, 3584)
            gate = dot(here, win[:, cols])
            lift = dot(here, win[:, more])
            hid[0, :, cols] = (gate / (1.0 + jnp.exp(-gate)) * lift).astype(BF16)
            return carry

        lax.fori_loop(0, 4, hidden, 0)
        for part, lo, n in PARTS:
            if part:
                hid[part] = dot(swap[part - 1], hid[0]).astype(BF16)
            sent(half, lo, n, d_s.at[half * 3 + part])
            value = dot(hid[part], wdown[:, pl.ds(lo, n)])
            outg[half, :, :, :, pl.ds(lo, n)] = value.astype(BF16).reshape(4, 4, 16, n)
            if half:
                exchange(half, outg, lambda part: part4, t_s, t_r, ((part, lo, n),))
        if half == 0:
            exchange(half, outg, lambda part: part4, t_s, t_r, PARTS)

    dispatch(0)
    dispatch(1)
    expert(0)
    expert(1)

    for half in range(2):
        for part, lo, n in PARTS:
            cols = pl.ds(lo, n)
            back_rows = part4.at[:, :, pl.ds(half * 16, 16), cols]
            whole(back_rows, t_r.at[half * 3 + part])
            value = dot(wgt[part, half], back_rows[...].reshape(256, n))
            if half == 0:
                half_sum[:, cols] = value
                continue
            psum[:, :, :, cols] = (half_sum[:, cols] + value).astype(BF16).reshape(4, 2, 32, n)
            send(psum.at[:, 1 - me.c, :, cols], other_core.at[:, :, cols], x_s.at[part], x_r.at[part], twin)
    for part, lo, n in PARTS:
        cols = pl.ds(lo, n)
        own = me.own_line(part)
        whole(other_core.at[:, :, cols], x_r.at[part])
        both = psum[:, me.c, :, cols].astype(F32) + other_core[:, :, cols].astype(F32)
        psum[:, me.c, :, cols] = both.astype(BF16)
        for step in (1, 3, 2):
            send(
                psum.at[up(own, step), me.c, :, cols], recv.at[own, :, cols],
                c_s.at[part], c_r.at[part], to_line(part, step),
            )
        pltpu.make_async_copy(psum.at[own, me.c, :, cols], recv.at[own, :, cols], c_r.at[part]).start()
    for part, lo, n in PARTS:
        cols = pl.ds(lo, n)
        whole(recv.at[:, :, cols], c_r.at[part])
        total = stream_ref[:, cols]
        for q in range(4):
            total += recv[q, :, cols].astype(F32)
        out_ref[:, cols] = total
    for part, lo, n in PARTS:
        cols = pl.ds(lo, n)
        for half in range(2):
            sent(half, lo, n, t_s.at[half * 3 + part])
        whole(toks.at[pl.ds(0, 3), :, :, cols], g_s.at[part])
        whole(nrm.at[:, cols], g_s.at[part])
        whole(other_core.at[:, :, cols], x_s.at[part])
        whole(recv.at[pl.ds(0, 3), :, cols], c_s.at[part])
        whole(metas.at[part, pl.ds(0, 7)], m_s.at[part])


def back(stream, norm_gain, routes, weights, expert_in, expert_down):
    vmem = pl.BlockSpec(memory_space=pltpu.VMEM)
    hbm = pl.BlockSpec(memory_space=pl.ANY)
    dma = pltpu.SemaphoreType.DMA
    halves = (2, 4, 4, 16, 3584)
    return pl.pallas_call(
        back_kernel,
        out_shape=jax.ShapeDtypeStruct((32, 3584), F32),
        in_specs=[vmem, vmem, vmem, vmem, hbm, hbm],
        out_specs=vmem,
        scratch_shapes=[
            pltpu.VMEM((3584, 2048), BF16),
            pltpu.VMEM((1024, 3584), BF16),
            pltpu.VMEM((4, 4, 32, 3584), BF16),
            pltpu.VMEM((128, 128), F32),
            pltpu.VMEM((32, 128), F32),
            pltpu.VMEM((3, 8, 32, 128), F32),
            pltpu.VMEM((3, 2, 256, 256), BF16),
            pltpu.VMEM((3, 2, 256, 256), BF16),
            pltpu.VMEM((2, 256, 256), BF16),
            pltpu.VMEM((32, 3584), BF16),
            pltpu.VMEM((4, 2, 32, 3584), BF16),
            pltpu.VMEM(halves, BF16),
            pltpu.VMEM(halves, BF16),
            pltpu.VMEM(halves, BF16),
            pltpu.VMEM((3, 256, 1024), BF16),
            pltpu.VMEM((256, 3584), F32),
            pltpu.VMEM((4, 2, 32, 3584), BF16),
            pltpu.VMEM((4, 32, 3584), BF16),
            pltpu.VMEM((4, 32, 3584), BF16),
            dma((2,)),
            dma((3,)),
            dma((3,)),
            dma((3,)),
            dma((12,)),
            dma((6,)),
            dma((6,)),
            dma((6,)),
            dma((6,)),
            dma((3,)),
            dma((3,)),
            dma((3,)),
            dma((3,)),
        ],
        compiler_params=pltpu.CompilerParams(
            collective_id=1, has_side_effects=True, vmem_limit_bytes=67043328
        ),
        name="back",
    )(stream, norm_gain, routes, weights, expert_in, expert_down)


LOWEST = -1e30


def front_kernel(
    scale, off_ref, q_ref, cache_ref, vup_ref, wot_ref, resid_ref,
    stream_ref,
    keys, kc, vt, qt, vupt, places, bias, scores, probs, acc, top, tot, slabs, wide, ho,
    part4, r1, l1, r2, l2, mid, r1b, l1b, r2b, l2b,
    k_s, k_r, w_s, w_r, own_sem, rs_s, rs_r,
):
    me = Place()
    here = me.z * 2 + me.c

    def along(axis, n):
        if axis == 0:
            return (here, up(me.x, n) * 4 + me.y)
        return (here, me.x * 4 + up(me.y, n))

    own_copy = pltpu.make_async_copy(cache_ref, keys.at[me.x, me.y], own_sem)
    own_copy.start()

    slabs[me.z, me.c] = wot_ref[...].T
    twin = (me.z * 2 + 1 - me.c, me.x * 4 + me.y)
    above = [(up(me.z, n) * 2 + me.c, me.x * 4 + me.y) for n in (1, 3, 2)]
    others = [along(0, 1), along(0, 3), along(1, 1), along(1, 3), twin] + above
    barrier = pltpu.get_barrier_semaphore()
    for other in others:
        pl.semaphore_signal(barrier, inc=1, device_id=other, device_id_type=MESH)
    pl.semaphore_wait(barrier, len(others))

    def send(src, dst, ssem, rsem, device):
        copy = pltpu.make_async_remote_copy(
            src_ref=src, dst_ref=dst, send_sem=ssem, recv_sem=rsem,
            device_id=device, device_id_type=MESH,
        )
        copy.start()
        return copy

    def axis_of(half, phase):
        return half if phase == 0 else 1 - half

    def spot(half, phase, n, lo, rows, part=0):
        rows = pl.ds(half * 96 + lo, rows)
        two = pl.ds(part * 2, 2)
        if axis_of(half, phase) == 0:
            a = up(me.x, n)
            return keys.at[a, me.y, rows] if phase == 0 else keys.at[a, two, rows]
        b = up(me.y, n)
        return keys.at[me.x, b, rows] if phase == 0 else keys.at[two, b, rows]

    def sem(half, phase, k, part=0):
        return half * 12 + phase * 4 + part * 4 + k

    def spread(half, phase, part=0):
        axis = axis_of(half, phase)
        for k, n in ((0, 1), (1, 3)):
            at = spot(half, phase, 0, 0, 96, part)
            src = cache_ref.at[pl.ds(half * 96, 96)] if phase == 0 else at
            i = sem(half, phase, k, part)
            send(src, at, k_s.at[i], k_r.at[i], along(axis, n))

    def forward(half, phase, part=0):
        axis = axis_of(half, phase)
        for k, n, lo in ((0, 3, 0), (1, 1, 48)):
            whole(spot(half, phase, n, 0, 96, part), k_r.at[sem(half, phase, k, part)])
            some = spot(half, phase, n, lo, 48, part)
            i = sem(half, phase, 2 + k, part)
            send(some, some, k_s.at[i], k_r.at[i], along(axis, 4 - n))

    def far(half, phase, part=0):
        for k, lo in ((0, 0), (1, 48)):
            whole(spot(half, phase, 2, lo, 48, part), k_r.at[sem(half, phase, 2 + k, part)])

    for half in range(2):
        spread(half, 0)
    mine = slabs.at[me.z, me.c]
    send(mine, mine, w_s.at[0], w_r.at[0], twin)
    for k, to in enumerate(above):
        send(mine, mine, w_s.at[1 + k], w_r.at[1 + k], to)

    qt[:, :, pl.ds(576, 64), :] = jnp.zeros((2, 2, 64, 512), BF16)
    for tile in range(2):
        for h in range(4):
            lo = h * 576 - h % 2 * 64
            some = q_ref[:, pl.ds(tile * 16, 16), lo : lo + 640].reshape(256, 640).T
            lanes = pl.ds(h % 2 * 256, 256)
            qt[tile, h // 2, pl.ds(0, 576), lanes] = some[64:] if h % 2 else some[:576]
    for half in range(2):
        forward(half, 0)
    for h in range(4):
        vupt[h] = vup_ref[h].T
    kc[:, :, pl.ds(512, 128)] = jnp.zeros((4, 768, 128), BF16)
    top[...] = jnp.full((2, 2, 1, 512), -3e38, F32)
    tot[...] = jnp.zeros((2, 2, 1, 512), F32)
    acc[...] = jnp.zeros((2, 2, 512, 512), F32)
    own_copy.wait()
    for half in range(2):
        far(half, 0)
    for part in range(2):
        for half in range(2):
            spread(half, 1, part)

    lane = lax.broadcasted_iota(I32, (1, 256), 1)
    query = lane // 16 * 32 + lane % 16

    def build(chunk):
        for half in range(2):
            mine = me.x if half else me.y
            at = pl.ds(half * 384, 384)
            rows = pl.ds(half * 96, 96)
            if chunk in (0, 3):
                n = up(mine, 0 if chunk == 0 else 2)
                block = keys[n, :, rows, :] if half else keys[:, n, rows, :]
                kc[chunk, at, pl.ds(0, 576)] = block.reshape(384, 576)
                continue
            two = pl.ds(chunk * 2 - 2, 2)
            for k, n in enumerate((1, 3)):
                n = up(mine, n)
                block = keys[n, two, rows, :] if half else keys[two, n, rows, :]
                kc[chunk, pl.ds(half * 384 + k * 192, 192), pl.ds(0, 576)] = block.reshape(192, 576)
        vt[chunk] = kc[chunk, :, pl.ds(0, 512)].T

    low_row = lax.broadcasted_iota(I32, (96, 128), 0) - off_ref[0]
    for chunk in range(4):
        for half in range(2):
            for k in range(4):
                step, order = (0 if chunk == 0 else 2), k
                if chunk in (1, 2):
                    step, order = (1, 3)[k // 2], k % 2 + chunk * 2 - 2
                across = up(me.x if half else me.y, step)
                block = across * 4 + order if half else order * 4 + across
                places[chunk, pl.ds((half * 4 + k) * 96, 96)] = low_row + (block * 192 + half * 96)

    def heads(tile):
        for g in range(2):
            context = (acc[tile, g] * (1.0 / tot[tile, g])).astype(BF16)
            for k in range(2):
                value = dot(vupt[2 * g + k], context[:, k * 256 : k * 256 + 256]).T.astype(BF16)
                ho[tile, :, :, :, pl.ds((2 * g + k) * 128, 128)] = value.reshape(4, 4, 16, 128)

    def project(tile, h):
        for b in range(2):
            value = dot(ho[tile].reshape(256, 512), wide[2 * h + b])
            cols = pl.ds(h * 1792 + b * 896, 896)
            part4[tile, :, :, :, cols] = value.astype(BF16).reshape(4, 4, 16, 896)

    def position(h, phase):
        return me.x if h == phase else me.y

    def piece(tile, h, phase, k, lo, n):
        if phase:
            return mid.at[tile, h, k, :, pl.ds(lo, n)]
        cols = pl.ds(h * 1792 + lo, n)
        return part4.at[tile, :, k, :, cols] if h else part4.at[tile, k, :, :, cols]

    def box(i, tile, h, phase, lo, n):
        ref = (r1b, l1b, r2b, l2b)[i] if phase else (r1, l1, r2, l2)[i]
        if phase:
            return ref.at[tile, h, :, pl.ds(lo, n)]
        return ref.at[tile, h, :, :, pl.ds(lo, n)]

    def rs_sem(tile, h, phase, k):
        return ((tile * 2 + h) * 2 + phase) * 6 + k

    def give(tile, h, phase, k, src, dst, n):
        i = rs_sem(tile, h, phase, k)
        send(src, dst, rs_s.at[i], rs_r.at[i], along(0 if h == phase else 1, n))

    def first_far(tile, h, phase):
        for side, (lo, n) in enumerate(((0, 1), (896, 3))):
            src = piece(tile, h, phase, up(position(h, phase), 2), lo, 896)
            give(tile, h, phase, side, src, box(side, tile, h, phase, 0, 896), n)

    def first_near(tile, h, phase):
        for side, (lo, n) in enumerate(((896, 1), (0, 3))):
            src = piece(tile, h, phase, up(position(h, phase), n), lo, 896)
            give(tile, h, phase, 2 + side, src, box(2 + side, tile, h, phase, lo, 896), n)

    def finish(tile):
        heads(tile)
        for h in range(2):
            project(tile, h)
            first_far(tile, h, 0)
        for h in range(2):
            first_near(tile, h, 0)

    def second(tile, phase):
        for h in range(2):
            for side, (lo, n) in enumerate(((0, 1), (896, 3))):
                came = box(side, tile, h, phase, 0, 896)
                whole(came, rs_r.at[rs_sem(tile, h, phase, side)])
                own = piece(tile, h, phase, up(position(h, phase), n), lo, 896)
                own[...] = (own[...].astype(F32) + came[...].astype(F32)).astype(BF16)
                give(tile, h, phase, 4 + side, own, box(2 + side, tile, h, phase, lo, 896), n)

    def last(tile, h, phase):
        for k, (side, lo) in enumerate(((2, 896), (3, 0), (2, 0), (3, 896))):
            whole(box(side, tile, h, phase, lo, 896), rs_r.at[rs_sem(tile, h, phase, 2 + k)])
        total = piece(tile, h, phase, position(h, phase), 0, 1792)[...].astype(F32)
        total += box(2, tile, h, phase, 0, 1792)[...].astype(F32)
        return total + box(3, tile, h, phase, 0, 1792)[...].astype(F32)

    def middle(tile):
        for h in range(2):
            mid[tile, h] = last(tile, h, 0).astype(BF16)
        for h in range(2):
            first_far(tile, h, 1)
        for h in range(2):
            first_near(tile, h, 1)

    def settle(tile):
        rows, cols = pl.ds(tile * 16, 16), (pl.ds(0, 1792), pl.ds(1792, 1792))
        for h in range(2):
            stream_ref[rows, cols[h]] = last(tile, h, 1) + resid_ref[rows, cols[h]].astype(F32)

    build(0)

    def step(i, carry):
        @pl.when(i == 1)
        def _():
            for half in range(2):
                forward(half, 1, 0)
            build(1)

        @pl.when(i == 2)
        def _():
            for part in range(2):
                for half in range(2):
                    far(half, 1, part)
            build(3)
            for k, n in enumerate((3, 1, 2)):
                got = slabs.at[up(me.z, n), me.c]
                whole(got, w_r.at[1 + k])
                send(got, got, w_s.at[4 + k], w_r.at[4 + k], twin)

        @pl.when(i == 3)
        def _():
            whole(slabs.at[me.z, 1 - me.c], w_r.at[0])
            for k, n in enumerate((3, 1, 2)):
                whole(slabs.at[up(me.z, n), 1 - me.c], w_r.at[4 + k])
            for z in range(4):
                wide[z] = jnp.concatenate([slabs[z, 0], slabs[z, 1]], axis=1)
            finish(0)

        tiles = (lax.div(i, 3), jnp.where(i == 1, 0, 1))
        chunks = (i + lax.div(i, 2) - 2 * lax.div(i, 3), jnp.where(i == 1, 2, jnp.where(i == 2, 1, i)))

        def score(u):
            scores[u % 2] = dot(kc[chunks[u // 2]], qt[tiles[u // 2], u % 2])

        def gather_values(u):
            tile, g = tiles[u // 2], u % 2
            acc[tile, g] += dot(vt[chunks[u // 2]], probs[g])

        score(0)
        for u in range(4):
            tile, g = tiles[u // 2], u % 2
            if u < 3:
                score(u + 1)
            if u > 0:
                gather_values(u - 1)
            if g == 0:
                place = places[chunks[u // 2]]
                place = jnp.concatenate([place, place], axis=1)
                bias[...] = jnp.where(place <= query + tile * 16, 0.0, LOWEST)
            for k in range(2):
                lanes = pl.ds(k * 256, 256)
                s = scores[g, :, lanes] * scale + bias[...]
                old = top[tile, g, :, lanes]
                new = jnp.maximum(old, jnp.max(s, axis=0, keepdims=True))
                p = jnp.exp2(s - new)
                shrink = jnp.exp2(old - new)
                top[tile, g, :, lanes] = new
                tot[tile, g, :, lanes] = tot[tile, g, :, lanes] * shrink + jnp.sum(p, axis=0, keepdims=True)
                acc[tile, g, :, lanes] = acc[tile, g, :, lanes] * shrink
                probs[g, :, lanes] = p.astype(BF16)
            if u == 0:

                @pl.when(i == 1)
                def _():
                    for half in range(2):
                        forward(half, 1, 1)
                    build(2)

            if u == 1:

                @pl.when(i == 3)
                def _():
                    second(0, 0)

        gather_values(3)
        return carry

    lax.fori_loop(0, 4, step, 0)
    finish(1)
    middle(0)
    second(1, 0)
    second(0, 1)
    middle(1)
    settle(0)
    second(1, 1)
    settle(1)
    for k, n in enumerate((3, 1, 2)):
        whole(mine, w_s.at[1 + k])
        whole(slabs.at[up(me.z, n), me.c], w_s.at[4 + k])
    whole(mine, w_s.at[0])
    for half in range(2):
        for phase, part in ((0, 0), (1, 0), (1, 1)):
            for k in range(2):
                whole(spot(half, phase, 0, 0, 96, part), k_s.at[sem(half, phase, k, part)])
                whole(spot(half, phase, 0, 0, 48, part), k_s.at[sem(half, phase, 2 + k, part)])
    for tile in range(2):
        for h in range(2):
            for phase in range(2):
                for k in range(6):
                    src = piece(tile, h, phase, 0, 0, 896)
                    whole(src, rs_s.at[rs_sem(tile, h, phase, k)])


def front(offsets, queries, cache, value_up, out_proj, resid, scale):
    vmem = pl.BlockSpec(memory_space=pltpu.VMEM)
    dma = pltpu.SemaphoreType.DMA
    return pl.pallas_call(
        functools.partial(front_kernel, scale),
        out_shape=jax.ShapeDtypeStruct((32, 3584), F32),
        in_specs=[pl.BlockSpec(memory_space=pltpu.SMEM), vmem, vmem, vmem, vmem, vmem],
        out_specs=vmem,
        scratch_shapes=[
            pltpu.VMEM((4, 4, 192, 576), BF16),
            pltpu.VMEM((4, 768, 640), BF16),
            pltpu.VMEM((4, 512, 768), BF16),
            pltpu.VMEM((2, 2, 640, 512), BF16),
            pltpu.VMEM((4, 128, 512), BF16),
            pltpu.VMEM((4, 768, 128), I32),
            pltpu.VMEM((768, 256), F32),
            pltpu.VMEM((2, 768, 512), F32),
            pltpu.VMEM((2, 768, 512), BF16),
            pltpu.VMEM((2, 2, 512, 512), F32),
            pltpu.VMEM((2, 2, 1, 512), F32),
            pltpu.VMEM((2, 2, 1, 512), F32),
            pltpu.VMEM((4, 2, 512, 448), BF16),
            pltpu.VMEM((4, 512, 896), BF16),
            pltpu.VMEM((2, 4, 4, 16, 512), BF16),
            pltpu.VMEM((2, 4, 4, 16, 3584), BF16),
            pltpu.VMEM((2, 2, 4, 16, 896), BF16),
            pltpu.VMEM((2, 2, 4, 16, 896), BF16),
            pltpu.VMEM((2, 2, 4, 16, 1792), BF16),
            pltpu.VMEM((2, 2, 4, 16, 1792), BF16),
            pltpu.VMEM((2, 2, 4, 16, 1792), BF16),
            pltpu.VMEM((2, 2, 16, 896), BF16),
            pltpu.VMEM((2, 2, 16, 896), BF16),
            pltpu.VMEM((2, 2, 16, 1792), BF16),
            pltpu.VMEM((2, 2, 16, 1792), BF16),
            dma((24,)),
            dma((24,)),
            dma((7,)),
            dma((7,)),
            dma(()),
            dma((48,)),
            dma((48,)),
        ],
        compiler_params=pltpu.CompilerParams(
            collective_id=2, has_side_effects=True, vmem_limit_bytes=67043328
        ),
        name="front",
    )(offsets, queries, cache, value_up, out_proj, resid)


def shards(
    queries,
    cache,
    offsets,
    value_up,
    out_proj,
    resid,
    norm_gain,
    routes,
    route_weights,
    expert_in,
    expert_down,
):
    latent_width = value_up.shape[1]
    key_width = cache.shape[2]
    score_scale = (value_up.shape[2] + key_width - latent_width) ** (-0.5)
    stream = front(
        offsets, queries.reshape(16, 32, -1), cache[0], value_up, out_proj.T, resid,
        score_scale * LOG2_E,
    )
    mixed = back(stream, norm_gain, routes.T, route_weights.T, expert_in[0], expert_down[0])
    return mixed.astype(BF16)


def solution(mesh):
    return jax.shard_map(
        shards,
        mesh=mesh,
        in_specs=(
            P("dp", "tensor"),
            P("dp", "tensor", None),
            P("dp"),
            P("tensor", None, None),
            P("tensor", "dp"),
            P(("dp", "tensor"), None),
            P(),
            P(("dp", "tensor"), None),
            P(("dp", "tensor"), None),
            P(("dp", "tensor"), None, None),
            P(("dp", "tensor"), None, None),
        ),
        out_specs=P(("dp", "tensor"), None),
        check_vma=False,
    )
```

```python
import functools

import jax
import jax.numpy as jnp
from jax import lax
from jax.experimental import pallas as pl
from jax.experimental.pallas import tpu as pltpu
from jax.sharding import PartitionSpec as P

MESH = pl.DeviceIdType.MESH
LOG2_E = 1.4426950408889634
BF16, F32, I32 = jnp.bfloat16, jnp.float32, jnp.int32
NEAR = (
    (1, 0), (0, 1), (3, 0), (0, 3), (1, 1), (3, 3), (1, 3), (3, 1),
    (2, 0), (0, 2), (2, 2), (2, 1), (1, 2), (2, 3), (3, 2),
)
PARTS = ((0, 0, 1280), (1, 1280, 1152), (2, 2432, 1152))


def whole(ref, sem):
    pltpu.make_async_copy(ref, ref, sem).wait()


def dot(a, b):
    return jnp.dot(a, b, preferred_element_type=F32)


class Place:
    def __init__(self):
        dp, t = lax.axis_index("dp"), lax.axis_index("tensor")
        self.z, self.c = lax.div(dp, 2), lax.rem(dp, 2)
        self.x, self.y = lax.div(t, 4), lax.rem(t, 4)

    def line(self, part, a, core):
        if part == 0:
            return (a * 2 + core, self.x * 4 + self.y)
        if part == 1:
            return (self.z * 2 + core, a * 4 + self.y)
        return (self.z * 2 + core, self.x * 4 + a)

    def own_line(self, part):
        return (self.z, self.x, self.y)[part]

    def plane(self, part, b1, b2):
        if part == 0:
            return (self.z * 2 + self.c, b1 * 4 + b2)
        if part == 1:
            return (b1 * 2 + self.c, self.x * 4 + b2)
        return (b2 * 2 + self.c, b1 * 4 + self.y)

    def own_plane(self, part):
        return ((self.x, self.y), (self.z, self.y), (self.x, self.z))[part]

    def expert(self, part, j):
        b1, b2 = j // 4, j % 4
        if part == 0:
            return (self.z * 2 + self.c) * 16 + j
        if part == 1:
            return (b1 * 2 + self.c) * 16 + self.x * 4 + b2
        return (b2 * 2 + self.c) * 16 + b1 * 4 + self.y


def up(v, n):
    return lax.rem(v + n, 4)


def partners(me):
    out = [(me.z * 2 + 1 - me.c, me.x * 4 + me.y)]
    for part in range(3):
        for n in (1, 2, 3):
            out.append(me.line(part, up(me.own_line(part), n), 1 - me.c))
    for dz in range(4):
        for dx in range(4):
            for dy in range(4):
                if (dz, dx, dy) != (0, 0, 0) and 0 in (dz, dx, dy):
                    out.append((up(me.z, dz) * 2 + me.c, up(me.x, dx) * 4 + up(me.y, dy)))
    return out


def back_kernel(
    stream_ref, gain_ref, routes_ref, weights_ref, win_hbm, wdown_hbm,
    out_ref,
    win, wdown, part4, turned, table_ref, metas, ranks, pick, wgt, swap,
    nrm, toks, outg, rows, stage, hid, half_sum, psum, other_core, recv,
    wsem, m_s, m_r, g_s, g_r, d_s, d_r, t_s, t_r, x_s, x_r, c_s, c_r,
):
    me = Place()
    barrier = pltpu.get_barrier_semaphore()
    others = partners(me)
    for other in others:
        pl.semaphore_signal(barrier, inc=1, device_id=other, device_id_type=MESH)
    loads = [
        pltpu.make_async_copy(win_hbm, win, wsem.at[0]),
        pltpu.make_async_copy(wdown_hbm, wdown, wsem.at[1]),
    ]
    for load in loads:
        load.start()
    turned[...] = jnp.zeros((128, 128), F32)
    turned[pl.ds(0, 8), pl.ds(0, 32)] = routes_ref[...].astype(F32)
    turned[pl.ds(8, 8), pl.ds(0, 32)] = weights_ref[...]
    table_ref[...] = turned[...].T[:32]
    value = stream_ref[...]
    mean_square = jnp.mean(value * value, axis=1, keepdims=True)
    nrm[...] = (value * lax.rsqrt(mean_square + 1e-06) * gain_ref[...].reshape(1, 3584)).astype(BF16)
    pl.semaphore_wait(barrier, len(others))

    def send(src, dst, ssem, rsem, device):
        copy = pltpu.make_async_remote_copy(
            src_ref=src, dst_ref=dst, send_sem=ssem, recv_sem=rsem,
            device_id=device, device_id_type=MESH,
        )
        copy.start()
        return copy

    meta_sends = []
    for part in range(3):
        own = me.own_line(part) * 2 + me.c
        for n in range(4):
            for core in range(2):
                if (n, core) == (0, 0):
                    continue
                to = me.line(part, up(me.own_line(part), n), lax.rem(me.c + core, 2))
                meta_sends.append(send(table_ref, metas.at[part, own], m_s.at[part], m_r.at[part], to))
        pltpu.make_async_copy(table_ref, metas.at[part, own], m_r.at[part]).start()

    def to_line(part, n):
        return me.line(part, up(me.own_line(part), n), me.c)

    twin = (me.z * 2 + 1 - me.c, me.x * 4 + me.y)
    for part, lo, n in PARTS:
        spot = (me.own_line(part), me.c, slice(None), pl.ds(lo, n))
        toks[spot] = nrm[:, pl.ds(lo, n)]
        for k, step in enumerate((1, 3, 2)):
            send(nrm.at[:, pl.ds(lo, n)], toks.at[spot], g_s.at[part], g_r.at[part * 4 + k], to_line(part, step))
        send(nrm.at[:, pl.ds(lo, n)], toks.at[spot], g_s.at[part], g_r.at[part * 4 + 3], twin)

    def pass_on(k):
        for part, lo, n in PARTS:
            got = toks.at[up(me.own_line(part), (3, 1, 2)[k]), me.c, :, pl.ds(lo, n)]
            whole(got, g_r.at[part * 4 + k])
            send(got, got, g_s.at[part], g_r.at[part * 4 + 3], twin)

    token = lax.broadcasted_iota(I32, (256, 256), 0)
    other = lax.broadcasted_iota(I32, (256, 256), 1)
    earlier = jnp.where((token // 32 == other // 32) & (other < token), 1.0, 0.0).astype(BF16)
    lane = lax.broadcasted_iota(I32, (128, 256), 1)
    spread = jnp.where(lane // 16 == lax.broadcasted_iota(I32, (128, 256), 0), 1.0, 0.0).astype(BF16)
    of_source = other % 16 // 2 == token // 32
    rank_wanted = (other % 2).astype(F32)
    rx, ry, rz, low = token // 64, token // 16 % 4, token // 4 % 4, token % 4
    swap[0] = jnp.where(other == rz * 64 + ry * 16 + rx * 4 + low, 1.0, 0.0).astype(BF16)
    swap[1] = jnp.where(other == rx * 64 + rz * 16 + ry * 4 + low, 1.0, 0.0).astype(BF16)
    column = lax.broadcasted_iota(I32, (256, 128), 1)

    def wanted(part):
        return jnp.where(column < 16, me.expert(part, column), -1).astype(F32)

    def picks(part, half):
        pick[part, half] = jnp.where(ranks[part] == half * 2.0, 1.0, 0.0).T.astype(BF16)

    def weigh(part):
        table, asked = metas[part].reshape(256, 128), wanted(part)
        weight = jnp.zeros((256, 128), F32)
        for k in range(8):
            weight = jnp.where(table[:, k : k + 1] == asked, table[:, 8 + k : 9 + k], weight)
        weight = dot(weight.astype(BF16), spread)
        for half in range(2):
            wgt[part, half] = jnp.where(ranks[part] == half * 2.0, weight, 0.0).astype(BF16)

    for part in range(3):
        whole(metas.at[part], m_r.at[part])
        table, asked = metas[part].reshape(256, 128), wanted(part)
        hit = jnp.zeros((256, 128), F32)
        for k in range(8):
            hit = jnp.where(table[:, k : k + 1] == asked, 1.0, hit)
        rank = dot(earlier, hit.astype(BF16))
        rank = jnp.where(hit > 0.5, rank, -1.0)
        ranks[part] = jnp.where(of_source, dot(rank.astype(BF16), spread) - rank_wanted, -1.0)
        picks(part, 0)
        if part == 1:
            pass_on(0)
            pass_on(1)
    pass_on(2)

    def half_of(ref, half):
        if ref is part4:
            return lambda b1, b2, cols: part4.at[b1, b2, pl.ds(half * 16, 16), cols]
        return lambda b1, b2, cols: ref.at[half, b1, b2, :, cols]

    def exchange(half, src, dst_of, ssem, rsem, parts):
        for d1, d2 in NEAR:
            for part, lo, n in parts:
                b1, b2 = me.own_plane(part)
                e1, e2 = up(b1, d1), up(b2, d2)
                at, cols = half * 3 + part, pl.ds(lo, n)
                send(
                    half_of(src, half)(e1, e2, cols), half_of(dst_of(part), half)(b1, b2, cols),
                    ssem.at[at], rsem.at[at], me.plane(part, e1, e2),
                )
        for part, lo, n in parts:
            b1, b2 = me.own_plane(part)
            at, cols = half * 3 + part, pl.ds(lo, n)
            pltpu.make_async_copy(
                half_of(src, half)(b1, b2, cols), half_of(dst_of(part), half)(b1, b2, cols), rsem.at[at]
            ).start()

    def landing(part):
        return rows if part == 0 else stage

    def sent(half, lo, n, sem):
        for k in range(3):
            whole(outg.at[half, k, :, :, pl.ds(lo, n)], sem)
        whole(outg.at[half, 3, pl.ds(0, 3), :, pl.ds(lo, n)], sem)

    def dispatch(half):
        for part, lo, n in PARTS:
            cols = pl.ds(lo, n)
            if half == 0:
                whole(toks.at[:, 1 - me.c, :, cols], g_r.at[part * 4 + 3])
            value = dot(pick[part, half], toks[:, :, :, cols].reshape(256, n))
            outg[half, :, :, :, cols] = value.astype(BF16).reshape(4, 4, 16, n)
        exchange(half, outg, landing, d_s, d_r, PARTS)

    def expert(half):
        for part, lo, n in PARTS:
            cols = pl.ds(lo, n)
            whole(landing(part).at[half, :, :, :, cols], d_r.at[half * 3 + part])
            if part:
                value = dot(swap[part - 1], stage[half, :, :, :, cols].reshape(256, n))
                rows[half, :, :, :, cols] = value.astype(BF16).reshape(4, 4, 16, n)
        if half == 0:
            loads[0].wait()
            loads[1].wait()

        def hidden(j, carry):
            cols = pl.ds(pl.multiple_of(j * 256, 256), 256)
            more = pl.ds(pl.multiple_of(j * 256 + 1024, 256), 256)
            here = rows[half].reshape(256, 3584)
            gate = dot(here, win[:, cols])
            lift = dot(here, win[:, more])
            hid[0, :, cols] = (gate / (1.0 + jnp.exp(-gate)) * lift).astype(BF16)
            return carry

        lax.fori_loop(0, 4, hidden, 0)
        for part, lo, n in PARTS:
            if part:
                hid[part] = dot(swap[part - 1], hid[0]).astype(BF16)
            sent(half, lo, n, d_s.at[half * 3 + part])
            value = dot(hid[part], wdown[:, pl.ds(lo, n)])
            outg[half, :, :, :, pl.ds(lo, n)] = value.astype(BF16).reshape(4, 4, 16, n)
            if half:
                exchange(half, outg, lambda part: part4, t_s, t_r, ((part, lo, n),))
        if half == 0:
            exchange(half, outg, lambda part: part4, t_s, t_r, PARTS)

    dispatch(0)
    for part in range(3):
        picks(part, 1)
    dispatch(1)
    for part in range(3):
        weigh(part)
    expert(0)
    expert(1)

    for half in range(2):
        for part, lo, n in PARTS:
            cols = pl.ds(lo, n)
            back_rows = part4.at[:, :, pl.ds(half * 16, 16), cols]
            whole(back_rows, t_r.at[half * 3 + part])
            value = dot(wgt[part, half], back_rows[...].reshape(256, n))
            if half == 0:
                half_sum[:, cols] = value
                continue
            psum[:, :, :, cols] = (half_sum[:, cols] + value).astype(BF16).reshape(4, 2, 32, n)
            send(psum.at[:, 1 - me.c, :, cols], other_core.at[:, :, cols], x_s.at[part], x_r.at[part], twin)
    for part, lo, n in PARTS:
        cols = pl.ds(lo, n)
        own = me.own_line(part)
        whole(other_core.at[:, :, cols], x_r.at[part])
        both = psum[:, me.c, :, cols].astype(F32) + other_core[:, :, cols].astype(F32)
        psum[:, me.c, :, cols] = both.astype(BF16)
        for step in (1, 3, 2):
            send(
                psum.at[up(own, step), me.c, :, cols], recv.at[own, :, cols],
                c_s.at[part], c_r.at[part], to_line(part, step),
            )
        pltpu.make_async_copy(psum.at[own, me.c, :, cols], recv.at[own, :, cols], c_r.at[part]).start()
    for part, lo, n in PARTS:
        cols = pl.ds(lo, n)
        whole(recv.at[:, :, cols], c_r.at[part])
        total = stream_ref[:, cols]
        for q in range(4):
            total += recv[q, :, cols].astype(F32)
        out_ref[:, cols] = total
    for part, lo, n in PARTS:
        cols = pl.ds(lo, n)
        for half in range(2):
            sent(half, lo, n, t_s.at[half * 3 + part])
        whole(toks.at[pl.ds(0, 3), :, :, cols], g_s.at[part])
        whole(nrm.at[:, cols], g_s.at[part])
        whole(other_core.at[:, :, cols], x_s.at[part])
        whole(recv.at[pl.ds(0, 3), :, cols], c_s.at[part])
        whole(metas.at[part, pl.ds(0, 7)], m_s.at[part])


def back(stream, norm_gain, routes, weights, expert_in, expert_down):
    vmem = pl.BlockSpec(memory_space=pltpu.VMEM)
    hbm = pl.BlockSpec(memory_space=pl.ANY)
    dma = pltpu.SemaphoreType.DMA
    halves = (2, 4, 4, 16, 3584)
    return pl.pallas_call(
        back_kernel,
        out_shape=jax.ShapeDtypeStruct((32, 3584), F32),
        in_specs=[vmem, vmem, vmem, vmem, hbm, hbm],
        out_specs=vmem,
        scratch_shapes=[
            pltpu.VMEM((3584, 2048), BF16),
            pltpu.VMEM((1024, 3584), BF16),
            pltpu.VMEM((4, 4, 32, 3584), BF16),
            pltpu.VMEM((128, 128), F32),
            pltpu.VMEM((32, 128), F32),
            pltpu.VMEM((3, 8, 32, 128), F32),
            pltpu.VMEM((3, 256, 256), F32),
            pltpu.VMEM((3, 2, 256, 256), BF16),
            pltpu.VMEM((3, 2, 256, 256), BF16),
            pltpu.VMEM((2, 256, 256), BF16),
            pltpu.VMEM((32, 3584), BF16),
            pltpu.VMEM((4, 2, 32, 3584), BF16),
            pltpu.VMEM(halves, BF16),
            pltpu.VMEM(halves, BF16),
            pltpu.VMEM(halves, BF16),
            pltpu.VMEM((3, 256, 1024), BF16),
            pltpu.VMEM((256, 3584), F32),
            pltpu.VMEM((4, 2, 32, 3584), BF16),
            pltpu.VMEM((4, 32, 3584), BF16),
            pltpu.VMEM((4, 32, 3584), BF16),
            dma((2,)),
            dma((3,)),
            dma((3,)),
            dma((3,)),
            dma((12,)),
            dma((6,)),
            dma((6,)),
            dma((6,)),
            dma((6,)),
            dma((3,)),
            dma((3,)),
            dma((3,)),
            dma((3,)),
        ],
        compiler_params=pltpu.CompilerParams(
            collective_id=1, has_side_effects=True, vmem_limit_bytes=67043328
        ),
        name="back",
    )(stream, norm_gain, routes, weights, expert_in, expert_down)


LOWEST = -1e30


def front_kernel(
    scale, off_ref, q_ref, cache_ref, vup_ref, wot_ref, resid_ref,
    stream_ref,
    keys, kc, vt, qt, vupt, places, bias, scores, probs, acc, top, tot, slabs, wide, ho,
    part4, r1, l1, r2, l2, mid, r1b, l1b, r2b, l2b,
    k_s, k_r, w_s, w_r, own_sem, rs_s, rs_r,
):
    me = Place()
    here = me.z * 2 + me.c

    def along(axis, n):
        if axis == 0:
            return (here, up(me.x, n) * 4 + me.y)
        return (here, me.x * 4 + up(me.y, n))

    own_copy = pltpu.make_async_copy(cache_ref, keys.at[me.x, me.y], own_sem)
    own_copy.start()

    slabs[me.z, me.c] = wot_ref[...].T
    twin = (me.z * 2 + 1 - me.c, me.x * 4 + me.y)
    above = [(up(me.z, n) * 2 + me.c, me.x * 4 + me.y) for n in (1, 3, 2)]
    others = [along(0, 1), along(0, 3), along(1, 1), along(1, 3), twin] + above
    barrier = pltpu.get_barrier_semaphore()
    for other in others:
        pl.semaphore_signal(barrier, inc=1, device_id=other, device_id_type=MESH)
    pl.semaphore_wait(barrier, len(others))

    def send(src, dst, ssem, rsem, device):
        copy = pltpu.make_async_remote_copy(
            src_ref=src, dst_ref=dst, send_sem=ssem, recv_sem=rsem,
            device_id=device, device_id_type=MESH,
        )
        copy.start()
        return copy

    def axis_of(half, phase):
        return half if phase == 0 else 1 - half

    def spot(half, phase, n, lo, rows, part=0):
        rows = pl.ds(half * 96 + lo, rows)
        two = pl.ds(part * 2, 2)
        if axis_of(half, phase) == 0:
            a = up(me.x, n)
            return keys.at[a, me.y, rows] if phase == 0 else keys.at[a, two, rows]
        b = up(me.y, n)
        return keys.at[me.x, b, rows] if phase == 0 else keys.at[two, b, rows]

    def sem(half, phase, k, part=0):
        return half * 12 + phase * 4 + part * 4 + k

    def spread(half, phase, part=0):
        axis = axis_of(half, phase)
        for k, n in ((0, 1), (1, 3)):
            at = spot(half, phase, 0, 0, 96, part)
            src = cache_ref.at[pl.ds(half * 96, 96)] if phase == 0 else at
            i = sem(half, phase, k, part)
            send(src, at, k_s.at[i], k_r.at[i], along(axis, n))

    def forward(half, phase, part=0):
        axis = axis_of(half, phase)
        for k, n, lo in ((0, 3, 0), (1, 1, 48)):
            whole(spot(half, phase, n, 0, 96, part), k_r.at[sem(half, phase, k, part)])
            some = spot(half, phase, n, lo, 48, part)
            i = sem(half, phase, 2 + k, part)
            send(some, some, k_s.at[i], k_r.at[i], along(axis, 4 - n))

    def far(half, phase, part=0):
        for k, lo in ((0, 0), (1, 48)):
            whole(spot(half, phase, 2, lo, 48, part), k_r.at[sem(half, phase, 2 + k, part)])

    for half in range(2):
        spread(half, 0)
    mine = slabs.at[me.z, me.c]
    send(mine, mine, w_s.at[0], w_r.at[0], twin)
    for k, to in enumerate(above):
        send(mine, mine, w_s.at[1 + k], w_r.at[1 + k], to)

    qt[:, :, pl.ds(576, 64), :] = jnp.zeros((2, 2, 64, 512), BF16)
    for tile in range(2):
        for h in range(4):
            lo = h * 576 - h % 2 * 64
            some = q_ref[:, pl.ds(tile * 16, 16), lo : lo + 640].reshape(256, 640).T
            lanes = pl.ds(h % 2 * 256, 256)
            qt[tile, h // 2, pl.ds(0, 576), lanes] = some[64:] if h % 2 else some[:576]
    for half in range(2):
        forward(half, 0)
    for h in range(4):
        vupt[h] = vup_ref[h].T
    kc[:, :, pl.ds(512, 128)] = jnp.zeros((4, 768, 128), BF16)
    top[...] = jnp.full((2, 2, 1, 512), -3e38, F32)
    tot[...] = jnp.zeros((2, 2, 1, 512), F32)
    acc[...] = jnp.zeros((2, 2, 512, 512), F32)
    own_copy.wait()
    for half in range(2):
        far(half, 0)
    for part in range(2):
        for half in range(2):
            spread(half, 1, part)

    lane = lax.broadcasted_iota(I32, (1, 256), 1)
    query = lane // 16 * 32 + lane % 16

    def build(chunk):
        for half in range(2):
            mine = me.x if half else me.y
            at = pl.ds(half * 384, 384)
            rows = pl.ds(half * 96, 96)
            if chunk in (0, 3):
                n = up(mine, 0 if chunk == 0 else 2)
                block = keys[n, :, rows, :] if half else keys[:, n, rows, :]
                kc[chunk, at, pl.ds(0, 576)] = block.reshape(384, 576)
                continue
            two = pl.ds(chunk * 2 - 2, 2)
            for k, n in enumerate((1, 3)):
                n = up(mine, n)
                block = keys[n, two, rows, :] if half else keys[two, n, rows, :]
                kc[chunk, pl.ds(half * 384 + k * 192, 192), pl.ds(0, 576)] = block.reshape(192, 576)
        vt[chunk] = kc[chunk, :, pl.ds(0, 512)].T

    low_row = lax.broadcasted_iota(I32, (96, 128), 0) - off_ref[0]
    for chunk in range(4):
        for half in range(2):
            for k in range(4):
                step, order = (0 if chunk == 0 else 2), k
                if chunk in (1, 2):
                    step, order = (1, 3)[k // 2], k % 2 + chunk * 2 - 2
                across = up(me.x if half else me.y, step)
                block = across * 4 + order if half else order * 4 + across
                places[chunk, pl.ds((half * 4 + k) * 96, 96)] = low_row + (block * 192 + half * 96)

    def heads(tile):
        for g in range(2):
            context = (acc[tile, g] * (1.0 / tot[tile, g])).astype(BF16)
            for k in range(2):
                value = dot(vupt[2 * g + k], context[:, k * 256 : k * 256 + 256]).T.astype(BF16)
                ho[tile, :, :, :, pl.ds((2 * g + k) * 128, 128)] = value.reshape(4, 4, 16, 128)

    def project(tile, h):
        for b in range(2):
            value = dot(ho[tile].reshape(256, 512), wide[2 * h + b])
            cols = pl.ds(h * 1792 + b * 896, 896)
            part4[tile, :, :, :, cols] = value.astype(BF16).reshape(4, 4, 16, 896)

    def position(h, phase):
        return me.x if h == phase else me.y

    def piece(tile, h, phase, k, lo, n):
        if phase:
            return mid.at[tile, h, k, :, pl.ds(lo, n)]
        cols = pl.ds(h * 1792 + lo, n)
        return part4.at[tile, :, k, :, cols] if h else part4.at[tile, k, :, :, cols]

    def box(i, tile, h, phase, lo, n):
        ref = (r1b, l1b, r2b, l2b)[i] if phase else (r1, l1, r2, l2)[i]
        if phase:
            return ref.at[tile, h, :, pl.ds(lo, n)]
        return ref.at[tile, h, :, :, pl.ds(lo, n)]

    def rs_sem(tile, h, phase, k):
        return ((tile * 2 + h) * 2 + phase) * 6 + k

    def give(tile, h, phase, k, src, dst, n):
        i = rs_sem(tile, h, phase, k)
        send(src, dst, rs_s.at[i], rs_r.at[i], along(0 if h == phase else 1, n))

    def first_far(tile, h, phase):
        for side, (lo, n) in enumerate(((0, 1), (896, 3))):
            src = piece(tile, h, phase, up(position(h, phase), 2), lo, 896)
            give(tile, h, phase, side, src, box(side, tile, h, phase, 0, 896), n)

    def first_near(tile, h, phase):
        for side, (lo, n) in enumerate(((896, 1), (0, 3))):
            src = piece(tile, h, phase, up(position(h, phase), n), lo, 896)
            give(tile, h, phase, 2 + side, src, box(2 + side, tile, h, phase, lo, 896), n)

    def finish(tile):
        heads(tile)
        for h in range(2):
            project(tile, h)
            first_far(tile, h, 0)
        for h in range(2):
            first_near(tile, h, 0)

    def second(tile, phase):
        for h in range(2):
            for side, (lo, n) in enumerate(((0, 1), (896, 3))):
                came = box(side, tile, h, phase, 0, 896)
                whole(came, rs_r.at[rs_sem(tile, h, phase, side)])
                own = piece(tile, h, phase, up(position(h, phase), n), lo, 896)
                own[...] = (own[...].astype(F32) + came[...].astype(F32)).astype(BF16)
                give(tile, h, phase, 4 + side, own, box(2 + side, tile, h, phase, lo, 896), n)

    def last(tile, h, phase):
        for k, (side, lo) in enumerate(((2, 896), (3, 0), (2, 0), (3, 896))):
            whole(box(side, tile, h, phase, lo, 896), rs_r.at[rs_sem(tile, h, phase, 2 + k)])
        total = piece(tile, h, phase, position(h, phase), 0, 1792)[...].astype(F32)
        total += box(2, tile, h, phase, 0, 1792)[...].astype(F32)
        return total + box(3, tile, h, phase, 0, 1792)[...].astype(F32)

    def middle(tile):
        for h in range(2):
            mid[tile, h] = last(tile, h, 0).astype(BF16)
        for h in range(2):
            first_far(tile, h, 1)
        for h in range(2):
            first_near(tile, h, 1)

    def settle(tile):
        rows, cols = pl.ds(tile * 16, 16), (pl.ds(0, 1792), pl.ds(1792, 1792))
        for h in range(2):
            stream_ref[rows, cols[h]] = last(tile, h, 1) + resid_ref[rows, cols[h]].astype(F32)

    build(0)

    def step(i, carry):
        @pl.when(i == 1)
        def _():
            for half in range(2):
                forward(half, 1, 0)
            build(1)

        @pl.when(i == 2)
        def _():
            for part in range(2):
                for half in range(2):
                    far(half, 1, part)
            build(3)
            for k, n in enumerate((3, 1, 2)):
                got = slabs.at[up(me.z, n), me.c]
                whole(got, w_r.at[1 + k])
                send(got, got, w_s.at[4 + k], w_r.at[4 + k], twin)

        @pl.when(i == 3)
        def _():
            whole(slabs.at[me.z, 1 - me.c], w_r.at[0])
            for k, n in enumerate((3, 1, 2)):
                whole(slabs.at[up(me.z, n), 1 - me.c], w_r.at[4 + k])
            for z in range(4):
                wide[z] = jnp.concatenate([slabs[z, 0], slabs[z, 1]], axis=1)
            finish(0)

        tiles = (lax.div(i, 3), jnp.where(i == 1, 0, 1))
        chunks = (i + lax.div(i, 2) - 2 * lax.div(i, 3), jnp.where(i == 1, 2, jnp.where(i == 2, 1, i)))

        def score(u):
            scores[u % 2] = dot(kc[chunks[u // 2]], qt[tiles[u // 2], u % 2])

        def gather_values(u):
            tile, g = tiles[u // 2], u % 2
            acc[tile, g] += dot(vt[chunks[u // 2]], probs[g])

        score(0)
        for u in range(4):
            tile, g = tiles[u // 2], u % 2
            if u < 3:
                score(u + 1)
            if u > 0:
                gather_values(u - 1)
            if g == 0:
                place = places[chunks[u // 2]]
                place = jnp.concatenate([place, place], axis=1)
                bias[...] = jnp.where(place <= query + tile * 16, 0.0, LOWEST)
            for k in range(2):
                lanes = pl.ds(k * 256, 256)
                s = scores[g, :, lanes] * scale + bias[...]
                old = top[tile, g, :, lanes]
                new = jnp.maximum(old, jnp.max(s, axis=0, keepdims=True))
                p = jnp.exp2(s - new)
                shrink = jnp.exp2(old - new)
                top[tile, g, :, lanes] = new
                tot[tile, g, :, lanes] = tot[tile, g, :, lanes] * shrink + jnp.sum(p, axis=0, keepdims=True)
                acc[tile, g, :, lanes] = acc[tile, g, :, lanes] * shrink
                probs[g, :, lanes] = p.astype(BF16)
            if u == 0:

                @pl.when(i == 1)
                def _():
                    for half in range(2):
                        forward(half, 1, 1)
                    build(2)

            if u == 1:

                @pl.when(i == 3)
                def _():
                    second(0, 0)

        gather_values(3)
        return carry

    lax.fori_loop(0, 4, step, 0)
    finish(1)
    middle(0)
    second(1, 0)
    second(0, 1)
    middle(1)
    settle(0)
    second(1, 1)
    settle(1)
    for k, n in enumerate((3, 1, 2)):
        whole(mine, w_s.at[1 + k])
        whole(slabs.at[up(me.z, n), me.c], w_s.at[4 + k])
    whole(mine, w_s.at[0])
    for half in range(2):
        for phase, part in ((0, 0), (1, 0), (1, 1)):
            for k in range(2):
                whole(spot(half, phase, 0, 0, 96, part), k_s.at[sem(half, phase, k, part)])
                whole(spot(half, phase, 0, 0, 48, part), k_s.at[sem(half, phase, 2 + k, part)])
    for tile in range(2):
        for h in range(2):
            for phase in range(2):
                for k in range(6):
                    src = piece(tile, h, phase, 0, 0, 896)
                    whole(src, rs_s.at[rs_sem(tile, h, phase, k)])


def front(offsets, queries, cache, value_up, out_proj, resid, scale):
    vmem = pl.BlockSpec(memory_space=pltpu.VMEM)
    dma = pltpu.SemaphoreType.DMA
    return pl.pallas_call(
        functools.partial(front_kernel, scale),
        out_shape=jax.ShapeDtypeStruct((32, 3584), F32),
        in_specs=[pl.BlockSpec(memory_space=pltpu.SMEM), vmem, vmem, vmem, vmem, vmem],
        out_specs=vmem,
        scratch_shapes=[
            pltpu.VMEM((4, 4, 192, 576), BF16),
            pltpu.VMEM((4, 768, 640), BF16),
            pltpu.VMEM((4, 512, 768), BF16),
            pltpu.VMEM((2, 2, 640, 512), BF16),
            pltpu.VMEM((4, 128, 512), BF16),
            pltpu.VMEM((4, 768, 128), I32),
            pltpu.VMEM((768, 256), F32),
            pltpu.VMEM((2, 768, 512), F32),
            pltpu.VMEM((2, 768, 512), BF16),
            pltpu.VMEM((2, 2, 512, 512), F32),
            pltpu.VMEM((2, 2, 1, 512), F32),
            pltpu.VMEM((2, 2, 1, 512), F32),
            pltpu.VMEM((4, 2, 512, 448), BF16),
            pltpu.VMEM((4, 512, 896), BF16),
            pltpu.VMEM((2, 4, 4, 16, 512), BF16),
            pltpu.VMEM((2, 4, 4, 16, 3584), BF16),
            pltpu.VMEM((2, 2, 4, 16, 896), BF16),
            pltpu.VMEM((2, 2, 4, 16, 896), BF16),
            pltpu.VMEM((2, 2, 4, 16, 1792), BF16),
            pltpu.VMEM((2, 2, 4, 16, 1792), BF16),
            pltpu.VMEM((2, 2, 4, 16, 1792), BF16),
            pltpu.VMEM((2, 2, 16, 896), BF16),
            pltpu.VMEM((2, 2, 16, 896), BF16),
            pltpu.VMEM((2, 2, 16, 1792), BF16),
            pltpu.VMEM((2, 2, 16, 1792), BF16),
            dma((24,)),
            dma((24,)),
            dma((7,)),
            dma((7,)),
            dma(()),
            dma((48,)),
            dma((48,)),
        ],
        compiler_params=pltpu.CompilerParams(
            collective_id=2, has_side_effects=True, vmem_limit_bytes=67043328
        ),
        name="front",
    )(offsets, queries, cache, value_up, out_proj, resid)


def shards(
    queries,
    cache,
    offsets,
    value_up,
    out_proj,
    resid,
    norm_gain,
    routes,
    route_weights,
    expert_in,
    expert_down,
):
    latent_width = value_up.shape[1]
    key_width = cache.shape[2]
    score_scale = (value_up.shape[2] + key_width - latent_width) ** (-0.5)
    stream = front(
        offsets, queries.reshape(16, 32, -1), cache[0], value_up, out_proj.T, resid,
        score_scale * LOG2_E,
    )
    mixed = back(stream, norm_gain, routes.T, route_weights.T, expert_in[0], expert_down[0])
    return mixed.astype(BF16)


def solution(mesh):
    return jax.shard_map(
        shards,
        mesh=mesh,
        in_specs=(
            P("dp", "tensor"),
            P("dp", "tensor", None),
            P("dp"),
            P("tensor", None, None),
            P("tensor", "dp"),
            P(("dp", "tensor"), None),
            P(),
            P(("dp", "tensor"), None),
            P(("dp", "tensor"), None),
            P(("dp", "tensor"), None, None),
            P(("dp", "tensor"), None, None),
        ),
        out_specs=P(("dp", "tensor"), None),
        check_vma=False,
    )
```

```python
import functools

import jax
import jax.numpy as jnp
from jax import lax
from jax.experimental import pallas as pl
from jax.experimental.pallas import tpu as pltpu
from jax.sharding import PartitionSpec as P

MESH = pl.DeviceIdType.MESH
LOG2_E = 1.4426950408889634
BF16, F32, I32 = jnp.bfloat16, jnp.float32, jnp.int32
NEAR = (
    (1, 0), (0, 1), (3, 0), (0, 3), (1, 1), (3, 3), (1, 3), (3, 1),
    (2, 0), (0, 2), (2, 2), (2, 1), (1, 2), (2, 3), (3, 2),
)
PARTS = ((0, 0, 1280), (1, 1280, 1152), (2, 2432, 1152))


def whole(ref, sem):
    pltpu.make_async_copy(ref, ref, sem).wait()


def dot(a, b):
    return jnp.dot(a, b, preferred_element_type=F32)


class Place:
    def __init__(self):
        dp, t = lax.axis_index("dp"), lax.axis_index("tensor")
        self.z, self.c = lax.div(dp, 2), lax.rem(dp, 2)
        self.x, self.y = lax.div(t, 4), lax.rem(t, 4)

    def line(self, part, a, core):
        if part == 0:
            return (a * 2 + core, self.x * 4 + self.y)
        if part == 1:
            return (self.z * 2 + core, a * 4 + self.y)
        return (self.z * 2 + core, self.x * 4 + a)

    def own_line(self, part):
        return (self.z, self.x, self.y)[part]

    def plane(self, part, b1, b2):
        if part == 0:
            return (self.z * 2 + self.c, b1 * 4 + b2)
        if part == 1:
            return (b1 * 2 + self.c, self.x * 4 + b2)
        return (b2 * 2 + self.c, b1 * 4 + self.y)

    def own_plane(self, part):
        return ((self.x, self.y), (self.z, self.y), (self.x, self.z))[part]

    def expert(self, part, j):
        b1, b2 = j // 4, j % 4
        if part == 0:
            return (self.z * 2 + self.c) * 16 + j
        if part == 1:
            return (b1 * 2 + self.c) * 16 + self.x * 4 + b2
        return (b2 * 2 + self.c) * 16 + b1 * 4 + self.y


def up(v, n):
    return lax.rem(v + n, 4)


def partners(me):
    out = [(me.z * 2 + 1 - me.c, me.x * 4 + me.y)]
    for part in range(3):
        for n in (1, 2, 3):
            out.append(me.line(part, up(me.own_line(part), n), 1 - me.c))
    for dz in range(4):
        for dx in range(4):
            for dy in range(4):
                if (dz, dx, dy) != (0, 0, 0) and 0 in (dz, dx, dy):
                    out.append((up(me.z, dz) * 2 + me.c, up(me.x, dx) * 4 + up(me.y, dy)))
    return out


def back_kernel(
    stream_ref, gain_ref, routes_ref, weights_ref, win_hbm, wdown_hbm,
    out_ref,
    win, wdown, part4, turned, table_ref, metas, ranks, pick, wgt, swap,
    nrm, toks, outg, rows, stage, hid, half_sum, psum, other_core, recv,
    wsem, m_s, m_r, g_s, g_r, d_s, d_r, t_s, t_r, x_s, x_r, c_s, c_r,
):
    me = Place()
    barrier = pltpu.get_barrier_semaphore()
    others = partners(me)
    for other in others:
        pl.semaphore_signal(barrier, inc=1, device_id=other, device_id_type=MESH)
    loads = [
        pltpu.make_async_copy(win_hbm, win, wsem.at[0]),
        pltpu.make_async_copy(wdown_hbm, wdown, wsem.at[1]),
    ]
    for load in loads:
        load.start()
    turned[...] = jnp.zeros((128, 128), F32)
    turned[pl.ds(0, 8), pl.ds(0, 32)] = routes_ref[...].astype(F32)
    turned[pl.ds(8, 8), pl.ds(0, 32)] = weights_ref[...]
    table_ref[...] = turned[...].T[:32]
    value = stream_ref[...]
    mean_square = jnp.mean(value * value, axis=1, keepdims=True)
    nrm[...] = (value * lax.rsqrt(mean_square + 1e-06) * gain_ref[...].reshape(1, 3584)).astype(BF16)
    pl.semaphore_wait(barrier, len(others))

    def send(src, dst, ssem, rsem, device):
        copy = pltpu.make_async_remote_copy(
            src_ref=src, dst_ref=dst, send_sem=ssem, recv_sem=rsem,
            device_id=device, device_id_type=MESH,
        )
        copy.start()
        return copy

    meta_sends = []
    for part in range(3):
        own = me.own_line(part) * 2 + me.c
        for n in range(4):
            for core in range(2):
                if (n, core) == (0, 0):
                    continue
                to = me.line(part, up(me.own_line(part), n), lax.rem(me.c + core, 2))
                meta_sends.append(send(table_ref, metas.at[part, own], m_s.at[part], m_r.at[part], to))
        pltpu.make_async_copy(table_ref, metas.at[part, own], m_r.at[part]).start()

    def to_line(part, n):
        return me.line(part, up(me.own_line(part), n), me.c)

    twin = (me.z * 2 + 1 - me.c, me.x * 4 + me.y)
    for part, lo, n in PARTS:
        spot = (me.own_line(part), me.c, slice(None), pl.ds(lo, n))
        toks[spot] = nrm[:, pl.ds(lo, n)]
        for k, step in enumerate((1, 3, 2)):
            send(nrm.at[:, pl.ds(lo, n)], toks.at[spot], g_s.at[part], g_r.at[part * 4 + k], to_line(part, step))
        send(nrm.at[:, pl.ds(lo, n)], toks.at[spot], g_s.at[part], g_r.at[part * 4 + 3], twin)

    def pass_on(k):
        for part, lo, n in PARTS:
            got = toks.at[up(me.own_line(part), (3, 1, 2)[k]), me.c, :, pl.ds(lo, n)]
            whole(got, g_r.at[part * 4 + k])
            send(got, got, g_s.at[part], g_r.at[part * 4 + 3], twin)

    token = lax.broadcasted_iota(I32, (256, 256), 0)
    other = lax.broadcasted_iota(I32, (256, 256), 1)
    earlier = jnp.where((token // 32 == other // 32) & (other < token), 1.0, 0.0).astype(BF16)
    lane = lax.broadcasted_iota(I32, (128, 256), 1)
    spread = jnp.where(lane // 16 == lax.broadcasted_iota(I32, (128, 256), 0), 1.0, 0.0).astype(BF16)
    of_source = other % 16 // 2 == token // 32
    rank_wanted = (other % 2).astype(F32)
    rx, ry, rz, low = token // 64, token // 16 % 4, token // 4 % 4, token % 4
    swap[0] = jnp.where(other == rz * 64 + ry * 16 + rx * 4 + low, 1.0, 0.0).astype(BF16)
    swap[1] = jnp.where(other == rx * 64 + rz * 16 + ry * 4 + low, 1.0, 0.0).astype(BF16)
    column = lax.broadcasted_iota(I32, (256, 128), 1)

    def wanted(part):
        return jnp.where(column < 16, me.expert(part, column), -1).astype(F32)

    def picks(part, half):
        pick[part, half] = jnp.where(ranks[part] == half * 2.0, 1.0, 0.0).T.astype(BF16)

    def weigh(part):
        table, asked = metas[part].reshape(256, 128), wanted(part)
        weight = jnp.zeros((256, 128), F32)
        for k in range(8):
            weight = jnp.where(table[:, k : k + 1] == asked, table[:, 8 + k : 9 + k], weight)
        weight = dot(weight.astype(BF16), spread)
        for half in range(2):
            wgt[part, half] = jnp.where(ranks[part] == half * 2.0, weight, 0.0).astype(BF16)

    for part in range(3):
        whole(metas.at[part], m_r.at[part])
        table, asked = metas[part].reshape(256, 128), wanted(part)
        hit = jnp.zeros((256, 128), F32)
        for k in range(8):
            hit = jnp.where(table[:, k : k + 1] == asked, 1.0, hit)
        rank = dot(earlier, hit.astype(BF16))
        rank = jnp.where(hit > 0.5, rank, -1.0)
        ranks[part] = jnp.where(of_source, dot(rank.astype(BF16), spread) - rank_wanted, -1.0)
        picks(part, 0)
        if part == 1:
            pass_on(0)
            pass_on(1)
    pass_on(2)

    def half_of(ref, half):
        if ref is part4:
            return lambda b1, b2, cols: part4.at[b1, b2, pl.ds(half * 16, 16), cols]
        return lambda b1, b2, cols: ref.at[half, b1, b2, :, cols]

    def exchange(half, src, dst_of, ssem, rsem, parts):
        for d1, d2 in NEAR:
            for part, lo, n in parts:
                b1, b2 = me.own_plane(part)
                e1, e2 = up(b1, d1), up(b2, d2)
                at, cols = half * 3 + part, pl.ds(lo, n)
                send(
                    half_of(src, half)(e1, e2, cols), half_of(dst_of(part), half)(b1, b2, cols),
                    ssem.at[at], rsem.at[at], me.plane(part, e1, e2),
                )
        for part, lo, n in parts:
            b1, b2 = me.own_plane(part)
            at, cols = half * 3 + part, pl.ds(lo, n)
            pltpu.make_async_copy(
                half_of(src, half)(b1, b2, cols), half_of(dst_of(part), half)(b1, b2, cols), rsem.at[at]
            ).start()

    def landing(part):
        return rows if part == 0 else stage

    def sent(half, lo, n, sem):
        for k in range(3):
            whole(outg.at[half, k, :, :, pl.ds(lo, n)], sem)
        whole(outg.at[half, 3, pl.ds(0, 3), :, pl.ds(lo, n)], sem)

    def dispatch(half):
        for part, lo, n in PARTS:
            cols = pl.ds(lo, n)
            if half == 0:
                whole(toks.at[:, 1 - me.c, :, cols], g_r.at[part * 4 + 3])
            value = dot(pick[part, half], toks[:, :, :, cols].reshape(256, n))
            outg[half, :, :, :, cols] = value.astype(BF16).reshape(4, 4, 16, n)
        exchange(half, outg, landing, d_s, d_r, PARTS)

    def expert(half):
        for part, lo, n in PARTS:
            cols = pl.ds(lo, n)
            whole(landing(part).at[half, :, :, :, cols], d_r.at[half * 3 + part])
            if part:
                value = dot(swap[part - 1], stage[half, :, :, :, cols].reshape(256, n))
                rows[half, :, :, :, cols] = value.astype(BF16).reshape(4, 4, 16, n)
        if half == 0:
            loads[0].wait()
            loads[1].wait()

        def hidden(j, carry):
            cols = pl.ds(pl.multiple_of(j * 256, 256), 256)
            more = pl.ds(pl.multiple_of(j * 256 + 1024, 256), 256)
            here = rows[half].reshape(256, 3584)
            gate = dot(here, win[:, cols])
            lift = dot(here, win[:, more])
            hid[0, :, cols] = (gate / (1.0 + jnp.exp(-gate)) * lift).astype(BF16)
            return carry

        lax.fori_loop(0, 4, hidden, 0)
        for part, lo, n in PARTS:
            if part:
                hid[part] = dot(swap[part - 1], hid[0]).astype(BF16)
            sent(half, lo, n, d_s.at[half * 3 + part])
            value = dot(hid[part], wdown[:, pl.ds(lo, n)])
            outg[half, :, :, :, pl.ds(lo, n)] = value.astype(BF16).reshape(4, 4, 16, n)
            if half:
                exchange(half, outg, lambda part: part4, t_s, t_r, ((part, lo, n),))
        if half == 0:
            exchange(half, outg, lambda part: part4, t_s, t_r, PARTS)

    dispatch(0)
    for part in range(3):
        picks(part, 1)
    dispatch(1)
    for part in range(3):
        weigh(part)
    expert(0)
    expert(1)

    for half in range(2):
        for part, lo, n in PARTS:
            cols = pl.ds(lo, n)
            back_rows = part4.at[:, :, pl.ds(half * 16, 16), cols]
            whole(back_rows, t_r.at[half * 3 + part])
            value = dot(wgt[part, half], back_rows[...].reshape(256, n))
            if half == 0:
                half_sum[:, cols] = value
                continue
            psum[:, :, :, cols] = (half_sum[:, cols] + value).astype(BF16).reshape(4, 2, 32, n)
            send(psum.at[:, 1 - me.c, :, cols], other_core.at[:, :, cols], x_s.at[part], x_r.at[part], twin)
    for part, lo, n in PARTS:
        cols = pl.ds(lo, n)
        own = me.own_line(part)
        whole(other_core.at[:, :, cols], x_r.at[part])
        both = psum[:, me.c, :, cols].astype(F32) + other_core[:, :, cols].astype(F32)
        psum[:, me.c, :, cols] = both.astype(BF16)
        for step in (1, 3, 2):
            send(
                psum.at[up(own, step), me.c, :, cols], recv.at[own, :, cols],
                c_s.at[part], c_r.at[part], to_line(part, step),
            )
        pltpu.make_async_copy(psum.at[own, me.c, :, cols], recv.at[own, :, cols], c_r.at[part]).start()
    for part, lo, n in PARTS:
        cols = pl.ds(lo, n)
        whole(recv.at[:, :, cols], c_r.at[part])
        total = stream_ref[:, cols]
        for q in range(4):
            total += recv[q, :, cols].astype(F32)
        out_ref[:, cols] = total
    for part, lo, n in PARTS:
        cols = pl.ds(lo, n)
        for half in range(2):
            sent(half, lo, n, t_s.at[half * 3 + part])
        whole(toks.at[pl.ds(0, 3), :, :, cols], g_s.at[part])
        whole(nrm.at[:, cols], g_s.at[part])
        whole(other_core.at[:, :, cols], x_s.at[part])
        whole(recv.at[pl.ds(0, 3), :, cols], c_s.at[part])
        whole(metas.at[part, pl.ds(0, 7)], m_s.at[part])


def round_kernel(in_ref, out_ref):
    out_ref[...] = in_ref[...].astype(BF16)


def rounded(value):
    vmem = pl.BlockSpec(memory_space=pltpu.VMEM)
    return pl.pallas_call(
        round_kernel,
        out_shape=jax.ShapeDtypeStruct(value.shape, BF16),
        in_specs=[vmem],
        out_specs=vmem,
        name="rounded",
    )(value)


def back(stream, norm_gain, routes, weights, expert_in, expert_down):
    vmem = pl.BlockSpec(memory_space=pltpu.VMEM)
    hbm = pl.BlockSpec(memory_space=pl.ANY)
    dma = pltpu.SemaphoreType.DMA
    halves = (2, 4, 4, 16, 3584)
    return pl.pallas_call(
        back_kernel,
        out_shape=jax.ShapeDtypeStruct((32, 3584), F32),
        in_specs=[vmem, vmem, vmem, vmem, hbm, hbm],
        out_specs=vmem,
        scratch_shapes=[
            pltpu.VMEM((3584, 2048), BF16),
            pltpu.VMEM((1024, 3584), BF16),
            pltpu.VMEM((4, 4, 32, 3584), BF16),
            pltpu.VMEM((128, 128), F32),
            pltpu.VMEM((32, 128), F32),
            pltpu.VMEM((3, 8, 32, 128), F32),
            pltpu.VMEM((3, 256, 256), F32),
            pltpu.VMEM((3, 2, 256, 256), BF16),
            pltpu.VMEM((3, 2, 256, 256), BF16),
            pltpu.VMEM((2, 256, 256), BF16),
            pltpu.VMEM((32, 3584), BF16),
            pltpu.VMEM((4, 2, 32, 3584), BF16),
            pltpu.VMEM(halves, BF16),
            pltpu.VMEM(halves, BF16),
            pltpu.VMEM(halves, BF16),
            pltpu.VMEM((3, 256, 1024), BF16),
            pltpu.VMEM((256, 3584), F32),
            pltpu.VMEM((4, 2, 32, 3584), BF16),
            pltpu.VMEM((4, 32, 3584), BF16),
            pltpu.VMEM((4, 32, 3584), BF16),
            dma((2,)),
            dma((3,)),
            dma((3,)),
            dma((3,)),
            dma((12,)),
            dma((6,)),
            dma((6,)),
            dma((6,)),
            dma((6,)),
            dma((3,)),
            dma((3,)),
            dma((3,)),
            dma((3,)),
        ],
        compiler_params=pltpu.CompilerParams(
            collective_id=1, has_side_effects=True, vmem_limit_bytes=67043328
        ),
        name="back",
    )(stream, norm_gain, routes, weights, expert_in, expert_down)


LOWEST = -1e30


def front_kernel(
    scale, off_ref, q_ref, cache_ref, vup_ref, wot_ref, resid_ref,
    stream_ref,
    keys, kc, vt, qt, vupt, places, bias, scores, probs, acc, top, tot, slabs, wide, ho,
    part4, r1, l1, r2, l2, mid, r1b, l1b, r2b, l2b,
    k_s, k_r, w_s, w_r, own_sem, rs_s, rs_r,
):
    me = Place()
    here = me.z * 2 + me.c

    def along(axis, n):
        if axis == 0:
            return (here, up(me.x, n) * 4 + me.y)
        return (here, me.x * 4 + up(me.y, n))

    own_copy = pltpu.make_async_copy(cache_ref, keys.at[me.x, me.y], own_sem)
    own_copy.start()

    slabs[me.z, me.c] = wot_ref[...].T
    twin = (me.z * 2 + 1 - me.c, me.x * 4 + me.y)
    above = [(up(me.z, n) * 2 + me.c, me.x * 4 + me.y) for n in (1, 3, 2)]
    others = [along(0, 1), along(0, 3), along(1, 1), along(1, 3), twin] + above
    barrier = pltpu.get_barrier_semaphore()
    for other in others:
        pl.semaphore_signal(barrier, inc=1, device_id=other, device_id_type=MESH)
    pl.semaphore_wait(barrier, len(others))

    def send(src, dst, ssem, rsem, device):
        copy = pltpu.make_async_remote_copy(
            src_ref=src, dst_ref=dst, send_sem=ssem, recv_sem=rsem,
            device_id=device, device_id_type=MESH,
        )
        copy.start()
        return copy

    def axis_of(half, phase):
        return half if phase == 0 else 1 - half

    def spot(half, phase, n, lo, rows, part=0):
        rows = pl.ds(half * 96 + lo, rows)
        two = pl.ds(part * 2, 2)
        if axis_of(half, phase) == 0:
            a = up(me.x, n)
            return keys.at[a, me.y, rows] if phase == 0 else keys.at[a, two, rows]
        b = up(me.y, n)
        return keys.at[me.x, b, rows] if phase == 0 else keys.at[two, b, rows]

    def sem(half, phase, k, part=0):
        return half * 12 + phase * 4 + part * 4 + k

    def spread(half, phase, part=0):
        axis = axis_of(half, phase)
        for k, n in ((0, 1), (1, 3)):
            at = spot(half, phase, 0, 0, 96, part)
            src = cache_ref.at[pl.ds(half * 96, 96)] if phase == 0 else at
            i = sem(half, phase, k, part)
            send(src, at, k_s.at[i], k_r.at[i], along(axis, n))

    def forward(half, phase, part=0):
        axis = axis_of(half, phase)
        for k, n, lo in ((0, 3, 0), (1, 1, 48)):
            whole(spot(half, phase, n, 0, 96, part), k_r.at[sem(half, phase, k, part)])
            some = spot(half, phase, n, lo, 48, part)
            i = sem(half, phase, 2 + k, part)
            send(some, some, k_s.at[i], k_r.at[i], along(axis, 4 - n))

    def far(half, phase, part=0):
        for k, lo in ((0, 0), (1, 48)):
            whole(spot(half, phase, 2, lo, 48, part), k_r.at[sem(half, phase, 2 + k, part)])

    for half in range(2):
        spread(half, 0)
    mine = slabs.at[me.z, me.c]
    send(mine, mine, w_s.at[0], w_r.at[0], twin)
    for k, to in enumerate(above):
        send(mine, mine, w_s.at[1 + k], w_r.at[1 + k], to)

    qt[:, :, pl.ds(576, 64), :] = jnp.zeros((2, 2, 64, 512), BF16)
    for tile in range(2):
        for h in range(4):
            lo = h * 576 - h % 2 * 64
            some = q_ref[:, pl.ds(tile * 16, 16), lo : lo + 640].reshape(256, 640).T
            lanes = pl.ds(h % 2 * 256, 256)
            qt[tile, h // 2, pl.ds(0, 576), lanes] = some[64:] if h % 2 else some[:576]
    for half in range(2):
        forward(half, 0)
    for h in range(4):
        vupt[h] = vup_ref[h].T
    kc[:, :, pl.ds(512, 128)] = jnp.zeros((4, 768, 128), BF16)
    top[...] = jnp.full((2, 2, 1, 512), -3e38, F32)
    tot[...] = jnp.zeros((2, 2, 1, 512), F32)
    acc[...] = jnp.zeros((2, 2, 512, 512), F32)
    own_copy.wait()
    for half in range(2):
        far(half, 0)
    for part in range(2):
        for half in range(2):
            spread(half, 1, part)

    lane = lax.broadcasted_iota(I32, (1, 256), 1)
    query = lane // 16 * 32 + lane % 16

    def build(chunk):
        for half in range(2):
            mine = me.x if half else me.y
            at = pl.ds(half * 384, 384)
            rows = pl.ds(half * 96, 96)
            if chunk in (0, 3):
                n = up(mine, 0 if chunk == 0 else 2)
                block = keys[n, :, rows, :] if half else keys[:, n, rows, :]
                kc[chunk, at, pl.ds(0, 576)] = block.reshape(384, 576)
                continue
            two = pl.ds(chunk * 2 - 2, 2)
            for k, n in enumerate((1, 3)):
                n = up(mine, n)
                block = keys[n, two, rows, :] if half else keys[two, n, rows, :]
                kc[chunk, pl.ds(half * 384 + k * 192, 192), pl.ds(0, 576)] = block.reshape(192, 576)
        vt[chunk] = kc[chunk, :, pl.ds(0, 512)].T

    low_row = lax.broadcasted_iota(I32, (96, 128), 0) - off_ref[0]
    for chunk in range(4):
        for half in range(2):
            for k in range(4):
                step, order = (0 if chunk == 0 else 2), k
                if chunk in (1, 2):
                    step, order = (1, 3)[k // 2], k % 2 + chunk * 2 - 2
                across = up(me.x if half else me.y, step)
                block = across * 4 + order if half else order * 4 + across
                places[chunk, pl.ds((half * 4 + k) * 96, 96)] = low_row + (block * 192 + half * 96)

    def heads(tile):
        for g in range(2):
            context = (acc[tile, g] * (1.0 / tot[tile, g])).astype(BF16)
            for k in range(2):
                value = dot(vupt[2 * g + k], context[:, k * 256 : k * 256 + 256]).T.astype(BF16)
                ho[tile, :, :, :, pl.ds((2 * g + k) * 128, 128)] = value.reshape(4, 4, 16, 128)

    def project(tile, h):
        for b in range(2):
            value = dot(ho[tile].reshape(256, 512), wide[2 * h + b])
            cols = pl.ds(h * 1792 + b * 896, 896)
            part4[tile, :, :, :, cols] = value.astype(BF16).reshape(4, 4, 16, 896)

    def position(h, phase):
        return me.x if h == phase else me.y

    def piece(tile, h, phase, k, lo, n):
        if phase:
            return mid.at[tile, h, k, :, pl.ds(lo, n)]
        cols = pl.ds(h * 1792 + lo, n)
        return part4.at[tile, :, k, :, cols] if h else part4.at[tile, k, :, :, cols]

    def box(i, tile, h, phase, lo, n):
        ref = (r1b, l1b, r2b, l2b)[i] if phase else (r1, l1, r2, l2)[i]
        if phase:
            return ref.at[tile, h, :, pl.ds(lo, n)]
        return ref.at[tile, h, :, :, pl.ds(lo, n)]

    def rs_sem(tile, h, phase, k):
        return ((tile * 2 + h) * 2 + phase) * 6 + k

    def give(tile, h, phase, k, src, dst, n):
        i = rs_sem(tile, h, phase, k)
        send(src, dst, rs_s.at[i], rs_r.at[i], along(0 if h == phase else 1, n))

    def first_far(tile, h, phase):
        for side, (lo, n) in enumerate(((0, 1), (896, 3))):
            src = piece(tile, h, phase, up(position(h, phase), 2), lo, 896)
            give(tile, h, phase, side, src, box(side, tile, h, phase, 0, 896), n)

    def first_near(tile, h, phase):
        for side, (lo, n) in enumerate(((896, 1), (0, 3))):
            src = piece(tile, h, phase, up(position(h, phase), n), lo, 896)
            give(tile, h, phase, 2 + side, src, box(2 + side, tile, h, phase, lo, 896), n)

    def finish(tile):
        heads(tile)
        for h in range(2):
            project(tile, h)
            first_far(tile, h, 0)
        for h in range(2):
            first_near(tile, h, 0)

    def second(tile, phase):
        for h in range(2):
            for side, (lo, n) in enumerate(((0, 1), (896, 3))):
                came = box(side, tile, h, phase, 0, 896)
                whole(came, rs_r.at[rs_sem(tile, h, phase, side)])
                own = piece(tile, h, phase, up(position(h, phase), n), lo, 896)
                own[...] = (own[...].astype(F32) + came[...].astype(F32)).astype(BF16)
                give(tile, h, phase, 4 + side, own, box(2 + side, tile, h, phase, lo, 896), n)

    def last(tile, h, phase):
        for k, (side, lo) in enumerate(((2, 896), (3, 0), (2, 0), (3, 896))):
            whole(box(side, tile, h, phase, lo, 896), rs_r.at[rs_sem(tile, h, phase, 2 + k)])
        total = piece(tile, h, phase, position(h, phase), 0, 1792)[...].astype(F32)
        total += box(2, tile, h, phase, 0, 1792)[...].astype(F32)
        return total + box(3, tile, h, phase, 0, 1792)[...].astype(F32)

    def middle(tile):
        for h in range(2):
            mid[tile, h] = last(tile, h, 0).astype(BF16)
        for h in range(2):
            first_far(tile, h, 1)
        for h in range(2):
            first_near(tile, h, 1)

    def settle(tile):
        rows, cols = pl.ds(tile * 16, 16), (pl.ds(0, 1792), pl.ds(1792, 1792))
        for h in range(2):
            stream_ref[rows, cols[h]] = last(tile, h, 1) + resid_ref[rows, cols[h]].astype(F32)

    build(0)

    def step(i, carry):
        @pl.when(i == 1)
        def _():
            for half in range(2):
                forward(half, 1, 0)
            build(1)

        @pl.when(i == 2)
        def _():
            for part in range(2):
                for half in range(2):
                    far(half, 1, part)
            build(3)
            for k, n in enumerate((3, 1, 2)):
                got = slabs.at[up(me.z, n), me.c]
                whole(got, w_r.at[1 + k])
                send(got, got, w_s.at[4 + k], w_r.at[4 + k], twin)

        @pl.when(i == 3)
        def _():
            whole(slabs.at[me.z, 1 - me.c], w_r.at[0])
            for k, n in enumerate((3, 1, 2)):
                whole(slabs.at[up(me.z, n), 1 - me.c], w_r.at[4 + k])
            for z in range(4):
                wide[z] = jnp.concatenate([slabs[z, 0], slabs[z, 1]], axis=1)
            finish(0)

        tiles = (lax.div(i, 3), jnp.where(i == 1, 0, 1))
        chunks = (i + lax.div(i, 2) - 2 * lax.div(i, 3), jnp.where(i == 1, 2, jnp.where(i == 2, 1, i)))

        def score(u):
            scores[u % 2] = dot(kc[chunks[u // 2]], qt[tiles[u // 2], u % 2])

        def gather_values(u):
            tile, g = tiles[u // 2], u % 2
            acc[tile, g] += dot(vt[chunks[u // 2]], probs[g])

        score(0)
        for u in range(4):
            tile, g = tiles[u // 2], u % 2
            if u < 3:
                score(u + 1)
            if u > 0:
                gather_values(u - 1)
            if g == 0:
                place = places[chunks[u // 2]]
                place = jnp.concatenate([place, place], axis=1)
                bias[...] = jnp.where(place <= query + tile * 16, 0.0, LOWEST)
            for k in range(2):
                lanes = pl.ds(k * 256, 256)
                s = scores[g, :, lanes] * scale + bias[...]
                old = top[tile, g, :, lanes]
                new = jnp.maximum(old, jnp.max(s, axis=0, keepdims=True))
                p = jnp.exp2(s - new)
                shrink = jnp.exp2(old - new)
                top[tile, g, :, lanes] = new
                tot[tile, g, :, lanes] = tot[tile, g, :, lanes] * shrink + jnp.sum(p, axis=0, keepdims=True)
                acc[tile, g, :, lanes] = acc[tile, g, :, lanes] * shrink
                probs[g, :, lanes] = p.astype(BF16)
            if u == 0:

                @pl.when(i == 1)
                def _():
                    for half in range(2):
                        forward(half, 1, 1)
                    build(2)

            if u == 1:

                @pl.when(i == 3)
                def _():
                    second(0, 0)

        gather_values(3)
        return carry

    lax.fori_loop(0, 4, step, 0)
    finish(1)
    middle(0)
    second(1, 0)
    second(0, 1)
    middle(1)
    settle(0)
    second(1, 1)
    settle(1)
    for k, n in enumerate((3, 1, 2)):
        whole(mine, w_s.at[1 + k])
        whole(slabs.at[up(me.z, n), me.c], w_s.at[4 + k])
    whole(mine, w_s.at[0])
    for half in range(2):
        for phase, part in ((0, 0), (1, 0), (1, 1)):
            for k in range(2):
                whole(spot(half, phase, 0, 0, 96, part), k_s.at[sem(half, phase, k, part)])
                whole(spot(half, phase, 0, 0, 48, part), k_s.at[sem(half, phase, 2 + k, part)])
    for tile in range(2):
        for h in range(2):
            for phase in range(2):
                for k in range(6):
                    src = piece(tile, h, phase, 0, 0, 896)
                    whole(src, rs_s.at[rs_sem(tile, h, phase, k)])


def front(offsets, queries, cache, value_up, out_proj, resid, scale):
    vmem = pl.BlockSpec(memory_space=pltpu.VMEM)
    dma = pltpu.SemaphoreType.DMA
    return pl.pallas_call(
        functools.partial(front_kernel, scale),
        out_shape=jax.ShapeDtypeStruct((32, 3584), F32),
        in_specs=[pl.BlockSpec(memory_space=pltpu.SMEM), vmem, vmem, vmem, vmem, vmem],
        out_specs=vmem,
        scratch_shapes=[
            pltpu.VMEM((4, 4, 192, 576), BF16),
            pltpu.VMEM((4, 768, 640), BF16),
            pltpu.VMEM((4, 512, 768), BF16),
            pltpu.VMEM((2, 2, 640, 512), BF16),
            pltpu.VMEM((4, 128, 512), BF16),
            pltpu.VMEM((4, 768, 128), I32),
            pltpu.VMEM((768, 256), F32),
            pltpu.VMEM((2, 768, 512), F32),
            pltpu.VMEM((2, 768, 512), BF16),
            pltpu.VMEM((2, 2, 512, 512), F32),
            pltpu.VMEM((2, 2, 1, 512), F32),
            pltpu.VMEM((2, 2, 1, 512), F32),
            pltpu.VMEM((4, 2, 512, 448), BF16),
            pltpu.VMEM((4, 512, 896), BF16),
            pltpu.VMEM((2, 4, 4, 16, 512), BF16),
            pltpu.VMEM((2, 4, 4, 16, 3584), BF16),
            pltpu.VMEM((2, 2, 4, 16, 896), BF16),
            pltpu.VMEM((2, 2, 4, 16, 896), BF16),
            pltpu.VMEM((2, 2, 4, 16, 1792), BF16),
            pltpu.VMEM((2, 2, 4, 16, 1792), BF16),
            pltpu.VMEM((2, 2, 4, 16, 1792), BF16),
            pltpu.VMEM((2, 2, 16, 896), BF16),
            pltpu.VMEM((2, 2, 16, 896), BF16),
            pltpu.VMEM((2, 2, 16, 1792), BF16),
            pltpu.VMEM((2, 2, 16, 1792), BF16),
            dma((24,)),
            dma((24,)),
            dma((7,)),
            dma((7,)),
            dma(()),
            dma((48,)),
            dma((48,)),
        ],
        compiler_params=pltpu.CompilerParams(
            collective_id=2, has_side_effects=True, vmem_limit_bytes=67043328
        ),
        name="front",
    )(offsets, queries, cache, value_up, out_proj, resid)


def shards(
    queries,
    cache,
    offsets,
    value_up,
    out_proj,
    resid,
    norm_gain,
    routes,
    route_weights,
    expert_in,
    expert_down,
):
    latent_width = value_up.shape[1]
    key_width = cache.shape[2]
    score_scale = (value_up.shape[2] + key_width - latent_width) ** (-0.5)
    stream = front(
        offsets, queries.reshape(16, 32, -1), cache[0], value_up, out_proj.T, resid,
        score_scale * LOG2_E,
    )
    mixed = back(stream, norm_gain, routes.T, route_weights.T, expert_in[0], expert_down[0])
    return rounded(mixed)


def solution(mesh):
    return jax.shard_map(
        shards,
        mesh=mesh,
        in_specs=(
            P("dp", "tensor"),
            P("dp", "tensor", None),
            P("dp"),
            P("tensor", None, None),
            P("tensor", "dp"),
            P(("dp", "tensor"), None),
            P(),
            P(("dp", "tensor"), None),
            P(("dp", "tensor"), None),
            P(("dp", "tensor"), None, None),
            P(("dp", "tensor"), None, None),
        ),
        out_specs=P(("dp", "tensor"), None),
        check_vma=False,
    )
```
